32 devices in a mesh: dp: 16 (over z, y, x), tensor: 2 (over core).
Axes of the slice: x: 2, y: 2, z: 4, core: 2. Of those that a mesh axis runs over, the one named last changes fastest.
Arguments:
- tokens: bfloat16 [32768, 768], P('dp'), may hold values from -6.25 to 6.25, as said below
- long_lengths: int32 [32], P('dp'), may hold values from 128 to 512, as said below
- short_lengths: int32 [64], P('dp'), may hold values from 64 to 256, as said below
- query_weight: bfloat16 [768, 768], P(None, 'tensor'), may hold values from -0.21875 to 0.21875
- query_bias: float32 [768], P('tensor'), may hold values from -3 to 3
- key_weight: bfloat16 [768, 768], P(None, 'tensor'), may hold values from -0.21875 to 0.21875
- value_weight: bfloat16 [768, 768], P(None, 'tensor'), may hold values from -0.21875 to 0.21875
- value_bias: float32 [768], P('tensor'), may hold values from -3 to 3
- output_weight: bfloat16 [768, 768], P('tensor'), may hold values from -0.875 to 0.875
- output_bias: float32 [768], replicated, may hold values from -3 to 3
- first_gain: float32 [768], replicated, may hold values from 0.25 to 1.75
- first_shift: float32 [768], replicated, may hold values from -3 to 3
- inner_weight: bfloat16 [768, 3072], P(None, 'tensor'), may hold values from -0.21875 to 0.21875
- inner_bias: float32 [3072], P('tensor'), may hold values from -3 to 3
- outer_weight: bfloat16 [3072, 768], P('tensor'), may hold values from -0.109375 to 0.109375
- outer_bias: float32 [768], replicated, may hold values from -3 to 3
- second_gain: float32 [768], replicated, may hold values from 0.25 to 1.75
- second_shift: float32 [768], replicated, may hold values from -3 to 3
- out_grad: bfloat16 [32768, 768], P('dp'), may hold values from -6 to 6
Outputs:
- block_out: bfloat16 [32768, 768], P('dp')
- tokens_grad: bfloat16 [32768, 768], P('dp')
- query_weight_grad: float32 [768, 768], P('dp', 'tensor')
- query_bias_grad: float32 [768], P('tensor')
- key_weight_grad: float32 [768, 768], P('dp', 'tensor')
- value_weight_grad: float32 [768, 768], P('dp', 'tensor')
- value_bias_grad: float32 [768], P('tensor')
- output_weight_grad: float32 [768, 768], P('tensor', 'dp')
- output_bias_grad: float32 [768], replicated
- first_gain_grad: float32 [768], replicated
- first_shift_grad: float32 [768], replicated
- inner_weight_grad: float32 [768, 3072], P('dp', 'tensor')
- inner_bias_grad: float32 [3072], P('tensor')
- outer_weight_grad: float32 [3072, 768], P('tensor', 'dp')
- outer_bias_grad: float32 [768], replicated
- second_gain_grad: float32 [768], replicated
- second_shift_grad: float32 [768], replicated
- residual_rms: float32 [], replicated
- attention_rms: float32 [], replicated
- feedforward_rms: float32 [], replicated
The draws below stay inside these ranges and needn't reach their ends.
Inputs may be any that keep to these rules, and one draw needn't show every extreme that they name: `long_lengths`: the entry of a long-bucket sequence; its slot positions from this length on are padding. `short_lengths`: the entry of a short-bucket sequence; its slot positions from this length on are padding. `tokens`: activations of order one.
All inputs are finite; a program needn't handle non-finite values.
Results may differ from the reference program's by a relative error of at most 0.02.
Values may be sent and summed in bfloat16 or wider, within the bound.
No kernel may reach another device: no remote copies, remote signals or barrier semaphores. Data moves between devices by JAX's collectives and lax.ppermute only.
A program may use at most 192 MiB of HBM per device.

```python
import jax
import jax.numpy as jnp
from jax import lax

D = 768
HEADS = 12
HEAD_DIM = 64
FF = 3072
LONG = 512
SHORT = 256
NL_DEV = 2
NS_DEV = 4
TOK_DEV = 2048
TOKENS = 32768
NLONG = 32
NSHORT = 64
N_DP = 16
N_TENSOR = 2


def draw_tokens(key, part):
    rows = jnp.arange(TOKENS, dtype=jnp.int32)
    device_count = TOKENS // TOK_DEV
    owner = (rows // TOK_DEV).astype(jnp.float32)
    scale = 0.55 + 1.05 * owner / max(device_count - 1, 1)
    base = jnp.clip(jax.random.normal(key, (TOKENS, D), jnp.float32), -3.9, 3.9)
    return (base * scale[:, None]).astype(jnp.bfloat16)


def bounded_lengths(key, entries, most):
    drawn = jax.random.randint(key, (entries,), most // 4, most + 1)
    first = jax.random.randint(jax.random.fold_in(key, 7), (), 0, entries)
    offset = jax.random.randint(jax.random.fold_in(key, 11), (), 1, entries)
    drawn = drawn.at[first].set(most)
    return drawn.at[(first + offset) % entries].set(most // 4).astype(jnp.int32)


def draw_long_lengths(key, part):
    return bounded_lengths(key, NLONG, LONG)


def draw_short_lengths(key, part):
    return bounded_lengths(key, NSHORT, SHORT)


def strengthened(values, rng, source, target, parts, factor):
    def block_of(axis_at):
        return (jnp.arange(values.shape[axis_at]) // (values.shape[axis_at] // parts)).reshape((-1,) + (1,) * (values.ndim - 1 - axis_at))

    one_side = jax.random.permutation(rng, parts)[block_of(target)]
    other_side = (block_of(target) + parts // 2) % parts
    return jnp.where((block_of(source) == one_side) | (block_of(source) == other_side), factor * values, values)


def steps_of(key, shape, pieces, least, top_value):
    gain = 1.0
    for axis_at, blocks in pieces:
        draws = jax.random.uniform(jax.random.fold_in(jax.random.fold_in(key, 6), axis_at), (blocks,), jnp.float32, least / len(pieces), top_value / len(pieces))
        gain = gain * jnp.repeat(jnp.exp(draws), shape[axis_at] // blocks).reshape((-1,) + (1,) * (len(shape) - 1 - axis_at))
    return gain


def centred(rng, dims, scale, bound, pieces=(), kind=jnp.bfloat16):
    values = jax.random.normal(rng, dims, jnp.float32) * scale
    if len(pieces) > 0:
        values = steps_of(rng, dims, pieces, -0.22, 0.18) * values
    return jnp.clip(values, min=-bound, max=bound).astype(kind)


def bell_draw_with(own_key, extent, deviation, limit, cuts, heavy, held_as=jnp.bfloat16):
    values = deviation * jax.random.normal(own_key, extent, jnp.float32)
    if cuts:
        values = values * steps_of(own_key, extent, cuts, -0.22, 0.18)
    return jnp.clip(strengthened(values, jax.random.fold_in(own_key, 3), *heavy), -limit, limit).astype(held_as)


def setup_inputs(seed: int = 0) -> dict:
    splits = jax.random.split(jax.random.key(seed), 20)
    tokens = draw_tokens(jax.random.fold_in(splits[19], 71), 0)
    long_lengths = draw_long_lengths(jax.random.fold_in(splits[19], 71), 0)
    short_lengths = draw_short_lengths(jax.random.fold_in(splits[19], 71), 0)
    query_weight = centred(splits[3], (D, D), D ** -0.5, 0.21875, ((1, 2),))
    query_bias = centred(splits[4], (D,), 0.5, 3.0, ((0, 2),), jnp.float32)
    key_weight = centred(splits[5], (D, D), D ** -0.5, 0.21875, ((1, 2),))
    value_weight = centred(splits[6], (D, D), D ** -0.5, 0.21875, ((1, 2),))
    value_bias = centred(splits[7], (D,), 0.5, 3.0, ((0, 2),), jnp.float32)
    output_weight = centred(splits[8], (D, D), (D // 16) ** -0.5, 0.875, ((0, 2),))
    output_bias = centred(splits[9], (D,), 0.5, 3.0, (), jnp.float32)
    first_gain = jnp.clip(1.0 + 0.15 * jax.random.normal(splits[10], (D,), jnp.float32), 0.25, 1.75)
    first_shift = centred(splits[11], (D,), 0.5, 3.0, (), jnp.float32)
    inner_weight = centred(splits[12], (D, FF), D ** -0.5, 0.21875, ((1, 2),))
    inner_bias = centred(splits[13], (FF,), 0.5, 3.0, ((0, 2),), jnp.float32)
    outer_weight = centred(splits[14], (FF, D), FF ** -0.5, 0.109375, ((0, 2),))
    outer_bias = centred(splits[15], (D,), 0.5, 3.0, (), jnp.float32)
    second_gain = jnp.clip(1.0 + 0.15 * jax.random.normal(splits[16], (D,), jnp.float32), 0.25, 1.75)
    second_shift = centred(splits[17], (D,), 0.5, 3.0, (), jnp.float32)
    out_grad = bell_draw_with(splits[18], (TOKENS, D), 1.0, 6.0, ((0, 16),), (0, 1, 16, 2.0))
    return {"tokens": tokens, "long_lengths": long_lengths, "short_lengths": short_lengths, "query_weight": query_weight, "query_bias": query_bias, "key_weight": key_weight, "value_weight": value_weight, "value_bias": value_bias, "output_weight": output_weight, "output_bias": output_bias, "first_gain": first_gain, "first_shift": first_shift, "inner_weight": inner_weight, "inner_bias": inner_bias, "outer_weight": outer_weight, "outer_bias": outer_bias, "second_gain": second_gain, "second_shift": second_shift, "out_grad": out_grad}


@jax.custom_vjp
def low(v):
    return lax.optimization_barrier(v.astype(jnp.bfloat16)).astype(jnp.float32)

@jax.custom_vjp
def low_back(v):
    return v

def low_keep(v):
    return (low(v), None)

def low_pass(kept, grad):
    return (grad,)

def back_keep(v):
    return (v, None)

def back_low(kept, grad):
    return (low(grad),)
low.defvjp(low_keep, low_pass)
low_back.defvjp(back_keep, back_low)
high = lax.Precision.HIGHEST
eps_norm = 1e-05

def matmul(left, right):
    return jnp.dot(left, right, precision=high)

def normalize(values):
    centered = values - lax.optimization_barrier(jnp.mean(values, axis=-1, keepdims=True))
    spread = lax.optimization_barrier(jnp.mean(centered * centered, axis=-1, keepdims=True))
    return centered * lax.rsqrt(spread + eps_norm)

def key_usable(lengths, key_count):
    return jnp.arange(key_count, dtype=jnp.int32)[None, :] < lengths[:, None]

def token_usable(long_lengths, short_lengths):
    first = key_usable(long_lengths, LONG).reshape(-1)
    second = key_usable(short_lengths, SHORT).reshape(-1)
    return jnp.concatenate([first, second]).astype(jnp.float32)

def attend(queries, key_rows, values, lengths):
    scale = HEAD_DIM ** (-0.5)
    raw = jnp.einsum('bqhe,bkhe->bhqk', queries, key_rows, precision=high)
    scores = low_back(raw * scale)
    usable = key_usable(lengths, key_rows.shape[1])
    scores = jnp.where(usable[:, None, None, :], scores, -1e+30)
    top = lax.optimization_barrier(jnp.max(scores, axis=-1, keepdims=True))
    powers = jnp.exp(scores - top)
    weights = low(powers / lax.optimization_barrier(jnp.sum(powers, axis=-1, keepdims=True)))
    return jnp.einsum('bhqk,bkhe->bqhe', weights, values, precision=high)

def layer(inputs, long_lengths, short_lengths, usable, query_weight, query_bias, key_weight, value_weight, value_bias, output_weight, output_bias, first_gain, first_shift, inner_weight, inner_bias, outer_weight, outer_bias, second_gain, second_shift):
    queries = low_back(low(matmul(inputs, query_weight) + query_bias))
    key_rows = low_back(low(matmul(inputs, key_weight)))
    values = low_back(low(matmul(inputs, value_weight) + value_bias))
    long_rows = long_lengths.shape[0] * LONG

    def bucket(array, length):
        return array.reshape(-1, length, HEADS, HEAD_DIM)
    long_ctx = attend(bucket(queries[:long_rows], LONG), bucket(key_rows[:long_rows], LONG), bucket(values[:long_rows], LONG), long_lengths)
    short_ctx = attend(bucket(queries[long_rows:], SHORT), bucket(key_rows[long_rows:], SHORT), bucket(values[long_rows:], SHORT), short_lengths)
    context = low_back(low(jnp.concatenate([long_ctx.reshape(-1, D), short_ctx.reshape(-1, D)], 0)))
    group = D // N_TENSOR
    attn_total = 0.0
    for g in range(N_TENSOR):
        attn_total = attn_total + low(matmul(context[:, g * group:(g + 1) * group], output_weight[g * group:(g + 1) * group]))
    attention_branch = low_back(attn_total) + output_bias
    first_sum = inputs + attention_branch
    normed = normalize(first_sum) * first_gain + first_shift
    inner = low_back(matmul(low(normed), inner_weight) + inner_bias)
    active = low(jax.nn.gelu(inner, approximate=False))
    width = FF // N_TENSOR
    ffn_total = 0.0
    for g in range(N_TENSOR):
        ffn_total = ffn_total + low(matmul(active[:, g * width:(g + 1) * width], outer_weight[g * width:(g + 1) * width]))
    ffn_branch = low_back(ffn_total) + outer_bias
    second_sum = normed + ffn_branch
    result = normalize(second_sum) * second_gain + second_shift
    moments = (jnp.sum(usable * lax.optimization_barrier(jnp.sum(first_sum * first_sum, axis=-1))), jnp.sum(usable * lax.optimization_barrier(jnp.sum(attention_branch * attention_branch, axis=-1))), jnp.sum(usable * lax.optimization_barrier(jnp.sum(ffn_branch * ffn_branch, axis=-1))), jnp.sum(usable))
    return (result, moments)

def reference(tokens, long_lengths, short_lengths, query_weight, query_bias, key_weight, value_weight, value_bias, output_weight, output_bias, first_gain, first_shift, inner_weight, inner_bias, outer_weight, outer_bias, second_gain, second_shift, out_grad):
    weights_all = tuple((w.astype(jnp.float32) for w in (query_weight, query_bias, key_weight, value_weight, value_bias, output_weight, output_bias, first_gain, first_shift, inner_weight, inner_bias, outer_weight, outer_bias, second_gain, second_shift)))
    token_groups = tokens.reshape(N_DP, TOK_DEV, D)
    grad_groups = out_grad.reshape(N_DP, TOK_DEV, D)
    long_groups = long_lengths.reshape(N_DP, NL_DEV)
    short_groups = short_lengths.reshape(N_DP, NS_DEV)

    def one_group(running, slices_in):
        grad_total, moment_total = running
        group_tokens, group_long, group_short, group_grad = slices_in
        usable = token_usable(group_long, group_short)

        def forward(inputs, *weights):
            return layer(inputs, group_long, group_short, usable, *weights)
        result, pullback, moments = jax.vjp(forward, group_tokens.astype(jnp.float32), *weights_all, has_aux=True)
        gradients = pullback(group_grad.astype(jnp.float32) * usable[:, None])
        grad_total = tuple((a + b for a, b in zip(grad_total, gradients[1:])))
        moment_total = tuple((a + b for a, b in zip(moment_total, moments)))
        return ((grad_total, moment_total), (result.astype(jnp.bfloat16), gradients[0].astype(jnp.bfloat16)))
    start = (tuple((jnp.zeros_like(w) for w in weights_all)), tuple((jnp.zeros((), jnp.float32) for _ in range(4))))
    (gradients, moments), (outputs, input_grads) = lax.scan(one_group, start, (token_groups, long_groups, short_groups, grad_groups))
    count = moments[3] * D
    return (outputs.reshape(TOKENS, D), input_grads.reshape(TOKENS, D), gradients[0], gradients[1], gradients[2], gradients[3], gradients[4], gradients[5], gradients[6], gradients[7], gradients[8], gradients[9], gradients[10], gradients[11], gradients[12], gradients[13], gradients[14], jnp.sqrt(moments[0] / count), jnp.sqrt(moments[1] / count), jnp.sqrt(moments[2] / count))
```

```python
import jax
import jax.numpy as jnp
from jax import lax
from jax.experimental import pallas as pl
from jax.experimental.pallas import tpu as pltpu
from jax.sharding import PartitionSpec as P

D = 768
HEAD_DIM = 64
LONG = 512
SHORT = 256
eps_norm = 1e-05
bf = jnp.bfloat16
f32 = jnp.float32

def nt(a,b): return lax.dot_general(a,b,(((1,),(1,)),((),())),preferred_element_type=f32)
def nn(a,b): return lax.dot_general(a,b,(((1,),(0,)),((),())),preferred_element_type=f32)
def tn(a,b): return lax.dot_general(a,b,(((0,),(0,)),((),())),preferred_element_type=f32)

def fwd_seq(lens_ref, idx, q_ref,k_ref,v_ref,ctx_ref,linv_ref,e_ref, row, size, e_at):
    rows=pl.ds(row,size)
    lane=lax.broadcasted_iota(jnp.int32,(size,128),1)
    low=lane<64
    pos=lax.broadcasted_iota(jnp.int32,(size,128),0)
    bias=jnp.where(pos<lens_ref[idx],0.0,-1e30).astype(bf)
    q=q_ref[rows,:]*jnp.asarray(0.125,bf); k=k_ref[rows,:]; v=v_ref[rows,:]
    one=jnp.ones((),bf); zero=jnp.zeros((),bf)
    outs=[]
    for h in range(2):
        mine=low if h==0 else ~low
        flag=lane==(64 if h==0 else 0)
        qh=jnp.where(mine,q,jnp.where(flag,one,zero))
        kh=jnp.where(mine,k,jnp.where(flag,bias,zero))
        vh=jnp.where(mine,v,one)
        s=nt(qh,kh)
        m=jnp.max(s,axis=-1,keepdims=True)
        e=jnp.exp(s-m).astype(bf)
        e_ref[e_at(h)]=e
        outs.append(nn(e,vh))
    num=jnp.where(low,outs[0],outs[1])
    den=pltpu.roll(jnp.where(low,outs[1],outs[0]),64,1)
    inv=1.0/den
    linv_ref[rows,:]=inv
    ctx_ref[rows,:]=(num*inv).astype(bf)

def fwd_kernel(lens_ref,q_ref,k_ref,v_ref,ctx_ref,linv_ref,el_ref,es_ref):
    fwd_seq(lens_ref,0,q_ref,k_ref,v_ref,ctx_ref,linv_ref,el_ref,0,LONG,lambda h:(0,h))
    for s in range(2):
        fwd_seq(lens_ref,1+s,q_ref,k_ref,v_ref,ctx_ref,linv_ref,es_ref,LONG+s*SHORT,SHORT,lambda h,s=s:(0,2*s+h))

def attend_fwd(lens,q,k,v):
    pairs=q.shape[1]//128
    T=q.shape[0]
    col=pl.BlockSpec((T,128),lambda i,*_:(0,i))
    return pl.pallas_call(fwd_kernel,
        out_shape=(jax.ShapeDtypeStruct(q.shape,bf),jax.ShapeDtypeStruct(q.shape,f32),
                   jax.ShapeDtypeStruct((pairs,2,LONG,LONG),bf),jax.ShapeDtypeStruct((pairs,4,SHORT,SHORT),bf)),
        grid_spec=pltpu.PrefetchScalarGridSpec(num_scalar_prefetch=1,grid=(pairs,),
            in_specs=[col,col,col],
            out_specs=[col,col,pl.BlockSpec((1,2,LONG,LONG),lambda i,*_:(i,0,0,0)),pl.BlockSpec((1,4,SHORT,SHORT),lambda i,*_:(i,0,0,0))]),
        compiler_params=pltpu.CompilerParams(vmem_limit_bytes=48<<20),
        cost_estimate=pl.CostEstimate(flops=int(3e9),bytes_accessed=int(10e6),transcendentals=int(2.4e6)),
        name="attend_fwd")(lens,q,k,v)

def bwd_seq(q_ref,k_ref,v_ref,ctx_ref,linv_ref,g_ref,e_ref,dq_ref,dk_ref,dv_ref,row,size,e_at):
    rows=pl.ds(row,size)
    lane=lax.broadcasted_iota(jnp.int32,(size,128),1)
    low=lane<64
    q=q_ref[rows,:]*jnp.asarray(0.125,bf); k=k_ref[rows,:]*jnp.asarray(0.125,bf); v=v_ref[rows,:]
    g=g_ref[rows,:].astype(f32)*linv_ref[rows,:]
    prod=g*ctx_ref[rows,:].astype(f32)
    gl=g.astype(bf)
    one=jnp.ones((),bf); zero=jnp.zeros((),bf)
    dqs=[];dks=[];dvs=[]
    for h in range(2):
        mine=low if h==0 else ~low
        base=64 if h==0 else 0
        delta=-jnp.sum(jnp.where(mine,prod,0.0),axis=-1,keepdims=True)
        hi=delta.astype(bf); lo=(delta-hi.astype(f32)).astype(bf)
        gh=jnp.where(mine,gl,jnp.where(lane==base,hi,jnp.where(lane==base+1,lo,zero)))
        vh=jnp.where(mine,v,one)
        e=e_ref[e_at(h)]
        dp=nt(gh,vh)
        ds=(e.astype(f32)*dp).astype(bf)
        dqs.append(nn(ds,k))
        dks.append(tn(ds,q))
        dvs.append(tn(e,gl))
    dq_ref[rows,:]=jnp.where(low,dqs[0],dqs[1]).astype(bf)
    dk_ref[rows,:]=jnp.where(low,dks[0],dks[1]).astype(bf)
    dv_ref[rows,:]=jnp.where(low,dvs[0],dvs[1]).astype(bf)

def bwd_kernel(q_ref,k_ref,v_ref,ctx_ref,linv_ref,g_ref,el_ref,es_ref,dq_ref,dk_ref,dv_ref):
    bwd_seq(q_ref,k_ref,v_ref,ctx_ref,linv_ref,g_ref,el_ref,dq_ref,dk_ref,dv_ref,0,LONG,lambda h:(0,h))
    for s in range(2):
        bwd_seq(q_ref,k_ref,v_ref,ctx_ref,linv_ref,g_ref,es_ref,dq_ref,dk_ref,dv_ref,LONG+s*SHORT,SHORT,lambda h,s=s:(0,2*s+h))

def attend_bwd(q,k,v,ctx,linv,g,el,es):
    pairs=q.shape[1]//128
    T=q.shape[0]
    col=pl.BlockSpec((T,128),lambda i:(0,i))
    return pl.pallas_call(bwd_kernel,
        out_shape=(jax.ShapeDtypeStruct(q.shape,bf),)*3,
        grid=(pairs,),
        in_specs=[col]*6+[pl.BlockSpec((1,2,LONG,LONG),lambda i:(i,0,0,0)),pl.BlockSpec((1,4,SHORT,SHORT),lambda i:(i,0,0,0))],
        out_specs=[col]*3,
        compiler_params=pltpu.CompilerParams(vmem_limit_bytes=48<<20),
        cost_estimate=pl.CostEstimate(flops=int(6e9),bytes_accessed=int(10e6),transcendentals=0),
        name="attend_bwd")(q,k,v,ctx,linv,g,el,es)

def normalize(values):
    centered = values - jnp.mean(values, axis=-1, keepdims=True)
    inverse_dev = lax.rsqrt(jnp.mean(centered * centered, axis=-1, keepdims=True) + eps_norm)
    return (centered * inverse_dev, inverse_dev)


def norm_backward(scaled, normed, inverse_dev):
    centred_grad = scaled - jnp.mean(scaled, axis=-1, keepdims=True)
    return inverse_dev * (centred_grad - normed * jnp.mean(scaled * normed, axis=-1, keepdims=True))


def swap_tensor(value):
    return lax.ppermute(value, "tensor", [(0, 1), (1, 0)])


def dp_bits():
    count = lax.axis_size("dp")
    bits = []
    while (1 << len(bits)) < count:
        bits.append(1 << len(bits))
    return count, bits


def swap_dp(value, bit):
    count, _ = dp_bits()
    return lax.ppermute(value, "dp", [(i, i ^ bit) for i in range(count)])


def scatter_rows(total, order):
    count, bits = dp_bits()
    rows = total.shape[0] // count
    index = lax.axis_index("dp")
    names = list(reversed(bits))
    view = total.reshape([2] * len(names) + [rows, total.shape[1]])
    for step, bit in enumerate(order):
        axis = names.index(bit)
        mine = (index // bit) % 2
        send = lax.dynamic_index_in_dim(view, 1 - mine, axis, keepdims=False)
        keep = lax.dynamic_index_in_dim(view, mine, axis, keepdims=False)
        view = keep.astype(f32) + swap_dp(send, bit).astype(f32)
        if step < len(order) - 1:
            view = view.astype(bf)
        names.pop(axis)
    return view


def sum_dp(value):
    _, bits = dp_bits()
    for bit in bits:
        value = value + swap_dp(value, bit)
    return value


def rows_here(array, side):
    half = array.shape[0] // 4
    first = lax.dynamic_slice_in_dim(array, side * half, half, 0)
    second = lax.dynamic_slice_in_dim(array, 2 * half + side * half, half, 0)
    return jnp.concatenate([first, second], 0)


def rows_joined(own, other, side):
    half = own.shape[0] // 2
    zero = side == 0
    low, high = (jnp.where(zero, own, other), jnp.where(zero, other, own))
    return jnp.concatenate([low[:half], high[:half], low[half:], high[half:]], 0)


def dot(left, right):
    return jnp.dot(left, right, preferred_element_type=f32)


def dot_nt(left, right):
    return lax.dot_general(left, right, (((1,), (1,)), ((), ())), preferred_element_type=f32)


def dot_tn(left, right):
    return lax.dot_general(left, right, (((0,), (0,)), ((), ())), preferred_element_type=f32)


def local(
    tokens,
    long_lengths,
    short_lengths,
    query_weight,
    query_bias,
    key_weight,
    value_weight,
    value_bias,
    output_weight,
    output_bias,
    first_gain,
    first_shift,
    inner_weight,
    inner_bias,
    outer_weight,
    outer_bias,
    second_gain,
    second_shift,
    out_grad,
):
    side = lax.axis_index("tensor")
    _, bits = dp_bits()
    alternate = bits[1::-1] + bits[2:]
    nl, ns = (long_lengths.shape[0] // 2, short_lengths.shape[0] // 2)
    lens = jnp.concatenate(
        [
            lax.dynamic_slice_in_dim(long_lengths, side * nl, nl),
            lax.dynamic_slice_in_dim(short_lengths, side * ns, ns),
        ]
    )
    qkv_own = jnp.concatenate([query_weight, key_weight, value_weight], 1)
    qkv_other = swap_tensor(qkv_own)
    biases = jnp.concatenate([query_bias, value_bias, inner_bias])
    biases_other = swap_tensor(biases)
    width = query_weight.shape[1]
    output_other = swap_tensor(output_weight)
    inner_other = swap_tensor(inner_weight)
    outer_other = swap_tensor(outer_weight)
    qkv_w = (qkv_own, qkv_other)
    out_w = (output_weight, output_other)
    in_w = (inner_weight, inner_other)
    outer_w = (outer_weight, outer_other)
    bias_q = (query_bias, biases_other[:width])
    bias_v = (value_bias, biases_other[width : 2 * width])
    bias_i = (inner_bias, biases_other[2 * width :])

    x = rows_here(tokens, side)
    xf = x.astype(f32)
    usable = jnp.concatenate(
        [
            (jnp.arange(size, dtype=jnp.int32) < lens[i]).astype(f32)
            for i, size in enumerate([LONG] * nl + [SHORT] * ns)
        ]
    )
    out_cot = rows_here(out_grad, side).astype(f32) * usable[:, None]

    saved = []
    branch = output_bias
    for h in range(2):
        packed = dot(x, qkv_w[h])
        q = (packed[:, :width] + bias_q[h]).astype(bf)
        k = packed[:, width : 2 * width].astype(bf)
        v = (packed[:, 2 * width :] + bias_v[h]).astype(bf)
        ctx, linv, e_long, e_short = attend_fwd(lens, q, k, v)
        saved.append((q, k, v, ctx, linv, e_long, e_short))
        branch = branch + dot(ctx, out_w[h])
    first_sum = xf + branch
    first_normed, first_inverse = normalize(first_sum)
    normed = first_normed * first_gain + first_shift
    normed_low = normed.astype(bf)
    active, slope = ([], [])
    ffn = outer_bias
    for h in range(2):
        inner = dot(normed_low, in_w[h]) + bias_i[h]
        phi = 0.5 * (1.0 + lax.erf(inner * 0.7071067811865476))
        active.append((inner * phi).astype(bf))
        slope.append((phi + inner * (0.3989422804014327 * jnp.exp(-0.5 * inner * inner))).astype(bf))
        ffn = ffn + dot(active[h], outer_w[h])
    second_sum = normed + ffn
    second_normed, second_inverse = normalize(second_sum)
    block_own = (second_normed * second_gain + second_shift).astype(bf)
    block_other = swap_tensor(block_own)
    block_out = rows_joined(block_own, block_other, side)
    squares = [jnp.sum(usable[:, None] * a * a) for a in (first_sum, branch, ffn)]

    second_grad = norm_backward(out_cot * second_gain, second_normed, second_inverse)
    second_low = second_grad.astype(bf)
    outer_part = dot_tn(second_low, active[1]).astype(bf)
    outer_part = dot_tn(second_low, active[0]) + swap_tensor(outer_part).astype(f32)
    outer_rows = scatter_rows(outer_part.astype(bf), bits)
    inner_low = [
        (dot_nt(second_low, outer_w[h]) * slope[h].astype(f32)).astype(bf) for h in range(2)
    ]
    inner_part = dot_tn(normed_low, inner_low[1]).astype(bf)
    inner_part = dot_tn(normed_low, inner_low[0]) + swap_tensor(inner_part).astype(f32)
    inner_rows = scatter_rows(inner_part.astype(bf), alternate)
    normed_grad = second_grad
    for h in range(2):
        normed_grad = normed_grad + dot_nt(inner_low[h], in_w[h])
    first_grad = norm_backward(normed_grad * first_gain, first_normed, first_inverse)
    first_low = first_grad.astype(bf)
    shared = jnp.stack(
        [
            jnp.sum(first_grad, axis=0),
            jnp.sum(normed_grad * first_normed, axis=0),
            jnp.sum(normed_grad, axis=0),
            jnp.sum(second_grad, axis=0),
            jnp.sum(out_cot * second_normed, axis=0),
            jnp.sum(out_cot, axis=0),
            jnp.pad(jnp.stack(squares + [jnp.sum(lens).astype(f32)]), (0, D - 4)),
        ]
    )
    inner_sums = [jnp.sum(inner_low[h], axis=0, dtype=f32).reshape(-1, D) for h in range(2)]
    early = jnp.concatenate([shared, inner_sums[0]]) + swap_tensor(
        jnp.concatenate([shared, inner_sums[1]])
    )
    early = sum_dp(early)

    grads = []
    qkvo = [None, None]
    tokens_part = first_grad
    qv_sums = [None, None]
    for h in (1, 0):
        q, k, v, ctx, linv, e_long, e_short = saved[h]
        context_grad = dot_nt(first_low, out_w[h]).astype(bf)
        dq, dk, dv = attend_bwd(q, k, v, ctx, linv, context_grad, e_long, e_short)
        packed = jnp.concatenate([dq, dk, dv], 1)
        qv_sums[h] = jnp.concatenate([jnp.sum(dq, axis=0, dtype=f32), jnp.sum(dv, axis=0, dtype=f32)])
        qkvo[h] = (dot_tn(x, packed), dot_tn(first_low, ctx))
        tokens_part = tokens_part + dot_nt(packed, qkv_w[h])
    sent = swap_tensor(jnp.concatenate([a.astype(bf) for a in qkvo[1]], 1)).astype(f32)
    qkvo_part = (jnp.concatenate(qkvo[0], 1) + sent).astype(bf)
    half = 2 * width
    first_half = scatter_rows(qkvo_part[:, :half], bits)
    second_half = scatter_rows(qkvo_part[:, half:], alternate)
    late = sum_dp(qv_sums[0] + swap_tensor(qv_sums[1]))
    tokens_own = tokens_part.astype(bf)
    tokens_grad = rows_joined(tokens_own, swap_tensor(tokens_own), side)

    rms = jnp.sqrt(early[6, :3] / (early[6, 3] * D))
    return (
        block_out,
        tokens_grad,
        first_half[:, :width],
        late[:width],
        first_half[:, width:],
        second_half[:, :width],
        late[width:],
        second_half[:, width:].T,
        early[0],
        early[1],
        early[2],
        inner_rows,
        early[7:].reshape(-1),
        outer_rows.T,
        early[3],
        early[4],
        early[5],
        rms[0],
        rms[1],
        rms[2],
    )


def solution(mesh):
    return jax.shard_map(
        local,
        mesh=mesh,
        in_specs=(
            P("dp", None),
            P("dp"),
            P("dp"),
            P(None, "tensor"),
            P("tensor"),
            P(None, "tensor"),
            P(None, "tensor"),
            P("tensor"),
            P("tensor", None),
            P(),
            P(),
            P(),
            P(None, "tensor"),
            P("tensor"),
            P("tensor", None),
            P(),
            P(),
            P(),
            P("dp", None),
        ),
        out_specs=(
            P("dp", None),
            P("dp", None),
            P("dp", "tensor"),
            P("tensor"),
            P("dp", "tensor"),
            P("dp", "tensor"),
            P("tensor"),
            P("tensor", "dp"),
            P(),
            P(),
            P(),
            P("dp", "tensor"),
            P("tensor"),
            P("tensor", "dp"),
            P(),
            P(),
            P(),
            P(),
            P(),
            P(),
        ),
        check_vma=False,
    )
```

```python
import jax
import jax.numpy as jnp
from jax import lax
from jax.experimental import pallas as pl
from jax.experimental.pallas import tpu as pltpu
from jax.sharding import PartitionSpec as P

D = 768
LONG = 512
SHORT = 256
eps_norm = 1e-05
bf = jnp.bfloat16
f32 = jnp.float32


def nt(a, b):
    return lax.dot_general(a, b, (((1,), (1,)), ((), ())), preferred_element_type=f32)


def nn(a, b):
    return lax.dot_general(a, b, (((1,), (0,)), ((), ())), preferred_element_type=f32)


def tn(a, b):
    return lax.dot_general(a, b, (((0,), (0,)), ((), ())), preferred_element_type=f32)


def slots(rows):
    longs = rows // 2 // LONG
    shorts = rows // 2 // SHORT
    out = [(i * LONG, LONG, i) for i in range(longs)]
    return out + [(rows // 2 + i * SHORT, SHORT, longs + i) for i in range(shorts)]


def row_usable(lens_ref, rows, width):
    pos = lax.broadcasted_iota(jnp.int32, (rows, width), 0)
    out = jnp.zeros((rows, width), f32)
    for first, size, index in slots(rows):
        here = (pos >= first) & (pos < first + lens_ref[index])
        out = jnp.where(here, 1.0, out)
    return out


def pair_forward(length, q, k, v, put):
    size = q.shape[0]
    lane = lax.broadcasted_iota(jnp.int32, (size, 128), 1)
    low = lane < 64
    pos = lax.broadcasted_iota(jnp.int32, (size, 128), 0)
    bias = jnp.where(pos < length, 0.0, -1e30).astype(bf)
    one = jnp.ones((), bf)
    zero = jnp.zeros((), bf)
    es = []
    for h in range(2):
        mine = low if h == 0 else ~low
        flag = lane == (64 if h == 0 else 0)
        qh = jnp.where(mine, q, jnp.where(flag, one, zero))
        kh = jnp.where(mine, k, jnp.where(flag, bias, zero))
        s = nt(qh, kh)
        m = jnp.max(s, axis=-1, keepdims=True)
        e = jnp.exp(s - m).astype(bf)
        put(h, e)
        es.append(e)
    here = jnp.where(low, one, zero)
    there = jnp.where(low, zero, one)
    both = [jnp.concatenate([v * here, here], 1), jnp.concatenate([v * there, there], 1)]
    out = nn(jnp.concatenate(es, 1), jnp.concatenate(both, 0))
    inv = 1.0 / out[:, 128:]
    return out[:, :128] * inv, inv


def attention_forward_kernel(
    lens_ref, x_ref, wq0, wq1, wk0, wk1, wv0, wv1, bq0, bq1, bv0, bv1, wo0, wo1, bo_ref, gain_ref, shift_ref,
    qkv_ref, ctx_ref, inv_ref, el_ref, es_ref, xhat_ref, dev_ref, low_ref, sums_ref, acc_ref,
):
    step = pl.program_id(0)
    rows = x_ref.shape[0]
    x = x_ref[...]
    zero = jnp.zeros((1, 256), f32)
    weights = jnp.concatenate([w[...] for w in (wq0, wq1, wk0, wk1, wv0, wv1)], 1)
    bias = jnp.concatenate([bq0[...], bq1[...], zero, bv0[...], bv1[...]], 1)
    qkv_ref[...] = (nn(x, weights) + bias).astype(bf)
    scale = jnp.asarray(0.125, bf)
    for first, size, index in slots(rows):
        at = pl.ds(first, size)
        length = lens_ref[index]
        for p in range(2):
            cols = pl.ds(128 * p, 128)
            q = qkv_ref[at, 128 * p : 128 * p + 128] * scale
            k = qkv_ref[at, 256 + 128 * p : 384 + 128 * p]
            v = qkv_ref[at, 512 + 128 * p : 640 + 128 * p]

            def put(h, e, p=p, size=size, index=index):
                if size == LONG:
                    el_ref[0, 2 * p + h] = e
                else:
                    es_ref[0, 4 * (index - 1) + 2 * p + h] = e

            ctx, inv = pair_forward(length, q, k, v, put)
            ctx_ref[at, cols] = ctx.astype(bf)
            inv_ref[at, cols] = inv
    part = nn(ctx_ref[...], jnp.concatenate([wo0[...], wo1[...]], 0))

    @pl.when(step == 0)
    def _():
        acc_ref[...] = part

    @pl.when(step > 0)
    def _():
        acc_ref[...] += part

    @pl.when(step == pl.num_programs(0) - 1)
    def _():
        resid = jnp.zeros((1, D), f32)
        attn = jnp.zeros((1, D), f32)
        for first, size, index in slots(rows):
            at = pl.ds(first, size)
            pos = lax.broadcasted_iota(jnp.int32, (size, D), 0)
            usable = pos < lens_ref[index]
            branch = acc_ref[at, :] + bo_ref[...]
            total = x_ref[at, :].astype(f32) + branch
            resid += jnp.sum(jnp.where(usable, total * total, 0.0), axis=0, keepdims=True)
            attn += jnp.sum(jnp.where(usable, branch * branch, 0.0), axis=0, keepdims=True)
            centred = total - jnp.mean(total, axis=-1, keepdims=True)
            dev = lax.rsqrt(jnp.mean(centred * centred, axis=-1, keepdims=True) + eps_norm)
            xhat = centred * dev
            xhat_ref[at, :] = xhat
            dev_ref[at, :] = jnp.broadcast_to(dev, (size, 128))
            low_ref[at, :] = (xhat * gain_ref[...] + shift_ref[...]).astype(bf)
        sums_ref[...] = jnp.concatenate([resid, attn, jnp.zeros((6, D), f32)], 0)


def attention_forward(lens, x, wq, wk, wv, bq, bv, wo, bo, gain, shift):
    rows = x.shape[0]
    steps = wq[0].shape[1] // 128
    shorts = rows // 2 // SHORT
    longs = rows // 2 // LONG

    def whole(shape):
        return pl.BlockSpec(shape, lambda i, *_: (0,) * len(shape))

    wide = pl.BlockSpec((D, 128), lambda i, *_: (0, i))
    line = pl.BlockSpec((1, 128), lambda i, *_: (0, i))
    tall = pl.BlockSpec((128, D), lambda i, *_: (i, 0))
    return pl.pallas_call(
        attention_forward_kernel,
        out_shape=(
            jax.ShapeDtypeStruct((rows, steps * 768), bf),
            jax.ShapeDtypeStruct((rows, steps * 256), bf),
            jax.ShapeDtypeStruct((rows, steps * 256), f32),
            jax.ShapeDtypeStruct((steps, 4 * longs, LONG, LONG), bf),
            jax.ShapeDtypeStruct((steps, 4 * shorts, SHORT, SHORT), bf),
            jax.ShapeDtypeStruct((rows, D), f32),
            jax.ShapeDtypeStruct((rows, 128), f32),
            jax.ShapeDtypeStruct((rows, D), bf),
            jax.ShapeDtypeStruct((8, D), f32),
        ),
        grid_spec=pltpu.PrefetchScalarGridSpec(
            num_scalar_prefetch=1,
            grid=(steps,),
            in_specs=[whole((rows, D))] + [wide] * 6 + [line] * 4 + [tall] * 2 + [whole((1, D))] * 3,
            out_specs=[
                pl.BlockSpec((rows, 768), lambda i, *_: (0, i)),
                pl.BlockSpec((rows, 256), lambda i, *_: (0, i)),
                pl.BlockSpec((rows, 256), lambda i, *_: (0, i)),
                pl.BlockSpec((1, 4 * longs, LONG, LONG), lambda i, *_: (i, 0, 0, 0)),
                pl.BlockSpec((1, 4 * shorts, SHORT, SHORT), lambda i, *_: (i, 0, 0, 0)),
                whole((rows, D)),
                whole((rows, 128)),
                whole((rows, D)),
                whole((8, D)),
            ],
            scratch_shapes=[pltpu.VMEM((rows, D), f32)],
        ),
        compiler_params=pltpu.CompilerParams(vmem_limit_bytes=56 << 20),
        cost_estimate=pl.CostEstimate(flops=int(40e9), bytes_accessed=int(1e6), transcendentals=0),
        name="attention_forward",
    )(lens, x, wq[0], wq[1], wk[0], wk[1], wv[0], wv[1], bq[0], bq[1], bv[0], bv[1], wo[0], wo[1], bo, gain, shift)


def gelu_parts(v):
    cdf = 0.5 * (1.0 + lax.erf(v * 0.7071067811865476))
    return cdf, v * (0.3989422804014327 * jnp.exp(-0.5 * (v * v)))


def ffn_forward_kernel(
    lens_ref, low_ref, wi0, wi1, bi0, bi1, wo0, wo1, xhat_ref, gain1_ref, shift1_ref, bo_ref, gain_ref, shift_ref, grad_ref,
    act0, act1, slope0, slope1, out_ref, back_ref, back_low, sums_ref, acc_ref, *, chunk,
):
    step = pl.program_id(0)
    rows = low_ref.shape[0]
    win = jnp.concatenate([wi0[...], wi1[...]], 1)
    bias = jnp.concatenate([bi0[...], bi1[...]], 1)
    wout = jnp.concatenate([wo0[...], wo1[...]], 0)
    half = wi0.shape[1]

    @pl.when(step == 0)
    def _():
        acc_ref[...] = jnp.zeros_like(acc_ref)

    for first in range(0, rows, chunk):
        at = pl.ds(first, chunk)
        inner = nn(low_ref[at, :], win) + bias
        cdf, bell = gelu_parts(inner)
        active = (inner * cdf).astype(bf)
        slope = (cdf + bell).astype(bf)
        act0[at, :] = active[:, :half]
        act1[at, :] = active[:, half:]
        slope0[at, :] = slope[:, :half]
        slope1[at, :] = slope[:, half:]
        acc_ref[at, :] += nn(active, wout)

    @pl.when(step == pl.num_programs(0) - 1)
    def _():
        ffn_sum = jnp.zeros((1, D), f32)
        gain_sum = jnp.zeros((1, D), f32)
        shift_sum = jnp.zeros((1, D), f32)
        bias_sum = jnp.zeros((1, D), f32)
        for first, size, index in slots(rows):
            at = pl.ds(first, size)
            usable = lax.broadcasted_iota(jnp.int32, (size, D), 0) < lens_ref[index]
            ffn = acc_ref[at, :] + bo_ref[...]
            ffn_sum += jnp.sum(jnp.where(usable, ffn * ffn, 0.0), axis=0, keepdims=True)
            total = xhat_ref[at, :] * gain1_ref[...] + shift1_ref[...] + ffn
            centred = total - jnp.mean(total, axis=-1, keepdims=True)
            dev = lax.rsqrt(jnp.mean(centred * centred, axis=-1, keepdims=True) + eps_norm)
            xhat = centred * dev
            out_ref[at, :] = (xhat * gain_ref[...] + shift_ref[...]).astype(bf)
            cot = jnp.where(usable, grad_ref[at, :].astype(f32), 0.0)
            gain_sum += jnp.sum(cot * xhat, axis=0, keepdims=True)
            shift_sum += jnp.sum(cot, axis=0, keepdims=True)
            u = cot * gain_ref[...]
            slant = jnp.mean(u * xhat, axis=-1, keepdims=True)
            back = dev * (u - jnp.mean(u, axis=-1, keepdims=True) - xhat * slant)
            bias_sum += jnp.sum(back, axis=0, keepdims=True)
            back_ref[at, :] = back
            low = back.astype(bf)
            back_low[at, :] = low
        sums_ref[...] = jnp.concatenate([ffn_sum, gain_sum, shift_sum, bias_sum, jnp.zeros((4, D), f32)], 0)


def whole(shape):
    return pl.BlockSpec(shape, lambda *_: (0,) * len(shape))


def ffn_forward(lens, low, wi, bi, wo, xhat, gain1, shift1, bo, gain, shift, grad, width=512, chunk=512):
    rows = low.shape[0]
    half = wi[0].shape[1]
    cols = pl.BlockSpec((D, width), lambda i, *_: (0, i))
    line = pl.BlockSpec((1, width), lambda i, *_: (0, i))
    tall = pl.BlockSpec((width, D), lambda i, *_: (i, 0))
    act = pl.BlockSpec((rows, width), lambda i, *_: (0, i))
    full = whole((rows, D))
    row = whole((1, D))
    shape = jax.ShapeDtypeStruct
    return pl.pallas_call(
        lambda *refs: ffn_forward_kernel(*refs, chunk=chunk),
        out_shape=(shape((rows, half), bf),) * 4
        + (shape((rows, D), bf), shape((rows, D), f32), shape((rows, D), bf), shape((8, D), f32)),
        grid_spec=pltpu.PrefetchScalarGridSpec(
            num_scalar_prefetch=1,
            grid=(half // width,),
            in_specs=[full, cols, cols, line, line, tall, tall, full, row, row, row, row, row, full],
            out_specs=[act] * 4 + [full] * 3 + [whole((8, D))],
            scratch_shapes=[pltpu.VMEM((rows, D), f32)],
        ),
        compiler_params=pltpu.CompilerParams(vmem_limit_bytes=56 << 20),
        cost_estimate=pl.CostEstimate(flops=int(40e9), bytes_accessed=int(1e6), transcendentals=0),
        name="ffn_forward",
    )(lens, low, wi[0], wi[1], bi[0], bi[1], wo[0], wo[1], xhat, gain1, shift1, bo, gain, shift, grad)


def pair_backward(q, k, v, ctx, inv, grad, es):
    size = q.shape[0]
    lane = lax.broadcasted_iota(jnp.int32, (size, 128), 1)
    low = lane < 64
    one = jnp.ones((), bf)
    zero = jnp.zeros((), bf)
    grad = grad * inv
    prod = grad * ctx.astype(f32)
    grad = grad.astype(bf)
    dss = []
    for h in range(2):
        mine = low if h == 0 else ~low
        base = 64 if h == 0 else 0
        delta = -jnp.sum(jnp.where(mine, prod, 0.0), axis=-1, keepdims=True)
        high = delta.astype(bf)
        rest = (delta - high.astype(f32)).astype(bf)
        gh = jnp.where(mine, grad, jnp.where(lane == base, high, jnp.where(lane == base + 1, rest, zero)))
        dp = nt(gh, jnp.where(mine, v, one))
        dss.append((es[h].astype(f32) * dp).astype(bf))
    dq = jnp.where(low, nn(dss[0], k), nn(dss[1], k))
    q_t = q.T
    g_t = grad.T
    dk = jnp.concatenate([nn(q_t[:64], dss[0]), nn(q_t[64:], dss[1])], 0).T
    dv = jnp.concatenate([nn(g_t[:64], es[0]), nn(g_t[64:], es[1])], 0).T
    return dq.astype(bf), dk.astype(bf), dv.astype(bf)


def attention_backward_kernel(
    x_ref, low_ref, qkv_ref, ctx_ref, inv_ref, el_ref, es_ref, wo0, wo1, out_ref, own_ref, other_ref, sums_ref, grad_ref
):
    rows = x_ref.shape[0]
    scale = jnp.asarray(0.125, bf)
    low = low_ref[...]
    grad_ref[...] = nt(low, jnp.concatenate([wo0[...], wo1[...]], 0)).astype(bf)
    for first, size, index in slots(rows):
        at = pl.ds(first, size)
        for p in range(2):
            cols = [slice(256 * i + 128 * p, 256 * i + 128 * p + 128) for i in range(3)]
            q = qkv_ref[at, cols[0]] * scale
            k = qkv_ref[at, cols[1]] * scale
            v = qkv_ref[at, cols[2]]
            if size == LONG:
                es = [el_ref[0, 2 * p + h] for h in range(2)]
            else:
                es = [es_ref[0, 4 * (index - 1) + 2 * p + h] for h in range(2)]
            grads = pair_backward(q, k, v, ctx_ref[at, cols[0]], inv_ref[at, cols[0]], grad_ref[at, cols[0]].astype(f32), es)
            for i in range(3):
                out_ref[at, cols[i]] = grads[i]
    packed = out_ref[...]
    sums_ref[...] = jnp.broadcast_to(jnp.sum(packed.astype(f32), axis=0, keepdims=True), sums_ref.shape)
    wide = tn(x_ref[...], packed).astype(bf)
    tail = tn(low, ctx_ref[...]).astype(bf)
    for side, ref in enumerate((own_ref, other_ref)):
        for i in range(3):
            ref[:, 128 * i : 128 * i + 128] = wide[:, 256 * i + 128 * side : 256 * i + 128 * side + 128]
        ref[:, 384:512] = tail[:, 128 * side : 128 * side + 128]


def attention_backward(x, low, qkv, ctx, inv, e_long, e_short, wo):
    rows = x.shape[0]
    steps = ctx.shape[1] // 256
    full = whole((rows, D))
    tall = pl.BlockSpec((128, D), lambda i: (i, 0))

    def part(height, width):
        return pl.BlockSpec((height, width), lambda i: (0, i))

    shape = jax.ShapeDtypeStruct
    return pl.pallas_call(
        attention_backward_kernel,
        out_shape=(
            shape((rows, 768 * steps), bf),
            shape((D, 512 * steps), bf),
            shape((D, 512 * steps), bf),
            shape((8, 768 * steps), f32),
        ),
        grid=(steps,),
        in_specs=[
            full,
            full,
            part(rows, 768),
            part(rows, 256),
            part(rows, 256),
            pl.BlockSpec((1,) + e_long.shape[1:], lambda i: (i, 0, 0, 0)),
            pl.BlockSpec((1,) + e_short.shape[1:], lambda i: (i, 0, 0, 0)),
            tall,
            tall,
        ],
        out_specs=[part(rows, 768), part(D, 512), part(D, 512), part(8, 768)],
        scratch_shapes=[pltpu.VMEM((rows, 256), bf)],
        compiler_params=pltpu.CompilerParams(vmem_limit_bytes=56 << 20),
        cost_estimate=pl.CostEstimate(flops=int(40e9), bytes_accessed=int(1e6), transcendentals=0),
        name="attention_backward",
    )(x, low, qkv, ctx, inv, e_long, e_short, wo[0], wo[1])


def tokens_backward_kernel(first_ref, packed_ref, wq0, wq1, wk0, wk1, wv0, wv1, out_ref):
    total = first_ref[...]
    for i in range(packed_ref.shape[1] // 768):
        weights = jnp.concatenate([w[:, 128 * i : 128 * i + 128] for w in (wq0, wq1, wk0, wk1, wv0, wv1)], 1)
        total += nt(packed_ref[:, 768 * i : 768 * i + 768], weights)
    out_ref[...] = total.astype(bf)


def tokens_backward(first, packed, wq, wk, wv):
    rows = first.shape[0]
    chunk = 512
    return pl.pallas_call(
        tokens_backward_kernel,
        out_shape=jax.ShapeDtypeStruct((rows, D), bf),
        grid=(rows // chunk,),
        in_specs=[pl.BlockSpec((chunk, D), lambda i: (i, 0)), pl.BlockSpec((chunk, packed.shape[1]), lambda i: (i, 0))]
        + [whole(wq[0].shape)] * 6,
        out_specs=pl.BlockSpec((chunk, D), lambda i: (i, 0)),
        compiler_params=pltpu.CompilerParams(vmem_limit_bytes=40 << 20),
        cost_estimate=pl.CostEstimate(flops=int(1e6), bytes_accessed=int(1e4), transcendentals=0),
        name="tokens_backward",
    )(first, packed, wq[0], wq[1], wk[0], wk[1], wv[0], wv[1])


def ffn_backward_kernel(
    back_low, slope0, slope1, wo0, wo1, wi0, wi1, low_ref, back_ref, xhat_ref, dev_ref, gain_ref,
    own_ref, other_ref, bias0, bias1, first_ref, first_low, sums_ref, inner_ref, acc_ref, *, chunk,
):
    step = pl.program_id(0)
    rows = low_ref.shape[0]
    half = wi0.shape[1]
    wout = jnp.concatenate([wo0[...], wo1[...]], 0)
    win = jnp.concatenate([wi0[...], wi1[...]], 1)

    @pl.when(step == 0)
    def _():
        acc_ref[...] = back_ref[...]

    total = jnp.zeros((1, 2 * half), f32)
    for first in range(0, rows, chunk):
        at = pl.ds(first, chunk)
        slope = jnp.concatenate([slope0[at, :], slope1[at, :]], 1).astype(f32)
        inner = (nt(back_low[at, :], wout) * slope).astype(bf)
        total += jnp.sum(inner.astype(f32), axis=0, keepdims=True)
        inner_ref[at, :] = inner
        acc_ref[at, :] += nt(inner, win)
    bias0[...] = jnp.broadcast_to(total[:, :half], bias0.shape)
    bias1[...] = jnp.broadcast_to(total[:, half:], bias1.shape)
    own_ref[...] = tn(low_ref[...], inner_ref[:, :half]).astype(bf)
    other_ref[...] = tn(low_ref[...], inner_ref[:, half:]).astype(bf)

    @pl.when(step == pl.num_programs(0) - 1)
    def _():
        gain_sum = jnp.zeros((1, D), f32)
        shift_sum = jnp.zeros((1, D), f32)
        bias_sum = jnp.zeros((1, D), f32)
        for first in range(0, rows, chunk):
            at = pl.ds(first, chunk)
            grad = acc_ref[at, :]
            xhat = xhat_ref[at, :]
            gain_sum += jnp.sum(grad * xhat, axis=0, keepdims=True)
            shift_sum += jnp.sum(grad, axis=0, keepdims=True)
            u = grad * gain_ref[...]
            slant = jnp.mean(u * xhat, axis=-1, keepdims=True)
            out = dev_ref[at, 0:1] * (u - jnp.mean(u, axis=-1, keepdims=True) - xhat * slant)
            bias_sum += jnp.sum(out, axis=0, keepdims=True)
            first_ref[at, :] = out
            first_low[at, :] = out.astype(bf)
        sums_ref[...] = jnp.concatenate([bias_sum, gain_sum, shift_sum, jnp.zeros((5, D), f32)], 0)


def ffn_backward(back_low, slope, wo, wi, low, back, xhat, dev, gain, width=512, chunk=512):
    rows = low.shape[0]
    half = wi[0].shape[1]
    cols = pl.BlockSpec((D, width), lambda i: (0, i))
    tall = pl.BlockSpec((width, D), lambda i: (i, 0))
    act = pl.BlockSpec((rows, width), lambda i: (0, i))
    bias = pl.BlockSpec((8, width), lambda i: (0, i))
    full = whole((rows, D))
    shape = jax.ShapeDtypeStruct
    return pl.pallas_call(
        lambda *refs: ffn_backward_kernel(*refs, chunk=chunk),
        out_shape=(shape((D, half), bf),) * 2
        + (shape((8, half), f32),) * 2
        + (shape((rows, D), f32), shape((rows, D), bf), shape((8, D), f32)),
        grid=(half // width,),
        in_specs=[full, act, act, tall, tall, cols, cols, full, full, full, whole((rows, 128)), whole((1, D))],
        out_specs=[cols] * 2 + [bias] * 2 + [full] * 2 + [whole((8, D))],
        scratch_shapes=[pltpu.VMEM((rows, 2 * width), bf), pltpu.VMEM((rows, D), f32)],
        compiler_params=pltpu.CompilerParams(vmem_limit_bytes=58 << 20),
        cost_estimate=pl.CostEstimate(flops=int(40e9), bytes_accessed=int(1e6), transcendentals=0),
        name="ffn_backward",
    )(back_low, slope[0], slope[1], wo[0], wo[1], wi[0], wi[1], low, back, xhat, dev, gain)


def swap_tensor(value):
    return lax.ppermute(value, "tensor", [(0, 1), (1, 0)])


def dp_bits():
    count = lax.axis_size("dp")
    bits = []
    while (1 << len(bits)) < count:
        bits.append(1 << len(bits))
    return count, bits


def swap_dp(value, bit):
    count, _ = dp_bits()
    return lax.ppermute(value, "dp", [(i, i ^ bit) for i in range(count)])


def dot_tn(left, right):
    return lax.dot_general(left, right, (((0,), (0,)), ((), ())), preferred_element_type=f32)


def after(value, *others):
    return lax.optimization_barrier((value,) + others)[0]


class RowScatter:
    def __init__(self, view, names, order):
        self.view, self.names, self.order = (view, list(names), list(order))
        if self.order:
            self.split()

    def split(self):
        bit = self.order[0]
        axis = self.names.index(bit)
        mine = (lax.axis_index("dp") // bit) % 2
        self.send = lax.dynamic_index_in_dim(self.view, 1 - mine, axis, keepdims=False)
        self.keep = lax.dynamic_index_in_dim(self.view, mine, axis, keepdims=False)
        self.names.pop(axis)

    def step(self, *gates):
        if not self.order:
            return
        keep = after(self.keep, *gates) if gates else self.keep
        self.view = keep.astype(f32) + swap_dp(self.send, self.order.pop(0)).astype(f32)
        if self.names:
            self.view = self.view.astype(bf)
        if self.order:
            self.split()


def row_scatter(total, order):
    count, bits = dp_bits()
    view = total.reshape([2] * len(bits) + [total.shape[0] // count, total.shape[1]])
    return RowScatter(view, reversed(bits), order)


def merged(chains, order):
    return RowScatter(jnp.concatenate([chain.view for chain in chains], -1), chains[0].names, order)


def rows_here(array, side):
    half = array.shape[0] // 4
    first = lax.dynamic_slice_in_dim(array, side * half, half, 0)
    second = lax.dynamic_slice_in_dim(array, 2 * half + side * half, half, 0)
    return jnp.concatenate([first, second], 0)


def rows_joined(own, other, side):
    half = own.shape[0] // 2
    zero = side == 0
    low, high = (jnp.where(zero, own, other), jnp.where(zero, other, own))
    return jnp.concatenate([low[:half], high[:half], low[half:], high[half:]], 0)


def local(
    tokens,
    long_lengths,
    short_lengths,
    query_weight,
    query_bias,
    key_weight,
    value_weight,
    value_bias,
    output_weight,
    output_bias,
    first_gain,
    first_shift,
    inner_weight,
    inner_bias,
    outer_weight,
    outer_bias,
    second_gain,
    second_shift,
    out_grad,
):
    side = lax.axis_index("tensor")
    _, bits = dp_bits()
    alternate = bits[1::-1] + bits[2:]
    nl, ns = (long_lengths.shape[0] // 2, short_lengths.shape[0] // 2)
    lens = jnp.concatenate(
        [
            lax.dynamic_slice_in_dim(long_lengths, side * nl, nl),
            lax.dynamic_slice_in_dim(short_lengths, side * ns, ns),
        ]
    )
    width = query_weight.shape[1]
    biases = jnp.concatenate([query_bias, value_bias, inner_bias])
    biases_other = swap_tensor(biases)
    wq = (query_weight, swap_tensor(query_weight))
    wk = (key_weight, swap_tensor(key_weight))
    wv = (value_weight, swap_tensor(value_weight))
    wo = (output_weight, swap_tensor(output_weight))
    wi = (inner_weight, swap_tensor(inner_weight))
    w2 = (outer_weight, swap_tensor(outer_weight))
    bq = (query_bias[None], biases_other[None, :width])
    bv = (value_bias[None], biases_other[None, width : 2 * width])
    bi = (inner_bias[None], biases_other[None, 2 * width :])
    gain1, shift1, gain2, shift2 = (first_gain[None], first_shift[None], second_gain[None], second_shift[None])

    x = rows_here(tokens, side)
    grad = rows_here(out_grad, side)
    qkv, ctx, inv, e_long, e_short, xhat, dev, low, sums_a = attention_forward(
        lens, x, wq, wk, wv, bq, bv, wo, output_bias[None], gain1, shift1
    )
    act0, act1, slope0, slope1, block_own, back, back_low, sums_b = ffn_forward(
        lens, low, wi, bi, w2, xhat, gain1, shift1, outer_bias[None], gain2, shift2, grad
    )
    block_other = swap_tensor(block_own)
    block_out = rows_joined(block_own, block_other, side)

    outer_other = dot_tn(back_low, act1).astype(bf)
    act0 = after(act0, outer_other)
    outer_part = (dot_tn(back_low, act0) + swap_tensor(outer_other).astype(f32)).astype(bf)
    near, far = (bits[:2], bits[2:])
    outer = row_scatter(outer_part, near)
    back_low = after(back_low, outer.send, block_other)
    inner_own, inner_other, bias0, bias1, first, first_low, sums_c = ffn_backward(
        back_low, (slope0, slope1), w2, wi, low, back, xhat, dev, gain1
    )
    outer.step(sums_c)
    inner_own, inner_other, first_low, first = lax.optimization_barrier(
        (inner_own, inner_other, first_low, first, outer.send)
    )[:4]
    inner_part = (inner_own.astype(f32) + swap_tensor(inner_other).astype(f32)).astype(bf)
    half = inner_part.shape[1] // 2
    inner = [row_scatter(inner_part[:, :half], near), row_scatter(inner_part[:, half:], near[::-1])]
    first_low = after(first_low, inner[0].send, inner[1].send)
    packed, own, other, sums_d = attention_backward(x, first_low, qkv, ctx, inv, e_long, e_short, wo)
    outer.step(sums_d)
    for chain in inner:
        chain.step(sums_d)
    packed, own, other, sums_d = lax.optimization_barrier(
        (packed, own, other, sums_d, outer.view, inner[0].send, inner[1].send)
    )[:4]
    qkvo = (own.astype(f32) + swap_tensor(other).astype(f32)).astype(bf)
    half = qkvo.shape[1] // 2
    parts = [row_scatter(qkvo[:, :half], near), row_scatter(qkvo[:, half:], near[::-1])]
    for chain in inner:
        chain.step(parts[0].send, parts[1].send)
    ffn = merged([outer] + inner, far)
    first = after(first, parts[0].send, parts[1].send)
    tokens_own = tokens_backward(first, packed, wq, wk, wv)
    tokens_own, bias0, bias1 = lax.optimization_barrier((tokens_own, bias0, bias1, ffn.send))[:3]
    tokens_grad = rows_joined(tokens_own, swap_tensor(tokens_own), side)
    scalars = jnp.stack([sums_a[0].sum(), sums_a[1].sum(), sums_b[0].sum(), jnp.sum(lens).astype(f32)])
    qv = sums_d[0].reshape(-1, 3, 2, 128)[:, 0::2]
    shared = jnp.concatenate([sums_b[1:4], sums_c[:3], jnp.pad(scalars, (0, D - 4))[None]])
    small, small_other = [
        jnp.concatenate([shared, bias[0].reshape(-1, D), qv[:, :, h].transpose(1, 0, 2).reshape(-1, D)])
        for h, bias in enumerate((bias0, bias1))
    ]
    small = small + swap_tensor(small_other)
    for bit in near:
        for part in parts:
            part.step(small, tokens_own)
        ready = [part.send for part in parts] if parts[0].order else [part.view for part in parts]
        small = after(small, *ready) + swap_dp(small, bit)
        ffn.step(*ready)
    part = merged(parts, far)
    for bit in far:
        part.step(small)
        ready = part.send if part.order else part.view
        small = after(small, ready) + swap_dp(small, bit)
        ffn.step(ready)
    rows = part.view.reshape(part.view.shape[0], -1, 4, 128)
    grads = [rows[:, :, i].reshape(rows.shape[0], width) for i in range(4)]
    early = small[:9]
    late = small[9:].reshape(2, width)
    rms = jnp.sqrt(early[6, :3] / (early[6, 3] * D))
    return (
        block_out,
        tokens_grad,
        grads[0],
        late[0],
        grads[1],
        grads[2],
        late[1],
        grads[3].T,
        early[3],
        early[4],
        early[5],
        ffn.view[:, w2[0].shape[0] :],
        early[7:9].reshape(-1),
        ffn.view[:, : w2[0].shape[0]].T,
        early[2],
        early[0],
        early[1],
        rms[0],
        rms[1],
        rms[2],
    )


def solution(mesh):
    return jax.shard_map(
        local,
        mesh=mesh,
        in_specs=(
            P("dp", None),
            P("dp"),
            P("dp"),
            P(None, "tensor"),
            P("tensor"),
            P(None, "tensor"),
            P(None, "tensor"),
            P("tensor"),
            P("tensor", None),
            P(),
            P(),
            P(),
            P(None, "tensor"),
            P("tensor"),
            P("tensor", None),
            P(),
            P(),
            P(),
            P("dp", None),
        ),
        out_specs=(
            P("dp", None),
            P("dp", None),
            P("dp", "tensor"),
            P("tensor"),
            P("dp", "tensor"),
            P("dp", "tensor"),
            P("tensor"),
            P("tensor", "dp"),
            P(),
            P(),
            P(),
            P("dp", "tensor"),
            P("tensor"),
            P("tensor", "dp"),
            P(),
            P(),
            P(),
            P(),
            P(),
            P(),
        ),
        check_vma=False,
    )
```

```python
import jax
import jax.numpy as jnp
from jax import lax
from jax.experimental import pallas as pl
from jax.experimental.pallas import tpu as pltpu
from jax.sharding import PartitionSpec as P

D = 768
LONG = 512
SHORT = 256
eps_norm = 1e-05
bf = jnp.bfloat16
f32 = jnp.float32
shape = jax.ShapeDtypeStruct


def nt(a, b):
    return lax.dot_general(a, b, (((1,), (1,)), ((), ())), preferred_element_type=f32)


def nn(a, b):
    return lax.dot_general(a, b, (((1,), (0,)), ((), ())), preferred_element_type=f32)


def tn(a, b):
    return lax.dot_general(a, b, (((0,), (0,)), ((), ())), preferred_element_type=f32)


def whole(dims):
    return pl.BlockSpec(dims, lambda *_: (0,) * len(dims))


def anywhere():
    return pl.BlockSpec(memory_space=pl.ANY)


def settings(flops):
    return dict(
        compiler_params=pltpu.CompilerParams(vmem_limit_bytes=58 << 20),
        cost_estimate=pl.CostEstimate(flops=int(flops), bytes_accessed=int(1e6), transcendentals=0),
    )


def line(ref):
    return ref[...].reshape(1, ref.shape[0])


def slots(rows):
    longs = rows // 2 // LONG
    shorts = rows // 2 // SHORT
    out = [(i * LONG, LONG, i) for i in range(longs)]
    return out + [(rows // 2 + i * SHORT, SHORT, longs + i) for i in range(shorts)]


def slot_length(side_ref, long_ref, short_ref, rows, index):
    longs = rows // 2 // LONG
    shorts = rows // 2 // SHORT
    if index < longs:
        return long_ref[side_ref[0] * longs + index]
    return short_ref[side_ref[0] * shorts + index - longs]


def place_rows(ref, value, places):
    if places is None:
        ref[...] = value
        return
    size = value.shape[0] // len(places)
    for i, p in enumerate(places):
        ref[p * size : (p + 1) * size, :] = value[i * size : (i + 1) * size, :]


def pair_forward(length, q, k, v, put):
    size = q.shape[0]
    lane = lax.broadcasted_iota(jnp.int32, (size, 128), 1)
    low = lane < 64
    pos = lax.broadcasted_iota(jnp.int32, (size, 128), 0)
    bias = jnp.where(pos < length, 0.0, -1e30).astype(bf)
    one = jnp.ones((), bf)
    zero = jnp.zeros((), bf)
    es = []
    for h in range(2):
        mine = low if h == 0 else ~low
        flag = lane == (64 if h == 0 else 0)
        qh = jnp.where(mine, q, jnp.where(flag, one, zero))
        kh = jnp.where(mine, k, jnp.where(flag, bias, zero))
        s = nt(qh, kh)
        m = jnp.max(s, axis=-1, keepdims=True)
        e = jnp.exp(s - m).astype(bf)
        put(h, e)
        es.append(e)
    here = jnp.where(low, one, zero)
    there = jnp.where(low, zero, one)
    both = [jnp.concatenate([v * here, here], 1), jnp.concatenate([v * there, there], 1)]
    out = nn(jnp.concatenate(es, 1), jnp.concatenate(both, 0))
    inv = 1.0 / out[:, 128:]
    return out[:, :128] * inv, inv


def attention_forward_kernel(
    side_ref, long_ref, short_ref,
    x0, x1, wq0, wq1, wk0, wk1, wv0, wv1, bq0, bq1, bv0, bv1, wo0, wo1, bo_ref, gain_ref, shift_ref,
    qkv_ref, ctx_ref, inv_ref, el_ref, es_ref, xhat_ref, dev_ref, low_ref, sums_ref, acc_ref,
):
    step = pl.program_id(0)
    half = x0.shape[0]
    rows = 2 * half
    zero = jnp.zeros((1, 256), f32)
    cols = pl.ds(pl.multiple_of(128 * step, 128), 128)
    weights = jnp.concatenate([w[...] for w in (wq0, wq1, wk0, wk1, wv0, wv1)], 1)
    bias = [b[cols].reshape(1, 128) for b in (bq0, bq1, bv0, bv1)]
    bias = jnp.concatenate(bias[:2] + [zero] + bias[2:], 1)
    for i, x in enumerate((x0, x1)):
        qkv_ref[i * half : (i + 1) * half, :] = (nn(x[...], weights) + bias).astype(bf)
    scale = jnp.asarray(0.125, bf)
    for first, size, index in slots(rows):
        at = pl.ds(first, size)
        length = slot_length(side_ref, long_ref, short_ref, rows, index)
        for p in range(2):
            q = qkv_ref[at, 128 * p : 128 * p + 128] * scale
            k = qkv_ref[at, 256 + 128 * p : 384 + 128 * p]
            v = qkv_ref[at, 512 + 128 * p : 640 + 128 * p]

            def put(h, e, p=p, size=size, index=index):
                if size == LONG:
                    el_ref[0, 4 * index + 2 * p + h] = e
                else:
                    es_ref[0, 4 * (index - half // LONG) + 2 * p + h] = e

            ctx, inv = pair_forward(length, q, k, v, put)
            ctx_ref[at, 128 * p : 128 * p + 128] = ctx.astype(bf)
            inv_ref[at, 128 * p : 128 * p + 128] = inv
    part = nn(ctx_ref[...], jnp.concatenate([wo0[...], wo1[...]], 0))

    @pl.when(step == 0)
    def _():
        acc_ref[...] = part

    @pl.when(step > 0)
    def _():
        acc_ref[...] += part

    @pl.when(step == pl.num_programs(0) - 1)
    def _():
        resid = jnp.zeros((1, D), f32)
        attn = jnp.zeros((1, D), f32)
        count = jnp.zeros((), jnp.int32)
        for first, size, index in slots(rows):
            at = pl.ds(first, size)
            length = slot_length(side_ref, long_ref, short_ref, rows, index)
            count += length
            usable = lax.broadcasted_iota(jnp.int32, (size, D), 0) < length
            branch = acc_ref[at, :] + line(bo_ref)
            source = x0[at, :] if first < half else x1[first - half : first - half + size, :]
            total = source.astype(f32) + branch
            resid += jnp.sum(jnp.where(usable, total * total, 0.0), axis=0, keepdims=True)
            attn += jnp.sum(jnp.where(usable, branch * branch, 0.0), axis=0, keepdims=True)
            centred = total - jnp.mean(total, axis=-1, keepdims=True)
            dev = lax.rsqrt(jnp.mean(centred * centred, axis=-1, keepdims=True) + eps_norm)
            xhat = centred * dev
            xhat_ref[at, :] = xhat
            dev_ref[at, :] = jnp.broadcast_to(dev, (size, 128))
            low_ref[at, :] = (xhat * line(gain_ref) + line(shift_ref)).astype(bf)
        count = jnp.full((1, D), count, jnp.int32).astype(f32)
        sums_ref[...] = jnp.concatenate([resid, attn, count, jnp.zeros((5, D), f32)], 0)


def attention_forward(place, tokens, wq, wk, wv, bq, bv, wo, bo, gain, shift):
    half = tokens.shape[0] // 4
    rows = 2 * half
    width = wq[0].shape[1]
    steps = width // 128
    longs = half // LONG
    shorts = half // SHORT
    wide = pl.BlockSpec((D, 128), lambda i, *_: (0, i))
    tall = pl.BlockSpec((128, D), lambda i, *_: (i, 0))

    def part(columns):
        return pl.BlockSpec((rows, columns), lambda i, *_: (0, i))

    return pl.pallas_call(
        attention_forward_kernel,
        out_shape=(
            shape((rows, steps * 768), bf),
            shape((rows, steps * 256), bf),
            shape((rows, steps * 256), f32),
            shape((steps, 4 * longs, LONG, LONG), bf),
            shape((steps, 4 * shorts, SHORT, SHORT), bf),
            shape((rows, D), f32),
            shape((rows, 128), f32),
            shape((rows, D), bf),
            shape((8, D), f32),
        ),
        grid_spec=pltpu.PrefetchScalarGridSpec(
            num_scalar_prefetch=3,
            grid=(steps,),
            in_specs=[
                pl.BlockSpec((half, D), lambda i, side, *_: (side[0], 0)),
                pl.BlockSpec((half, D), lambda i, side, *_: (2 + side[0], 0)),
            ]
            + [wide] * 6
            + [whole((width,))] * 4
            + [tall] * 2
            + [whole((D,))] * 3,
            out_specs=[
                part(768),
                part(256),
                part(256),
                pl.BlockSpec((1, 4 * longs, LONG, LONG), lambda i, *_: (i, 0, 0, 0)),
                pl.BlockSpec((1, 4 * shorts, SHORT, SHORT), lambda i, *_: (i, 0, 0, 0)),
                whole((rows, D)),
                whole((rows, 128)),
                whole((rows, D)),
                whole((8, D)),
            ],
            scratch_shapes=[pltpu.VMEM((rows, D), f32)],
        ),
        name="attention_forward",
        **settings(40e9),
    )(*place, tokens, tokens, *wq, *wk, *wv, *bq, *bv, *wo, bo, gain, shift)


def gelu_parts(v):
    cdf = 0.5 * (1.0 + lax.erf(v * 0.7071067811865476))
    return cdf, v * (0.3989422804014327 * jnp.exp(-0.5 * (v * v)))


def ffn_forward_kernel(
    side_ref, long_ref, short_ref,
    low_ref, wi0, wi1, bi0, bi1, wo0, wo1, xhat_hbm, grad_hbm, gain1_ref, shift1_ref, bo_ref, gain_ref, shift_ref,
    act0, slope0, slope1, out_hbm, back_hbm, low_hbm, other_ref, sums_ref,
    acc_ref, act1, xhat_ref, grad_ref, out_ref, back_low, in_sem, out_sem, *, chunk, places,
):
    step = pl.program_id(0)
    rows = low_ref.shape[0]
    half = rows // 2
    width = wi0.shape[1]
    fetches = [pltpu.make_async_copy(xhat_hbm, xhat_ref, in_sem.at[0])]
    for i in range(2):
        source = grad_hbm.at[pl.ds(pl.multiple_of((2 * i + side_ref[0]) * half, half), half), :]
        fetches.append(pltpu.make_async_copy(source, grad_ref.at[i * half : (i + 1) * half, :], in_sem.at[1 + i]))

    @pl.when(step == 0)
    def _():
        for fetch in fetches:
            fetch.start()

    cols = pl.ds(pl.multiple_of(width * step, width), width)
    win = jnp.concatenate([wi0[...], wi1[...]], 1)
    bias = jnp.concatenate([b[cols].reshape(1, width) for b in (bi0, bi1)], 1)
    wout = jnp.concatenate([wo0[...], wo1[...]], 0)
    for first in range(0, rows, chunk):
        at = pl.ds(first, chunk)
        inner = nn(low_ref[at, :], win) + bias
        cdf, bell = gelu_parts(inner)
        active = (inner * cdf).astype(bf)
        slope = (cdf + bell).astype(bf)
        act0[at, :] = active[:, :width]
        act1[at, cols] = active[:, width:]
        slope0[at, :] = slope[:, :width]
        slope1[at, :] = slope[:, width:]
        part = nn(active, wout)

        @pl.when(step == 0)
        def _():
            acc_ref[at, :] = part

        @pl.when(step > 0)
        def _():
            acc_ref[at, :] += part

    @pl.when(step == pl.num_programs(0) - 1)
    def _():
        for fetch in fetches:
            fetch.wait()
        ffn_sum = jnp.zeros((1, D), f32)
        gain_sum = jnp.zeros((1, D), f32)
        shift_sum = jnp.zeros((1, D), f32)
        bias_sum = jnp.zeros((1, D), f32)
        stores = []
        for i, (first, size, index) in enumerate(slots(rows)):
            at = pl.ds(first, size)
            length = slot_length(side_ref, long_ref, short_ref, rows, index)
            usable = lax.broadcasted_iota(jnp.int32, (size, D), 0) < length
            ffn = acc_ref[at, :] + line(bo_ref)
            ffn_sum += jnp.sum(jnp.where(usable, ffn * ffn, 0.0), axis=0, keepdims=True)
            total = xhat_ref[at, :] * line(gain1_ref) + line(shift1_ref) + ffn
            centred = total - jnp.mean(total, axis=-1, keepdims=True)
            dev = lax.rsqrt(jnp.mean(centred * centred, axis=-1, keepdims=True) + eps_norm)
            xhat = centred * dev
            out_ref[at, :] = (xhat * line(gain_ref) + line(shift_ref)).astype(bf)
            cot = jnp.where(usable, grad_ref[at, :].astype(f32), 0.0)
            gain_sum += jnp.sum(cot * xhat, axis=0, keepdims=True)
            shift_sum += jnp.sum(cot, axis=0, keepdims=True)
            u = cot * line(gain_ref)
            slant = jnp.mean(u * xhat, axis=-1, keepdims=True)
            back = dev * (u - jnp.mean(u, axis=-1, keepdims=True) - xhat * slant)
            bias_sum += jnp.sum(back, axis=0, keepdims=True)
            acc_ref[at, :] = back
            back_low[at, :] = back.astype(bf)
            for j, (source, target) in enumerate(((out_ref, out_hbm), (acc_ref, back_hbm), (back_low, low_hbm))):
                store = pltpu.make_async_copy(source.at[at, :], target.at[at, :], out_sem.at[3 * i + j])
                store.start()
                stores.append(store)
        sums_ref[...] = jnp.concatenate([ffn_sum, gain_sum, shift_sum, bias_sum, jnp.zeros((4, D), f32)], 0)
        place_rows(other_ref, tn(back_low[...], act1[...]).astype(bf), places)
        for store in stores:
            store.wait()


def ffn_forward(place, low, wi, bi, wo, xhat, grad, gain1, shift1, bo, gain, shift, places, width=512, chunk=512):
    rows = low.shape[0]
    half = wi[0].shape[1]
    cols = pl.BlockSpec((D, width), lambda i, *_: (0, i))
    tall = pl.BlockSpec((width, D), lambda i, *_: (i, 0))
    act = pl.BlockSpec((rows, width), lambda i, *_: (0, i))
    row = whole((D,))
    count = len(slots(rows))
    return pl.pallas_call(
        lambda *refs: ffn_forward_kernel(*refs, chunk=chunk, places=places),
        out_shape=(shape((rows, half), bf),) * 3
        + (shape((rows, D), bf), shape((rows, D), f32), shape((rows, D), bf), shape((D, half), bf), shape((8, D), f32)),
        grid_spec=pltpu.PrefetchScalarGridSpec(
            num_scalar_prefetch=3,
            grid=(half // width,),
            in_specs=[whole((rows, D)), cols, cols, whole((half,)), whole((half,)), tall, tall, anywhere(), anywhere()] + [row] * 5,
            out_specs=[act] * 3 + [anywhere()] * 3 + [whole((D, half)), whole((8, D))],
            scratch_shapes=[
                pltpu.VMEM((rows, D), f32),
                pltpu.VMEM((rows, half), bf),
                pltpu.VMEM((rows, D), f32),
                pltpu.VMEM((rows, D), bf),
                pltpu.VMEM((rows, D), bf),
                pltpu.VMEM((rows, D), bf),
                pltpu.SemaphoreType.DMA((3,)),
                pltpu.SemaphoreType.DMA((3 * count,)),
            ],
        ),
        name="ffn_forward",
        **settings(40e9),
    )(*place, low, *wi, *bi, *wo, xhat, grad, gain1, shift1, bo, gain, shift)


def outer_weight_kernel(low_ref, act_ref, out_ref, *, places):
    place_rows(out_ref, tn(low_ref[...], act_ref[...]).astype(bf), places)


def outer_weight(low, act, places, width=512):
    rows, half = act.shape
    return pl.pallas_call(
        lambda *refs: outer_weight_kernel(*refs, places=places),
        out_shape=shape((D, half), bf),
        grid=(half // width,),
        in_specs=[whole((rows, D)), pl.BlockSpec((rows, width), lambda i: (0, i))],
        out_specs=pl.BlockSpec((D, width), lambda i: (0, i)),
        name="outer_weight",
        **settings(10e9),
    )(low, act)


def ffn_backward_kernel(
    back_low, slope0, slope1, wo0, wo1, wi0, wi1, low_ref, back_hbm, xhat_hbm, dev_ref, gain_ref,
    own_ref, other_ref, bias0, bias1, first_hbm, low_hbm, sums_ref,
    inner_ref, acc_ref, xhat_ref, first_low, in_sem, out_sem, *, chunk, places,
):
    step = pl.program_id(0)
    rows = low_ref.shape[0]
    half = wi0.shape[1]
    fetches = [
        pltpu.make_async_copy(back_hbm, acc_ref, in_sem.at[0]),
        pltpu.make_async_copy(xhat_hbm, xhat_ref, in_sem.at[1]),
    ]

    @pl.when(step == 0)
    def _():
        for fetch in fetches:
            fetch.start()

    wout = jnp.concatenate([wo0[...], wo1[...]], 0)
    win = jnp.concatenate([wi0[...], wi1[...]], 1)
    total = jnp.zeros((1, 2 * half), f32)
    for first in range(0, rows, chunk):
        at = pl.ds(first, chunk)
        slope = jnp.concatenate([slope0[at, :], slope1[at, :]], 1).astype(f32)
        inner = (nt(back_low[at, :], wout) * slope).astype(bf)
        total += jnp.sum(inner.astype(f32), axis=0, keepdims=True)
        inner_ref[at, :] = inner
    bias0[...] = jnp.broadcast_to(total[:, :half], bias0.shape)
    bias1[...] = jnp.broadcast_to(total[:, half:], bias1.shape)
    place_rows(own_ref, tn(low_ref[...], inner_ref[:, :half]).astype(bf), places)
    place_rows(other_ref, tn(low_ref[...], inner_ref[:, half:]).astype(bf), places)

    @pl.when(step == 0)
    def _():
        for fetch in fetches:
            fetch.wait()

    for first in range(0, rows, chunk):
        at = pl.ds(first, chunk)
        acc_ref[at, :] += nt(inner_ref[at, :], win)

    @pl.when(step == pl.num_programs(0) - 1)
    def _():
        gain_sum = jnp.zeros((1, D), f32)
        shift_sum = jnp.zeros((1, D), f32)
        bias_sum = jnp.zeros((1, D), f32)
        stores = []
        for i, first in enumerate(range(0, rows, chunk)):
            at = pl.ds(first, chunk)
            grad = acc_ref[at, :]
            xhat = xhat_ref[at, :]
            gain_sum += jnp.sum(grad * xhat, axis=0, keepdims=True)
            shift_sum += jnp.sum(grad, axis=0, keepdims=True)
            u = grad * line(gain_ref)
            slant = jnp.mean(u * xhat, axis=-1, keepdims=True)
            out = dev_ref[at, 0:1] * (u - jnp.mean(u, axis=-1, keepdims=True) - xhat * slant)
            bias_sum += jnp.sum(out, axis=0, keepdims=True)
            acc_ref[at, :] = out
            first_low[at, :] = out.astype(bf)
            for j, (source, target) in enumerate(((acc_ref, first_hbm), (first_low, low_hbm))):
                store = pltpu.make_async_copy(source.at[at, :], target.at[at, :], out_sem.at[2 * i + j])
                store.start()
                stores.append(store)
        sums_ref[...] = jnp.concatenate([bias_sum, gain_sum, shift_sum, jnp.zeros((5, D), f32)], 0)
        for store in stores:
            store.wait()


def ffn_backward(back_low, slope, wo, wi, low, back, xhat, dev, gain, places, width=512, chunk=512):
    rows = low.shape[0]
    half = wi[0].shape[1]
    cols = pl.BlockSpec((D, width), lambda i: (0, i))
    tall = pl.BlockSpec((width, D), lambda i: (i, 0))
    act = pl.BlockSpec((rows, width), lambda i: (0, i))
    bias = pl.BlockSpec((8, width), lambda i: (0, i))
    full = whole((rows, D))
    return pl.pallas_call(
        lambda *refs: ffn_backward_kernel(*refs, chunk=chunk, places=places),
        out_shape=(shape((D, half), bf),) * 2
        + (shape((8, half), f32),) * 2
        + (shape((rows, D), f32), shape((rows, D), bf), shape((8, D), f32)),
        grid=(half // width,),
        in_specs=[full, act, act, tall, tall, cols, cols, full, anywhere(), anywhere(), whole((rows, 128)), whole((D,))],
        out_specs=[cols] * 2 + [bias] * 2 + [anywhere()] * 2 + [whole((8, D))],
        scratch_shapes=[
            pltpu.VMEM((rows, 2 * width), bf),
            pltpu.VMEM((rows, D), f32),
            pltpu.VMEM((rows, D), f32),
            pltpu.VMEM((rows, D), bf),
            pltpu.SemaphoreType.DMA((2,)),
            pltpu.SemaphoreType.DMA((2 * (rows // chunk),)),
        ],
        name="ffn_backward",
        **settings(40e9),
    )(back_low, *slope, *wo, *wi, low, back, xhat, dev, gain)


def pair_backward(q, k, v, ctx, inv, grad, es):
    size = q.shape[0]
    lane = lax.broadcasted_iota(jnp.int32, (size, 128), 1)
    low = lane < 64
    one = jnp.ones((), bf)
    zero = jnp.zeros((), bf)
    grad = grad * inv
    prod = grad * ctx.astype(f32)
    grad = grad.astype(bf)
    dss = []
    for h in range(2):
        mine = low if h == 0 else ~low
        base = 64 if h == 0 else 0
        delta = -jnp.sum(jnp.where(mine, prod, 0.0), axis=-1, keepdims=True)
        high = delta.astype(bf)
        rest = (delta - high.astype(f32)).astype(bf)
        gh = jnp.where(mine, grad, jnp.where(lane == base, high, jnp.where(lane == base + 1, rest, zero)))
        dp = nt(gh, jnp.where(mine, v, one))
        dss.append((es[h].astype(f32) * dp).astype(bf))
    dq = jnp.where(low, nn(dss[0], k), nn(dss[1], k))
    q_t = q.T
    g_t = grad.T
    dk = jnp.concatenate([nn(q_t[:64], dss[0]), nn(q_t[64:], dss[1])], 0).T
    dv = jnp.concatenate([nn(g_t[:64], es[0]), nn(g_t[64:], es[1])], 0).T
    return dq.astype(bf), dk.astype(bf), dv.astype(bf)


def attention_backward_kernel(
    side_ref, x0, x1, low_ref, qkv_ref, ctx_ref, inv_ref, el_ref, es_ref, wo0, wo1, sums_a, sums_b, sums_c, bias0, bias1,
    out_ref, own_a, own_b, other_a, other_b, small0, small1, grad_ref, *, places_a, places_b,
):
    step = pl.program_id(0)
    half = x0.shape[0]
    rows = 2 * half
    scale = jnp.asarray(0.125, bf)
    low = low_ref[...]
    grad_ref[...] = nt(low, jnp.concatenate([wo0[...], wo1[...]], 0)).astype(bf)
    for first, size, index in slots(rows):
        at = pl.ds(first, size)
        for p in range(2):
            cols = [slice(256 * i + 128 * p, 256 * i + 128 * p + 128) for i in range(3)]
            q = qkv_ref[at, cols[0]] * scale
            k = qkv_ref[at, cols[1]] * scale
            v = qkv_ref[at, cols[2]]
            if size == LONG:
                es = [el_ref[0, 4 * index + 2 * p + h] for h in range(2)]
            else:
                es = [es_ref[0, 4 * (index - half // LONG) + 2 * p + h] for h in range(2)]
            grads = pair_backward(q, k, v, ctx_ref[at, cols[0]], inv_ref[at, cols[0]], grad_ref[at, cols[0]].astype(f32), es)
            for i in range(3):
                out_ref[at, cols[i]] = grads[i]
    packed = out_ref[...]
    wide = (tn(x0[...], packed[:half]) + tn(x1[...], packed[half:])).astype(bf)
    tail = tn(low, ctx_ref[...]).astype(bf)
    for side, (ref_a, ref_b) in enumerate(((own_a, own_b), (other_a, other_b))):
        pieces = [wide[:, 256 * i + 128 * side : 256 * i + 128 * side + 128] for i in range(3)]
        pieces.append(tail[:, 128 * side : 128 * side + 128])
        place_rows(ref_a, jnp.concatenate(pieces[:2], 1), places_a)
        place_rows(ref_b, jnp.concatenate(pieces[2:], 1), places_b)

    @pl.when(step == 0)
    def _():
        for ref, bias in ((small0, bias0), (small1, bias1)):
            ref[0:3, :] = sums_b[1:4, :]
            ref[3:6, :] = sums_c[0:3, :]
            ref[6:8, :] = sums_a[0:2, :]
            ref[8:9, :] = sums_b[0:1, :]
            ref[9:10, :] = sums_a[2:3, :]
            for i in range(bias.shape[1] // D):
                ref[10 + i : 11 + i, :] = bias[0:1, D * i : D * i + D]
            ref[12:16, :] = jnp.zeros((4, D), f32)

    sums = jnp.sum(packed.astype(f32), axis=0, keepdims=True)
    for side, ref in enumerate((small0, small1)):
        for i in range(2):
            start = pl.multiple_of(i * (D // 2) + 128 * step, 128)
            ref[12:13, pl.ds(start, 128)] = sums[:, 512 * i + 128 * side : 512 * i + 128 * side + 128]


def attention_backward(place, tokens, low, qkv, ctx, inv, e_long, e_short, wo, sums, bias, places_a, places_b):
    half = tokens.shape[0] // 4
    rows = 2 * half
    steps = ctx.shape[1] // 256
    tall = pl.BlockSpec((128, D), lambda i, *_: (i, 0))

    def part(height, width):
        return pl.BlockSpec((height, width), lambda i, *_: (0, i))

    return pl.pallas_call(
        lambda *refs: attention_backward_kernel(*refs, places_a=places_a, places_b=places_b),
        out_shape=(shape((rows, 768 * steps), bf),) + (shape((D, 256 * steps), bf),) * 4 + (shape((16, D), f32),) * 2,
        grid_spec=pltpu.PrefetchScalarGridSpec(
            num_scalar_prefetch=1,
            grid=(steps,),
            in_specs=[
                pl.BlockSpec((half, D), lambda i, side, *_: (side[0], 0)),
                pl.BlockSpec((half, D), lambda i, side, *_: (2 + side[0], 0)),
                whole((rows, D)),
                part(rows, 768),
                part(rows, 256),
                part(rows, 256),
                pl.BlockSpec((1,) + e_long.shape[1:], lambda i, *_: (i, 0, 0, 0)),
                pl.BlockSpec((1,) + e_short.shape[1:], lambda i, *_: (i, 0, 0, 0)),
                tall,
                tall,
            ]
            + [whole((8, D))] * 3
            + [whole(bias[0].shape)] * 2,
            out_specs=[part(rows, 768)] + [part(D, 256)] * 4 + [whole((16, D))] * 2,
            scratch_shapes=[pltpu.VMEM((rows, 256), bf)],
        ),
        name="attention_backward",
        **settings(40e9),
    )(place[0], tokens, tokens, low, qkv, ctx, inv, e_long, e_short, *wo, *sums, *bias)


def tokens_backward_kernel(first_ref, packed_ref, wq0, wq1, wk0, wk1, wv0, wv1, out_ref):
    total = first_ref[...]
    for i in range(packed_ref.shape[1] // 768):
        weights = jnp.concatenate([w[:, 128 * i : 128 * i + 128] for w in (wq0, wq1, wk0, wk1, wv0, wv1)], 1)
        total += nt(packed_ref[:, 768 * i : 768 * i + 768], weights)
    out_ref[...] = total.astype(bf)


def tokens_backward(first, packed, wq, wk, wv):
    rows = first.shape[0]
    chunk = 512
    return pl.pallas_call(
        tokens_backward_kernel,
        out_shape=shape((rows, D), bf),
        grid=(rows // chunk,),
        in_specs=[pl.BlockSpec((chunk, D), lambda i: (i, 0)), pl.BlockSpec((chunk, packed.shape[1]), lambda i: (i, 0))]
        + [whole(wq[0].shape)] * 6,
        out_specs=pl.BlockSpec((chunk, D), lambda i: (i, 0)),
        name="tokens_backward",
        **settings(1e6),
    )(first, packed, *wq, *wk, *wv)


def join_kernel(side_ref, own_ref, other_ref, out_ref):
    step = pl.program_id(0)

    @pl.when(step < 2)
    def _():
        out_ref[...] = own_ref[...]

    @pl.when(step >= 2)
    def _():
        out_ref[...] = other_ref[...]


def join_rows(place, own, other):
    half = own.shape[0] // 2
    return pl.pallas_call(
        join_kernel,
        out_shape=shape((2 * own.shape[0], D), own.dtype),
        grid_spec=pltpu.PrefetchScalarGridSpec(
            num_scalar_prefetch=1,
            grid=(4,),
            in_specs=[
                pl.BlockSpec((half, D), lambda i, side: (jnp.minimum(i, 1), 0)),
                pl.BlockSpec((half, D), lambda i, side: (jnp.maximum(i - 2, 0), 0)),
            ],
            out_specs=pl.BlockSpec(
                (half, D), lambda i, side: (2 * (i % 2) + jnp.where(i < 2, side[0], 1 - side[0]), 0)
            ),
        ),
        name="join_rows",
        **settings(1e6),
    )(place[0], own, other)


def swap_tensor(value):
    return lax.ppermute(value, "tensor", [(0, 1), (1, 0)])


def dp_bits():
    count = lax.axis_size("dp")
    bits = []
    while (1 << len(bits)) < count:
        bits.append(1 << len(bits))
    return count, bits


def swap_dp(value, bit):
    count, _ = dp_bits()
    return lax.ppermute(value, "dp", [(i, i ^ bit) for i in range(count)])


def after(value, *others):
    return lax.optimization_barrier((value,) + others)[0]


def places_of(order):
    count, bits = dp_bits()
    out = []
    for i in range(count):
        position = 0
        for bit in order:
            position = 2 * position + (i // bit) % 2
        out.append(position)
    return out


class RowScatter:
    def __init__(self, own, other, order, placed):
        if not placed:
            count, _ = dp_bits()
            places = places_of(order)
            source = [places.index(p) for p in range(count)]
            size = own.shape[0] // count
            own, other = [
                jnp.concatenate([v[i * size : (i + 1) * size] for i in source], 0) for v in (own, other)
            ]
        self.pair, self.order = ((own, other), list(order))
        self.split()

    def pick(self, side):
        size = self.pair[0].shape[0] // 2
        a, b = [lax.dynamic_slice_in_dim(v, side * size, size, 0).astype(f32) for v in self.pair]
        return (a + b).astype(bf)

    def split(self):
        mine = (lax.axis_index("dp") // self.order[0]) % 2
        self.send, self.keep = (self.pick(1 - mine), self.pick(mine))

    def step(self, *gates):
        keep = after(self.keep, *gates) if gates else self.keep
        self.pair = (keep, swap_dp(self.send, self.order.pop(0)))
        if self.order:
            self.split()

    def total(self):
        return self.pair[0].astype(f32) + self.pair[1].astype(f32)

    def ready(self):
        return self.send if self.order else self.pair[1]


def local(
    tokens,
    long_lengths,
    short_lengths,
    query_weight,
    query_bias,
    key_weight,
    value_weight,
    value_bias,
    output_weight,
    output_bias,
    first_gain,
    first_shift,
    inner_weight,
    inner_bias,
    outer_weight_here,
    outer_bias,
    second_gain,
    second_shift,
    out_grad,
):
    count, bits = dp_bits()
    order_a, order_b = (bits, bits[1::-1] + bits[2:])
    placed = D % (16 * count) == 0
    places_a, places_b = [places_of(order) if placed else None for order in (order_a, order_b)]
    width = query_weight.shape[1]
    place = (lax.axis_index("tensor").reshape(1), long_lengths, short_lengths)
    bq, bv, bi, wq, wk, wv, wo, wi, w2 = [
        (v, swap_tensor(v))
        for v in (
            query_bias,
            value_bias,
            inner_bias,
            query_weight,
            key_weight,
            value_weight,
            output_weight,
            inner_weight,
            outer_weight_here,
        )
    ]
    qkv, ctx, inv, e_long, e_short, xhat, dev, low, sums_a = attention_forward(
        place, tokens, wq, wk, wv, bq, bv, wo, output_bias, first_gain, first_shift
    )
    act, slope0, slope1, block_own, back, back_low, outer_other, sums_b = ffn_forward(
        place, low, wi, bi, w2, xhat, out_grad, first_gain, first_shift, outer_bias, second_gain, second_shift, places_a
    )
    outer_other = swap_tensor(outer_other)
    outer = RowScatter(outer_weight(back_low, act, places_a), outer_other, order_a, placed)
    block_other = swap_tensor(block_own)
    back_low = after(back_low, outer.send, block_other)
    inner_own, inner_other, bias0, bias1, first, first_low, sums_c = ffn_backward(
        back_low, (slope0, slope1), w2, wi, low, back, xhat, dev, first_gain, places_a
    )
    outer.step(sums_c)
    inner_own, inner_other, first_low, first = lax.optimization_barrier(
        (inner_own, inner_other, first_low, first, outer.send)
    )[:4]
    inner = RowScatter(inner_own, swap_tensor(inner_other), order_a, placed)
    first_low = after(first_low, inner.send)
    packed, own_a, own_b, other_a, other_b, small, small_other = attention_backward(
        place, tokens, first_low, qkv, ctx, inv, e_long, e_short, wo, (sums_a, sums_b, sums_c), (bias0, bias1), places_a, places_b
    )
    outer.step(small)
    inner.step(small)
    own_a, own_b, other_a, other_b, packed, small, small_other, block_own = lax.optimization_barrier(
        (own_a, own_b, other_a, other_b, packed, small, small_other, block_own, outer.send, inner.send)
    )[:8]
    parts = [
        RowScatter(own_a, swap_tensor(other_a), order_a, placed),
        RowScatter(own_b, swap_tensor(other_b), order_b, placed),
    ]
    packed, small_other = lax.optimization_barrier((packed, small_other, parts[0].send, parts[1].send))[:2]
    tokens_own = tokens_backward(first, packed, wq, wk, wv)
    small = small + swap_tensor(small_other)
    gates = [tokens_own]
    for i, bit in enumerate(bits):
        for part in parts:
            part.step(small, *gates)
        ready = [part.ready() for part in parts]
        small = after(small, *ready) + swap_dp(small, bit)
        for chain in (outer, inner):
            if chain.order:
                chain.step(*ready)
        gates = []
        if i == 0:
            tokens_own = after(tokens_own, *ready)
            tokens_other = swap_tensor(tokens_own)
            block_out = join_rows(place, after(block_own, *ready), block_other)
            gates = [block_out]
        if i == 1:
            tokens_grad = join_rows(place, after(tokens_own, *ready), tokens_other)
            gates = [tokens_grad]
    part_a, part_b = [part.total().reshape(D // count, -1, 2, 128) for part in parts]
    query_grad, key_grad, value_grad, output_grad = [
        v[:, :, i].reshape(-1, width) for v in (part_a, part_b) for i in range(2)
    ]
    sums = jnp.sum(small[6:9], axis=1)
    rms = jnp.sqrt(sums / (small[9, 0] * D))
    return (
        block_out,
        tokens_grad,
        query_grad,
        small[12, :width],
        key_grad,
        value_grad,
        small[12, width:],
        output_grad.T,
        small[3],
        small[4],
        small[5],
        inner.total(),
        small[10:12].reshape(-1),
        outer.total().T,
        small[2],
        small[0],
        small[1],
        rms[0],
        rms[1],
        rms[2],
    )


def solution(mesh):
    return jax.shard_map(
        local,
        mesh=mesh,
        in_specs=(
            P("dp", None),
            P("dp"),
            P("dp"),
            P(None, "tensor"),
            P("tensor"),
            P(None, "tensor"),
            P(None, "tensor"),
            P("tensor"),
            P("tensor", None),
            P(),
            P(),
            P(),
            P(None, "tensor"),
            P("tensor"),
            P("tensor", None),
            P(),
            P(),
            P(),
            P("dp", None),
        ),
        out_specs=(
            P("dp", None),
            P("dp", None),
            P("dp", "tensor"),
            P("tensor"),
            P("dp", "tensor"),
            P("dp", "tensor"),
            P("tensor"),
            P("tensor", "dp"),
            P(),
            P(),
            P(),
            P("dp", "tensor"),
            P("tensor"),
            P("tensor", "dp"),
            P(),
            P(),
            P(),
            P(),
            P(),
            P(),
        ),
        check_vma=False,
    )
```

```python
import jax
import jax.numpy as jnp
from jax import lax
from jax.experimental import pallas as pl
from jax.experimental.pallas import tpu as pltpu
from jax.sharding import PartitionSpec as P

D = 768
LONG = 512
SHORT = 256
eps_norm = 1e-05
bf = jnp.bfloat16
f32 = jnp.float32
shape = jax.ShapeDtypeStruct


def nt(a, b):
    return lax.dot_general(a, b, (((1,), (1,)), ((), ())), preferred_element_type=f32)


def nn(a, b):
    return lax.dot_general(a, b, (((1,), (0,)), ((), ())), preferred_element_type=f32)


def tn(a, b):
    return lax.dot_general(a, b, (((0,), (0,)), ((), ())), preferred_element_type=f32)


def whole(dims):
    return pl.BlockSpec(dims, lambda *_: (0,) * len(dims))


def anywhere():
    return pl.BlockSpec(memory_space=pl.ANY)


def settings(flops):
    return dict(
        compiler_params=pltpu.CompilerParams(vmem_limit_bytes=58 << 20),
        cost_estimate=pl.CostEstimate(flops=int(flops), bytes_accessed=int(1e6), transcendentals=0),
    )


def line(ref):
    return ref[...].reshape(1, ref.shape[0])


def slots(rows):
    longs = rows // 2 // LONG
    shorts = rows // 2 // SHORT
    out = [(i * LONG, LONG, i) for i in range(longs)]
    return out + [(rows // 2 + i * SHORT, SHORT, longs + i) for i in range(shorts)]


def slot_length(side_ref, long_ref, short_ref, rows, index):
    longs = rows // 2 // LONG
    shorts = rows // 2 // SHORT
    if index < longs:
        return long_ref[side_ref[0] * longs + index]
    return short_ref[side_ref[0] * shorts + index - longs]


def place_rows(ref, value, places):
    if places is None:
        ref[...] = value
        return
    size = value.shape[0] // len(places)
    for i, p in enumerate(places):
        ref[p * size : (p + 1) * size, :] = value[i * size : (i + 1) * size, :]


def pair_forward(length, q, k, v, put):
    size = q.shape[0]
    lane = lax.broadcasted_iota(jnp.int32, (size, 128), 1)
    low = lane < 64
    pos = lax.broadcasted_iota(jnp.int32, (size, 128), 0)
    bias = jnp.where(pos < length, 0.0, -1e30).astype(bf)
    one = jnp.ones((), bf)
    zero = jnp.zeros((), bf)
    es = []
    for h in range(2):
        mine = low if h == 0 else ~low
        flag = lane == (64 if h == 0 else 0)
        qh = jnp.where(mine, q, jnp.where(flag, one, zero))
        kh = jnp.where(mine, k, jnp.where(flag, bias, zero))
        s = nt(qh, kh)
        m = jnp.max(s, axis=-1, keepdims=True)
        e = jnp.exp(s - m).astype(bf)
        put(h, e)
        es.append(e)
    here = jnp.where(low, one, zero)
    there = jnp.where(low, zero, one)
    both = [jnp.concatenate([v * here, here], 1), jnp.concatenate([v * there, there], 1)]
    out = nn(jnp.concatenate(es, 1), jnp.concatenate(both, 0))
    inv = 1.0 / out[:, 128:]
    return out[:, :128] * inv, inv


def attention_forward_kernel(
    side_ref, long_ref, short_ref,
    x0, x1, wq0, wq1, wk0, wk1, wv0, wv1, bq0, bq1, bv0, bv1, wo0, wo1, bo_ref, gain_ref, shift_ref,
    qkv_ref, ctx_ref, inv_ref, el_ref, es_ref, xhat_ref, dev_ref, low_ref, sums_ref, acc_ref,
):
    step = pl.program_id(0)
    half = x0.shape[0]
    rows = 2 * half
    zero = jnp.zeros((1, 256), f32)
    cols = pl.ds(pl.multiple_of(128 * step, 128), 128)
    weights = jnp.concatenate([w[...] for w in (wq0, wq1, wk0, wk1, wv0, wv1)], 1)
    bias = [b[cols].reshape(1, 128) for b in (bq0, bq1, bv0, bv1)]
    bias = jnp.concatenate(bias[:2] + [zero] + bias[2:], 1)
    for i, x in enumerate((x0, x1)):
        qkv_ref[i * half : (i + 1) * half, :] = (nn(x[...], weights) + bias).astype(bf)
    scale = jnp.asarray(0.125, bf)
    for first, size, index in slots(rows):
        at = pl.ds(first, size)
        length = slot_length(side_ref, long_ref, short_ref, rows, index)
        for p in range(2):
            q = qkv_ref[at, 128 * p : 128 * p + 128] * scale
            k = qkv_ref[at, 256 + 128 * p : 384 + 128 * p]
            v = qkv_ref[at, 512 + 128 * p : 640 + 128 * p]

            def put(h, e, p=p, size=size, index=index):
                if size == LONG:
                    el_ref[0, 4 * index + 2 * p + h] = e
                else:
                    es_ref[0, 4 * (index - half // LONG) + 2 * p + h] = e

            ctx, inv = pair_forward(length, q, k, v, put)
            ctx_ref[at, 128 * p : 128 * p + 128] = ctx.astype(bf)
            inv_ref[at, 128 * p : 128 * p + 128] = inv
    part = nn(ctx_ref[...], jnp.concatenate([wo0[...], wo1[...]], 0))

    @pl.when(step == 0)
    def _():
        acc_ref[...] = part

    @pl.when(step > 0)
    def _():
        acc_ref[...] += part

    @pl.when(step == pl.num_programs(0) - 1)
    def _():
        resid = jnp.zeros((1, D), f32)
        attn = jnp.zeros((1, D), f32)
        count = jnp.zeros((), jnp.int32)
        for first, size, index in slots(rows):
            at = pl.ds(first, size)
            length = slot_length(side_ref, long_ref, short_ref, rows, index)
            count += length
            usable = lax.broadcasted_iota(jnp.int32, (size, D), 0) < length
            branch = acc_ref[at, :] + line(bo_ref)
            source = x0[at, :] if first < half else x1[first - half : first - half + size, :]
            total = source.astype(f32) + branch
            resid += jnp.sum(jnp.where(usable, total * total, 0.0), axis=0, keepdims=True)
            attn += jnp.sum(jnp.where(usable, branch * branch, 0.0), axis=0, keepdims=True)
            centred = total - jnp.mean(total, axis=-1, keepdims=True)
            dev = lax.rsqrt(jnp.mean(centred * centred, axis=-1, keepdims=True) + eps_norm)
            xhat = centred * dev
            xhat_ref[at, :] = xhat
            dev_ref[at, :] = jnp.broadcast_to(dev, (size, 128))
            low_ref[at, :] = (xhat * line(gain_ref) + line(shift_ref)).astype(bf)
        count = jnp.full((1, D), count, jnp.int32).astype(f32)
        sums_ref[...] = jnp.concatenate([resid, attn, count, jnp.zeros((5, D), f32)], 0)


def attention_forward(place, tokens, wq, wk, wv, bq, bv, wo, bo, gain, shift):
    half = tokens.shape[0] // 4
    rows = 2 * half
    width = wq[0].shape[1]
    steps = width // 128
    longs = half // LONG
    shorts = half // SHORT
    wide = pl.BlockSpec((D, 128), lambda i, *_: (0, i))
    tall = pl.BlockSpec((128, D), lambda i, *_: (i, 0))

    def part(columns):
        return pl.BlockSpec((rows, columns), lambda i, *_: (0, i))

    return pl.pallas_call(
        attention_forward_kernel,
        out_shape=(
            shape((rows, steps * 768), bf),
            shape((rows, steps * 256), bf),
            shape((rows, steps * 256), f32),
            shape((steps, 4 * longs, LONG, LONG), bf),
            shape((steps, 4 * shorts, SHORT, SHORT), bf),
            shape((rows, D), f32),
            shape((rows, 128), f32),
            shape((rows, D), bf),
            shape((8, D), f32),
        ),
        grid_spec=pltpu.PrefetchScalarGridSpec(
            num_scalar_prefetch=3,
            grid=(steps,),
            in_specs=[
                pl.BlockSpec((half, D), lambda i, side, *_: (side[0], 0)),
                pl.BlockSpec((half, D), lambda i, side, *_: (2 + side[0], 0)),
            ]
            + [wide] * 6
            + [whole((width,))] * 4
            + [tall] * 2
            + [whole((D,))] * 3,
            out_specs=[
                part(768),
                part(256),
                part(256),
                pl.BlockSpec((1, 4 * longs, LONG, LONG), lambda i, *_: (i, 0, 0, 0)),
                pl.BlockSpec((1, 4 * shorts, SHORT, SHORT), lambda i, *_: (i, 0, 0, 0)),
                whole((rows, D)),
                whole((rows, 128)),
                whole((rows, D)),
                whole((8, D)),
            ],
            scratch_shapes=[pltpu.VMEM((rows, D), f32)],
        ),
        name="attention_forward",
        **settings(40e9),
    )(*place, tokens, tokens, *wq, *wk, *wv, *bq, *bv, *wo, bo, gain, shift)


def gelu_parts(v):
    cdf = 0.5 * (1.0 + lax.erf(v * 0.7071067811865476))
    return cdf, v * (0.3989422804014327 * jnp.exp(-0.5 * (v * v)))


def ffn_forward_kernel(
    side_ref, long_ref, short_ref,
    low_ref, wi0, wi1, bi0, bi1, wo0, wo1, xhat_hbm, grad_hbm, gain1_ref, shift1_ref, bo_ref, gain_ref, shift_ref,
    act0, slope0, slope1, out_hbm, back_hbm, low_hbm, other_ref, sums_ref,
    acc_ref, act1, xhat_ref, grad_ref, out_ref, back_low, in_sem, out_sem, *, chunk, places,
):
    step = pl.program_id(0)
    rows = low_ref.shape[0]
    half = rows // 2
    width = wi0.shape[1]
    fetches = [pltpu.make_async_copy(xhat_hbm, xhat_ref, in_sem.at[0])]
    for i in range(2):
        source = grad_hbm.at[pl.ds(pl.multiple_of((2 * i + side_ref[0]) * half, half), half), :]
        fetches.append(pltpu.make_async_copy(source, grad_ref.at[i * half : (i + 1) * half, :], in_sem.at[1 + i]))

    @pl.when(step == 0)
    def _():
        for fetch in fetches:
            fetch.start()

    cols = pl.ds(pl.multiple_of(width * step, width), width)
    win = jnp.concatenate([wi0[...], wi1[...]], 1)
    bias = jnp.concatenate([b[cols].reshape(1, width) for b in (bi0, bi1)], 1)
    wout = jnp.concatenate([wo0[...], wo1[...]], 0)
    for first in range(0, rows, chunk):
        at = pl.ds(first, chunk)
        inner = nn(low_ref[at, :], win) + bias
        cdf, bell = gelu_parts(inner)
        active = (inner * cdf).astype(bf)
        slope = (cdf + bell).astype(bf)
        act0[at, :] = active[:, :width]
        act1[at, cols] = active[:, width:]
        slope0[at, :] = slope[:, :width]
        slope1[at, :] = slope[:, width:]
        part = nn(active, wout)

        @pl.when(step == 0)
        def _():
            acc_ref[at, :] = part

        @pl.when(step > 0)
        def _():
            acc_ref[at, :] += part

    @pl.when(step == pl.num_programs(0) - 1)
    def _():
        for fetch in fetches:
            fetch.wait()
        ffn_sum = jnp.zeros((1, D), f32)
        gain_sum = jnp.zeros((1, D), f32)
        shift_sum = jnp.zeros((1, D), f32)
        bias_sum = jnp.zeros((1, D), f32)
        stores = []
        for i, (first, size, index) in enumerate(slots(rows)):
            at = pl.ds(first, size)
            length = slot_length(side_ref, long_ref, short_ref, rows, index)
            usable = lax.broadcasted_iota(jnp.int32, (size, D), 0) < length
            ffn = acc_ref[at, :] + line(bo_ref)
            ffn_sum += jnp.sum(jnp.where(usable, ffn * ffn, 0.0), axis=0, keepdims=True)
            total = xhat_ref[at, :] * line(gain1_ref) + line(shift1_ref) + ffn
            centred = total - jnp.mean(total, axis=-1, keepdims=True)
            dev = lax.rsqrt(jnp.mean(centred * centred, axis=-1, keepdims=True) + eps_norm)
            xhat = centred * dev
            out_ref[at, :] = (xhat * line(gain_ref) + line(shift_ref)).astype(bf)
            cot = jnp.where(usable, grad_ref[at, :].astype(f32), 0.0)
            gain_sum += jnp.sum(cot * xhat, axis=0, keepdims=True)
            shift_sum += jnp.sum(cot, axis=0, keepdims=True)
            u = cot * line(gain_ref)
            slant = jnp.mean(u * xhat, axis=-1, keepdims=True)
            back = dev * (u - jnp.mean(u, axis=-1, keepdims=True) - xhat * slant)
            bias_sum += jnp.sum(back, axis=0, keepdims=True)
            acc_ref[at, :] = back
            back_low[at, :] = back.astype(bf)
            for j, (source, target) in enumerate(((out_ref, out_hbm), (acc_ref, back_hbm), (back_low, low_hbm))):
                store = pltpu.make_async_copy(source.at[at, :], target.at[at, :], out_sem.at[3 * i + j])
                store.start()
                stores.append(store)
        sums_ref[...] = jnp.concatenate([ffn_sum, gain_sum, shift_sum, bias_sum, jnp.zeros((4, D), f32)], 0)
        place_rows(other_ref, tn(back_low[...], act1[...]).astype(bf), places)
        for store in stores:
            store.wait()


def ffn_forward(place, low, wi, bi, wo, xhat, grad, gain1, shift1, bo, gain, shift, places, width=512, chunk=512):
    rows = low.shape[0]
    half = wi[0].shape[1]
    cols = pl.BlockSpec((D, width), lambda i, *_: (0, i))
    tall = pl.BlockSpec((width, D), lambda i, *_: (i, 0))
    act = pl.BlockSpec((rows, width), lambda i, *_: (0, i))
    row = whole((D,))
    count = len(slots(rows))
    return pl.pallas_call(
        lambda *refs: ffn_forward_kernel(*refs, chunk=chunk, places=places),
        out_shape=(shape((rows, half), bf),) * 3
        + (shape((rows, D), bf), shape((rows, D), f32), shape((rows, D), bf), shape((D, half), bf), shape((8, D), f32)),
        grid_spec=pltpu.PrefetchScalarGridSpec(
            num_scalar_prefetch=3,
            grid=(half // width,),
            in_specs=[whole((rows, D)), cols, cols, whole((half,)), whole((half,)), tall, tall, anywhere(), anywhere()] + [row] * 5,
            out_specs=[act] * 3 + [anywhere()] * 3 + [whole((D, half)), whole((8, D))],
            scratch_shapes=[
                pltpu.VMEM((rows, D), f32),
                pltpu.VMEM((rows, half), bf),
                pltpu.VMEM((rows, D), f32),
                pltpu.VMEM((rows, D), bf),
                pltpu.VMEM((rows, D), bf),
                pltpu.VMEM((rows, D), bf),
                pltpu.SemaphoreType.DMA((3,)),
                pltpu.SemaphoreType.DMA((3 * count,)),
            ],
        ),
        name="ffn_forward",
        **settings(40e9),
    )(*place, low, *wi, *bi, *wo, xhat, grad, gain1, shift1, bo, gain, shift)


def outer_weight_kernel(low_ref, act_ref, out_ref, *, places):
    place_rows(out_ref, tn(low_ref[...], act_ref[...]).astype(bf), places)


def outer_weight(low, act, places, width=512):
    rows, half = act.shape
    return pl.pallas_call(
        lambda *refs: outer_weight_kernel(*refs, places=places),
        out_shape=shape((D, half), bf),
        grid=(half // width,),
        in_specs=[whole((rows, D)), pl.BlockSpec((rows, width), lambda i: (0, i))],
        out_specs=pl.BlockSpec((D, width), lambda i: (0, i)),
        name="outer_weight",
        **settings(10e9),
    )(low, act)


def ffn_backward_kernel(
    back_low, slope0, slope1, wo0, wo1, wi0, wi1, low_ref, back_hbm, xhat_hbm, dev_ref, gain_ref,
    own_ref, other_ref, bias0, bias1, first_hbm, low_hbm, sums_ref,
    inner_ref, acc_ref, xhat_ref, first_low, in_sem, out_sem, *, chunk, places,
):
    step = pl.program_id(0)
    rows = low_ref.shape[0]
    half = wi0.shape[1]
    fetches = [
        pltpu.make_async_copy(back_hbm, acc_ref, in_sem.at[0]),
        pltpu.make_async_copy(xhat_hbm, xhat_ref, in_sem.at[1]),
    ]

    @pl.when(step == 0)
    def _():
        for fetch in fetches:
            fetch.start()

    wout = jnp.concatenate([wo0[...], wo1[...]], 0)
    win = jnp.concatenate([wi0[...], wi1[...]], 1)
    total = jnp.zeros((1, 2 * half), f32)
    for first in range(0, rows, chunk):
        at = pl.ds(first, chunk)
        slope = jnp.concatenate([slope0[at, :], slope1[at, :]], 1).astype(f32)
        inner = (nt(back_low[at, :], wout) * slope).astype(bf)
        total += jnp.sum(inner.astype(f32), axis=0, keepdims=True)
        inner_ref[at, :] = inner
    bias0[...] = jnp.broadcast_to(total[:, :half], bias0.shape)
    bias1[...] = jnp.broadcast_to(total[:, half:], bias1.shape)
    place_rows(own_ref, tn(low_ref[...], inner_ref[:, :half]).astype(bf), places)
    place_rows(other_ref, tn(low_ref[...], inner_ref[:, half:]).astype(bf), places)

    @pl.when(step == 0)
    def _():
        for fetch in fetches:
            fetch.wait()

    for first in range(0, rows, chunk):
        at = pl.ds(first, chunk)
        acc_ref[at, :] += nt(inner_ref[at, :], win)

    @pl.when(step == pl.num_programs(0) - 1)
    def _():
        gain_sum = jnp.zeros((1, D), f32)
        shift_sum = jnp.zeros((1, D), f32)
        bias_sum = jnp.zeros((1, D), f32)
        stores = []
        for i, first in enumerate(range(0, rows, chunk)):
            at = pl.ds(first, chunk)
            grad = acc_ref[at, :]
            xhat = xhat_ref[at, :]
            gain_sum += jnp.sum(grad * xhat, axis=0, keepdims=True)
            shift_sum += jnp.sum(grad, axis=0, keepdims=True)
            u = grad * line(gain_ref)
            slant = jnp.mean(u * xhat, axis=-1, keepdims=True)
            out = dev_ref[at, 0:1] * (u - jnp.mean(u, axis=-1, keepdims=True) - xhat * slant)
            bias_sum += jnp.sum(out, axis=0, keepdims=True)
            acc_ref[at, :] = out
            first_low[at, :] = out.astype(bf)
            for j, (source, target) in enumerate(((acc_ref, first_hbm), (first_low, low_hbm))):
                store = pltpu.make_async_copy(source.at[at, :], target.at[at, :], out_sem.at[2 * i + j])
                store.start()
                stores.append(store)
        sums_ref[...] = jnp.concatenate([bias_sum, gain_sum, shift_sum, jnp.zeros((5, D), f32)], 0)
        for store in stores:
            store.wait()


def ffn_backward(back_low, slope, wo, wi, low, back, xhat, dev, gain, places, width=512, chunk=512):
    rows = low.shape[0]
    half = wi[0].shape[1]
    cols = pl.BlockSpec((D, width), lambda i: (0, i))
    tall = pl.BlockSpec((width, D), lambda i: (i, 0))
    act = pl.BlockSpec((rows, width), lambda i: (0, i))
    bias = pl.BlockSpec((8, width), lambda i: (0, i))
    full = whole((rows, D))
    return pl.pallas_call(
        lambda *refs: ffn_backward_kernel(*refs, chunk=chunk, places=places),
        out_shape=(shape((D, half), bf),) * 2
        + (shape((8, half), f32),) * 2
        + (shape((rows, D), f32), shape((rows, D), bf), shape((8, D), f32)),
        grid=(half // width,),
        in_specs=[full, act, act, tall, tall, cols, cols, full, anywhere(), anywhere(), whole((rows, 128)), whole((D,))],
        out_specs=[cols] * 2 + [bias] * 2 + [anywhere()] * 2 + [whole((8, D))],
        scratch_shapes=[
            pltpu.VMEM((rows, 2 * width), bf),
            pltpu.VMEM((rows, D), f32),
            pltpu.VMEM((rows, D), f32),
            pltpu.VMEM((rows, D), bf),
            pltpu.SemaphoreType.DMA((2,)),
            pltpu.SemaphoreType.DMA((2 * (rows // chunk),)),
        ],
        name="ffn_backward",
        **settings(40e9),
    )(back_low, *slope, *wo, *wi, low, back, xhat, dev, gain)


def pair_backward(q, k, v, ctx, inv, grad, es):
    size = q.shape[0]
    lane = lax.broadcasted_iota(jnp.int32, (size, 128), 1)
    low = lane < 64
    one = jnp.ones((), bf)
    zero = jnp.zeros((), bf)
    grad = grad * inv
    prod = grad * ctx.astype(f32)
    grad = grad.astype(bf)
    dss = []
    for h in range(2):
        mine = low if h == 0 else ~low
        base = 64 if h == 0 else 0
        delta = -jnp.sum(jnp.where(mine, prod, 0.0), axis=-1, keepdims=True)
        high = delta.astype(bf)
        rest = (delta - high.astype(f32)).astype(bf)
        gh = jnp.where(mine, grad, jnp.where(lane == base, high, jnp.where(lane == base + 1, rest, zero)))
        dp = nt(gh, jnp.where(mine, v, one))
        dss.append((es[h].astype(f32) * dp).astype(bf))
    dq = jnp.where(low, nn(dss[0], k), nn(dss[1], k))
    q_t = q.T
    g_t = grad.T
    dk = jnp.concatenate([nn(q_t[:64], dss[0]), nn(q_t[64:], dss[1])], 0).T
    dv = jnp.concatenate([nn(g_t[:64], es[0]), nn(g_t[64:], es[1])], 0).T
    return dq.astype(bf), dk.astype(bf), dv.astype(bf)


def attention_backward_kernel(
    side_ref, x0, x1, low_ref, qkv_ref, ctx_ref, inv_ref, el_ref, es_ref, wo0, wo1, sums_a, sums_b, sums_c, bias0, bias1,
    out_ref, own_a, own_b, other_a, other_b, small0, small1, grad_ref, *, places_a, places_b,
):
    step = pl.program_id(0)
    half = x0.shape[0]
    rows = 2 * half
    scale = jnp.asarray(0.125, bf)
    low = low_ref[...]
    grad_ref[...] = nt(low, jnp.concatenate([wo0[...], wo1[...]], 0)).astype(bf)
    for first, size, index in slots(rows):
        at = pl.ds(first, size)
        for p in range(2):
            cols = [slice(256 * i + 128 * p, 256 * i + 128 * p + 128) for i in range(3)]
            q = qkv_ref[at, cols[0]] * scale
            k = qkv_ref[at, cols[1]] * scale
            v = qkv_ref[at, cols[2]]
            if size == LONG:
                es = [el_ref[0, 4 * index + 2 * p + h] for h in range(2)]
            else:
                es = [es_ref[0, 4 * (index - half // LONG) + 2 * p + h] for h in range(2)]
            grads = pair_backward(q, k, v, ctx_ref[at, cols[0]], inv_ref[at, cols[0]], grad_ref[at, cols[0]].astype(f32), es)
            for i in range(3):
                out_ref[at, cols[i]] = grads[i]
    packed = out_ref[...]
    wide = (tn(x0[...], packed[:half]) + tn(x1[...], packed[half:])).astype(bf)
    tail = tn(low, ctx_ref[...]).astype(bf)
    for side, (ref_a, ref_b) in enumerate(((own_a, own_b), (other_a, other_b))):
        pieces = [wide[:, 256 * i + 128 * side : 256 * i + 128 * side + 128] for i in range(3)]
        pieces.append(tail[:, 128 * side : 128 * side + 128])
        place_rows(ref_a, jnp.concatenate(pieces[:2], 1), places_a)
        place_rows(ref_b, jnp.concatenate(pieces[2:], 1), places_b)

    @pl.when(step == 0)
    def _():
        for ref, bias in ((small0, bias0), (small1, bias1)):
            ref[0:3, :] = sums_b[1:4, :]
            ref[3:6, :] = sums_c[0:3, :]
            ref[6:8, :] = sums_a[0:2, :]
            ref[8:9, :] = sums_b[0:1, :]
            ref[9:10, :] = sums_a[2:3, :]
            for i in range(bias.shape[1] // D):
                ref[10 + i : 11 + i, :] = bias[0:1, D * i : D * i + D]
            ref[12:16, :] = jnp.zeros((4, D), f32)

    sums = jnp.sum(packed.astype(f32), axis=0, keepdims=True)
    for side, ref in enumerate((small0, small1)):
        for i in range(2):
            start = pl.multiple_of(i * (D // 2) + 128 * step, 128)
            ref[12:13, pl.ds(start, 128)] = sums[:, 512 * i + 128 * side : 512 * i + 128 * side + 128]


def attention_backward(place, tokens, low, qkv, ctx, inv, e_long, e_short, wo, sums, bias, places_a, places_b):
    half = tokens.shape[0] // 4
    rows = 2 * half
    steps = ctx.shape[1] // 256
    tall = pl.BlockSpec((128, D), lambda i, *_: (i, 0))

    def part(height, width):
        return pl.BlockSpec((height, width), lambda i, *_: (0, i))

    return pl.pallas_call(
        lambda *refs: attention_backward_kernel(*refs, places_a=places_a, places_b=places_b),
        out_shape=(shape((rows, 768 * steps), bf),) + (shape((D, 256 * steps), bf),) * 4 + (shape((16, D), f32),) * 2,
        grid_spec=pltpu.PrefetchScalarGridSpec(
            num_scalar_prefetch=1,
            grid=(steps,),
            in_specs=[
                pl.BlockSpec((half, D), lambda i, side, *_: (side[0], 0)),
                pl.BlockSpec((half, D), lambda i, side, *_: (2 + side[0], 0)),
                whole((rows, D)),
                part(rows, 768),
                part(rows, 256),
                part(rows, 256),
                pl.BlockSpec((1,) + e_long.shape[1:], lambda i, *_: (i, 0, 0, 0)),
                pl.BlockSpec((1,) + e_short.shape[1:], lambda i, *_: (i, 0, 0, 0)),
                tall,
                tall,
            ]
            + [whole((8, D))] * 3
            + [whole(bias[0].shape)] * 2,
            out_specs=[part(rows, 768)] + [part(D, 256)] * 4 + [whole((16, D))] * 2,
            scratch_shapes=[pltpu.VMEM((rows, 256), bf)],
        ),
        name="attention_backward",
        **settings(1e6),
    )(place[0], tokens, tokens, low, qkv, ctx, inv, e_long, e_short, *wo, *sums, *bias)


def tokens_backward_kernel(first_ref, packed_ref, wq0, wq1, wk0, wk1, wv0, wv1, out_ref):
    total = first_ref[...]
    for i in range(packed_ref.shape[1] // 768):
        weights = jnp.concatenate([w[:, 128 * i : 128 * i + 128] for w in (wq0, wq1, wk0, wk1, wv0, wv1)], 1)
        total += nt(packed_ref[:, 768 * i : 768 * i + 768], weights)
    out_ref[...] = total.astype(bf)


def tokens_backward(first, packed, wq, wk, wv):
    rows = first.shape[0]
    chunk = 512
    return pl.pallas_call(
        tokens_backward_kernel,
        out_shape=shape((rows, D), bf),
        grid=(rows // chunk,),
        in_specs=[pl.BlockSpec((chunk, D), lambda i: (i, 0)), pl.BlockSpec((chunk, packed.shape[1]), lambda i: (i, 0))]
        + [whole(wq[0].shape)] * 6,
        out_specs=pl.BlockSpec((chunk, D), lambda i: (i, 0)),
        name="tokens_backward",
        **settings(1e6),
    )(first, packed, *wq, *wk, *wv)


def join_kernel(side_ref, own_ref, other_ref, out_ref, sems):
    half = own_ref.shape[0] // 2
    copies = []
    for i, ref in enumerate((own_ref, other_ref)):
        for j in range(2):
            block = 2 * j + (side_ref[0] if i == 0 else 1 - side_ref[0])
            target = out_ref.at[pl.ds(pl.multiple_of(block * half, half), half), :]
            copies.append(pltpu.make_async_copy(ref.at[j * half : (j + 1) * half, :], target, sems.at[2 * i + j]))
    for copy in copies:
        copy.start()
    for copy in copies:
        copy.wait()


def join_rows(place, own, other):
    return pl.pallas_call(
        join_kernel,
        out_shape=shape((2 * own.shape[0], D), own.dtype),
        grid_spec=pltpu.PrefetchScalarGridSpec(
            num_scalar_prefetch=1,
            grid=(1,),
            in_specs=[anywhere(), anywhere()],
            out_specs=anywhere(),
            scratch_shapes=[pltpu.SemaphoreType.DMA((4,))],
        ),
        name="join_rows",
        **settings(1e6),
    )(place[0], own, other)


def finish_kernel(keep_a, recv_a, keep_b, recv_b, query_ref, key_ref, value_ref, output_ref):
    pairs = []
    for keep, recv in ((keep_a, recv_a), (keep_b, recv_b)):
        total = keep[...].astype(f32) + recv[...].astype(f32)
        for i in range(2):
            blocks = [total[:, 256 * j + 128 * i : 256 * j + 128 * i + 128] for j in range(total.shape[1] // 256)]
            pairs.append(jnp.concatenate(blocks, 1))
    query_ref[...] = pairs[0]
    key_ref[...] = pairs[1]
    value_ref[...] = pairs[2]
    output_ref[...] = pairs[3]


def finish(pair_a, pair_b):
    rows, columns = pair_a[0].shape
    width = columns // 2
    return pl.pallas_call(
        finish_kernel,
        out_shape=(shape((rows, width), f32),) * 4,
        name="finish",
        **settings(1e6),
    )(*pair_a, *pair_b)


def swap_tensor(value):
    return lax.ppermute(value, "tensor", [(0, 1), (1, 0)])


def dp_bits():
    count = lax.axis_size("dp")
    bits = []
    while (1 << len(bits)) < count:
        bits.append(1 << len(bits))
    return count, bits


def swap_dp(value, bit):
    count, _ = dp_bits()
    return lax.ppermute(value, "dp", [(i, i ^ bit) for i in range(count)])


def after(value, *others):
    return lax.optimization_barrier((value,) + others)[0]


def places_of(order):
    count, bits = dp_bits()
    out = []
    for i in range(count):
        position = 0
        for bit in order:
            position = 2 * position + (i // bit) % 2
        out.append(position)
    return out


def sorted_rows(value, places):
    size = value.shape[0] // len(places)
    source = [places.index(p) for p in range(len(places))]
    return jnp.concatenate([value[i * size : (i + 1) * size] for i in source], 0)


class RowScatter:
    def __init__(self, own, other, order, placed):
        if not placed:
            own, other = [sorted_rows(v, places_of(order)) for v in (own, other)]
        self.pair, self.order = ((own, other), list(order))
        self.split()

    def pick(self, side):
        size = self.pair[0].shape[0] // 2
        a, b = [lax.dynamic_slice_in_dim(v, side * size, size, 0).astype(f32) for v in self.pair]
        return (a + b).astype(bf)

    def split(self):
        mine = (lax.axis_index("dp") // self.order[0]) % 2
        self.send, self.keep = (self.pick(1 - mine), self.pick(mine))

    def step(self, *gates):
        keep = after(self.keep, *gates) if gates else self.keep
        self.pair = (keep, swap_dp(self.send, self.order.pop(0)))
        if self.order:
            self.split()

    def total(self):
        return self.pair[0].astype(f32) + self.pair[1].astype(f32)

    def ready(self):
        return self.send if self.order else self.pair[1]


def near_groups():
    count, bits = dp_bits()
    near = 1 << (len(bits) // 2)
    return [[i * near + j for j in range(near)] for i in range(count // near)]


def places_near():
    _, bits = dp_bits()
    cut = len(bits) // 2
    return places_of(bits[:cut][::-1] + bits[cut:][::-1])


def scatter_near(own, other, placed, gated):
    total = (own.astype(f32) + other.astype(f32)).astype(bf)
    if not placed:
        total = sorted_rows(total, places_near())
    total, gated = lax.optimization_barrier((total, gated))
    groups = near_groups()
    return gated, lax.psum_scatter(total, "dp", scatter_dimension=0, axis_index_groups=groups, tiled=True)


def scatter_far(total):
    groups = [list(g) for g in zip(*near_groups())]
    return lax.psum_scatter(total, "dp", scatter_dimension=0, axis_index_groups=groups, tiled=True)


def local(
    tokens,
    long_lengths,
    short_lengths,
    query_weight,
    query_bias,
    key_weight,
    value_weight,
    value_bias,
    output_weight,
    output_bias,
    first_gain,
    first_shift,
    inner_weight,
    inner_bias,
    outer_weight_here,
    outer_bias,
    second_gain,
    second_shift,
    out_grad,
):
    count, bits = dp_bits()
    order_a, order_b = (bits, bits[1::-1] + bits[2:])
    placed = D % (16 * count) == 0
    places_a, places_b, places_n = [
        p if placed else None for p in (places_of(order_a), places_of(order_b), places_near())
    ]
    width = query_weight.shape[1]
    place = (lax.axis_index("tensor").reshape(1), long_lengths, short_lengths)
    bq, bv, bi, wq, wk, wv, wo, wi, w2 = [
        (v, swap_tensor(v))
        for v in (
            query_bias,
            value_bias,
            inner_bias,
            query_weight,
            key_weight,
            value_weight,
            output_weight,
            inner_weight,
            outer_weight_here,
        )
    ]
    qkv, ctx, inv, e_long, e_short, xhat, dev, low, sums_a = attention_forward(
        place, tokens, wq, wk, wv, bq, bv, wo, output_bias, first_gain, first_shift
    )
    act, slope0, slope1, block_own, back, back_low, outer_other, sums_b = ffn_forward(
        place, low, wi, bi, w2, xhat, out_grad, first_gain, first_shift, outer_bias, second_gain, second_shift, places_n
    )
    outer_other = swap_tensor(outer_other)
    outer_own = outer_weight(back_low, act, places_n)
    block_other = swap_tensor(block_own)
    back_low, outer_near = scatter_near(outer_own, outer_other, placed, back_low)
    back_low = after(back_low, block_other)
    inner_own, inner_other, bias0, bias1, first, first_low, sums_c = ffn_backward(
        back_low, (slope0, slope1), w2, wi, low, back, xhat, dev, first_gain, places_n
    )
    first_low, inner_near = scatter_near(inner_own, swap_tensor(inner_other), placed, first_low)
    packed, own_a, own_b, other_a, other_b, small, small_other = attention_backward(
        place, tokens, first_low, qkv, ctx, inv, e_long, e_short, wo, (sums_a, sums_b, sums_c), (bias0, bias1), places_a, places_b
    )
    own_a, own_b, other_a, other_b, packed, small, small_other, block_own = lax.optimization_barrier(
        (own_a, own_b, other_a, other_b, packed, small, small_other, block_own, outer_near)
    )[:8]
    parts = [
        RowScatter(own_a, swap_tensor(other_a), order_a, placed),
        RowScatter(own_b, swap_tensor(other_b), order_b, placed),
    ]
    small = small + swap_tensor(small_other)
    packed = after(packed, parts[0].send, parts[1].send)
    tokens_own = tokens_backward(first, packed, wq, wk, wv)
    inner_near = after(inner_near, tokens_own)
    ffn_rows = scatter_far(jnp.concatenate([inner_near, outer_near], 1)).astype(f32)
    small_bits = list(bits)

    def small_step(value, *gates):
        if not small_bits:
            return value
        return after(value, *gates) + swap_dp(value, small_bits.pop(0))

    small = small_step(small, parts[0].send, parts[1].send)
    small = small_step(small, tokens_own)
    gates = [tokens_own]
    for i in range(len(bits)):
        for part in parts:
            part.step(small, *gates)
        ready = [part.ready() for part in parts]
        small = small_step(small, *ready)
        gates = []
        if i == 0:
            tokens_own = after(tokens_own, *ready)
            tokens_other = swap_tensor(tokens_own)
            block_out = join_rows(place, after(block_own, *ready), block_other)
            gates = [block_out]
        if i == 1:
            tokens_grad = join_rows(place, after(tokens_own, *ready), tokens_other)
            gates = [tokens_grad]
    query_grad, key_grad, value_grad, output_grad = finish(parts[0].pair, parts[1].pair)
    sums = jnp.sum(small[6:9], axis=1)
    rms = jnp.sqrt(sums / (small[9, 0] * D))
    return (
        block_out,
        tokens_grad,
        query_grad,
        small[12, :width],
        key_grad,
        value_grad,
        small[12, width:],
        output_grad.T,
        small[3],
        small[4],
        small[5],
        ffn_rows[:, : inner_near.shape[1]],
        small[10:12].reshape(-1),
        ffn_rows[:, inner_near.shape[1] :].T,
        small[2],
        small[0],
        small[1],
        rms[0],
        rms[1],
        rms[2],
    )


def solution(mesh):
    return jax.shard_map(
        local,
        mesh=mesh,
        in_specs=(
            P("dp", None),
            P("dp"),
            P("dp"),
            P(None, "tensor"),
            P("tensor"),
            P(None, "tensor"),
            P(None, "tensor"),
            P("tensor"),
            P("tensor", None),
            P(),
            P(),
            P(),
            P(None, "tensor"),
            P("tensor"),
            P("tensor", None),
            P(),
            P(),
            P(),
            P("dp", None),
        ),
        out_specs=(
            P("dp", None),
            P("dp", None),
            P("dp", "tensor"),
            P("tensor"),
            P("dp", "tensor"),
            P("dp", "tensor"),
            P("tensor"),
            P("tensor", "dp"),
            P(),
            P(),
            P(),
            P("dp", "tensor"),
            P("tensor"),
            P("tensor", "dp"),
            P(),
            P(),
            P(),
            P(),
            P(),
            P(),
        ),
        check_vma=False,
    )
```

```python
import jax
import jax.numpy as jnp
from jax import lax
from jax.experimental import pallas as pl
from jax.experimental.pallas import tpu as pltpu
from jax.sharding import PartitionSpec as P

D = 768
LONG = 512
SHORT = 256
eps_norm = 1e-05
bf = jnp.bfloat16
f32 = jnp.float32
shape = jax.ShapeDtypeStruct


def nt(a, b):
    return lax.dot_general(a, b, (((1,), (1,)), ((), ())), preferred_element_type=f32)


def nn(a, b):
    return lax.dot_general(a, b, (((1,), (0,)), ((), ())), preferred_element_type=f32)


def tn(a, b):
    return lax.dot_general(a, b, (((0,), (0,)), ((), ())), preferred_element_type=f32)


def whole(dims):
    return pl.BlockSpec(dims, lambda *_: (0,) * len(dims))


def anywhere():
    return pl.BlockSpec(memory_space=pl.ANY)


def settings(flops, mebibytes):
    return dict(
        compiler_params=pltpu.CompilerParams(vmem_limit_bytes=mebibytes << 20),
        cost_estimate=pl.CostEstimate(flops=int(flops), bytes_accessed=int(1e6), transcendentals=0),
    )


def line(ref):
    return ref[...].reshape(1, ref.shape[0])


def slots(rows):
    longs = rows // 2 // LONG
    shorts = rows // 2 // SHORT
    out = [(i * LONG, LONG, i) for i in range(longs)]
    return out + [(rows // 2 + i * SHORT, SHORT, longs + i) for i in range(shorts)]


def slot_length(side_ref, long_ref, short_ref, rows, index):
    longs = rows // 2 // LONG
    shorts = rows // 2 // SHORT
    if index < longs:
        return long_ref[side_ref[0] * longs + index]
    return short_ref[side_ref[0] * shorts + index - longs]


def place_rows(ref, value, places):
    if places is None:
        ref[...] = value
        return
    size = value.shape[0] // len(places)
    for i, p in enumerate(places):
        ref[p * size : (p + 1) * size, :] = value[i * size : (i + 1) * size, :]


def pair_forward(length, q, k, v, put):
    size = q.shape[0]
    lane = lax.broadcasted_iota(jnp.int32, (size, 128), 1)
    low = lane < 64
    pos = lax.broadcasted_iota(jnp.int32, (size, 128), 0)
    bias = jnp.where(pos < length, 0.0, -1e30).astype(bf)
    one = jnp.ones((), bf)
    zero = jnp.zeros((), bf)
    es = []
    for h in range(2):
        mine = low if h == 0 else ~low
        flag = lane == (64 if h == 0 else 0)
        qh = jnp.where(mine, q, jnp.where(flag, one, zero))
        kh = jnp.where(mine, k, jnp.where(flag, bias, zero))
        s = nt(qh, kh)
        m = jnp.max(s, axis=-1, keepdims=True)
        e = jnp.exp(s - m).astype(bf)
        put(h, e)
        es.append(e)
    here = jnp.where(low, one, zero)
    there = jnp.where(low, zero, one)
    both = [jnp.concatenate([v * here, here], 1), jnp.concatenate([v * there, there], 1)]
    out = nn(jnp.concatenate(es, 1), jnp.concatenate(both, 0))
    inv = 1.0 / out[:, 128:]
    return out[:, :128] * inv, inv


def attention_forward_kernel(
    side_ref, long_ref, short_ref,
    x0, x1, wq0, wq1, wk0, wk1, wv0, wv1, bq0, bq1, bv0, bv1, wo0, wo1, bo_ref, gain_ref, shift_ref,
    qkv_ref, ctx_ref, inv_ref, el_ref, es_ref, xhat_ref, dev_ref, low_ref, sums_ref, acc_ref,
):
    step = pl.program_id(0)
    half = x0.shape[0]
    rows = 2 * half
    zero = jnp.zeros((1, 256), f32)
    cols = pl.ds(pl.multiple_of(128 * step, 128), 128)
    weights = jnp.concatenate([w[...] for w in (wq0, wq1, wk0, wk1, wv0, wv1)], 1)
    bias = [b[cols].reshape(1, 128) for b in (bq0, bq1, bv0, bv1)]
    bias = jnp.concatenate(bias[:2] + [zero] + bias[2:], 1)
    for i, x in enumerate((x0, x1)):
        qkv_ref[i * half : (i + 1) * half, :] = (nn(x[...], weights) + bias).astype(bf)
    scale = jnp.asarray(0.125, bf)
    for first, size, index in slots(rows):
        at = pl.ds(first, size)
        length = slot_length(side_ref, long_ref, short_ref, rows, index)
        for p in range(2):
            q = qkv_ref[at, 128 * p : 128 * p + 128] * scale
            k = qkv_ref[at, 256 + 128 * p : 384 + 128 * p]
            v = qkv_ref[at, 512 + 128 * p : 640 + 128 * p]

            def put(h, e, p=p, size=size, index=index):
                if size == LONG:
                    el_ref[0, 4 * index + 2 * p + h] = e
                else:
                    es_ref[0, 4 * (index - half // LONG) + 2 * p + h] = e

            ctx, inv = pair_forward(length, q, k, v, put)
            ctx_ref[at, 128 * p : 128 * p + 128] = ctx.astype(bf)
            inv_ref[at, 128 * p : 128 * p + 128] = inv
    part = nn(ctx_ref[...], jnp.concatenate([wo0[...], wo1[...]], 0))

    @pl.when(step == 0)
    def _():
        acc_ref[...] = part

    @pl.when(step > 0)
    def _():
        acc_ref[...] += part

    @pl.when(step == pl.num_programs(0) - 1)
    def _():
        resid = jnp.zeros((1, D), f32)
        attn = jnp.zeros((1, D), f32)
        count = jnp.zeros((), jnp.int32)
        for first, size, index in slots(rows):
            at = pl.ds(first, size)
            length = slot_length(side_ref, long_ref, short_ref, rows, index)
            count += length
            usable = lax.broadcasted_iota(jnp.int32, (size, D), 0) < length
            branch = acc_ref[at, :] + line(bo_ref)
            source = x0[at, :] if first < half else x1[first - half : first - half + size, :]
            total = source.astype(f32) + branch
            resid += jnp.sum(jnp.where(usable, total * total, 0.0), axis=0, keepdims=True)
            attn += jnp.sum(jnp.where(usable, branch * branch, 0.0), axis=0, keepdims=True)
            centred = total - jnp.mean(total, axis=-1, keepdims=True)
            dev = lax.rsqrt(jnp.mean(centred * centred, axis=-1, keepdims=True) + eps_norm)
            xhat = centred * dev
            xhat_ref[at, :] = xhat
            dev_ref[at, :] = jnp.broadcast_to(dev, (size, 128))
            low_ref[at, :] = (xhat * line(gain_ref) + line(shift_ref)).astype(bf)
        count = jnp.full((1, D), count, jnp.int32).astype(f32)
        sums_ref[...] = jnp.concatenate([resid, attn, count, jnp.zeros((5, D), f32)], 0)


def attention_forward(place, tokens, wq, wk, wv, bq, bv, wo, bo, gain, shift):
    half = tokens.shape[0] // 4
    rows = 2 * half
    width = wq[0].shape[1]
    steps = width // 128
    longs = half // LONG
    shorts = half // SHORT
    wide = pl.BlockSpec((D, 128), lambda i, *_: (0, i))
    tall = pl.BlockSpec((128, D), lambda i, *_: (i, 0))

    def part(columns):
        return pl.BlockSpec((rows, columns), lambda i, *_: (0, i))

    return pl.pallas_call(
        attention_forward_kernel,
        out_shape=(
            shape((rows, steps * 768), bf),
            shape((rows, steps * 256), bf),
            shape((rows, steps * 256), f32),
            shape((steps, 4 * longs, LONG, LONG), bf),
            shape((steps, 4 * shorts, SHORT, SHORT), bf),
            shape((rows, D), f32),
            shape((rows, 128), f32),
            shape((rows, D), bf),
            shape((8, D), f32),
        ),
        grid_spec=pltpu.PrefetchScalarGridSpec(
            num_scalar_prefetch=3,
            grid=(steps,),
            in_specs=[
                pl.BlockSpec((half, D), lambda i, side, *_: (side[0], 0)),
                pl.BlockSpec((half, D), lambda i, side, *_: (2 + side[0], 0)),
            ]
            + [wide] * 6
            + [whole((width,))] * 4
            + [tall] * 2
            + [whole((D,))] * 3,
            out_specs=[
                part(768),
                part(256),
                part(256),
                pl.BlockSpec((1, 4 * longs, LONG, LONG), lambda i, *_: (i, 0, 0, 0)),
                pl.BlockSpec((1, 4 * shorts, SHORT, SHORT), lambda i, *_: (i, 0, 0, 0)),
                whole((rows, D)),
                whole((rows, 128)),
                whole((rows, D)),
                whole((8, D)),
            ],
            scratch_shapes=[pltpu.VMEM((rows, D), f32)],
        ),
        name="attention_forward",
        **settings(40e9, 32),
    )(*place, tokens, tokens, *wq, *wk, *wv, *bq, *bv, *wo, bo, gain, shift)


def gelu_parts(v):
    cdf = 0.5 * (1.0 + lax.erf(v * 0.7071067811865476))
    return cdf, v * (0.3989422804014327 * jnp.exp(-0.5 * (v * v)))


def ffn_forward_kernel(
    side_ref, long_ref, short_ref,
    low_ref, wi0, wi1, bi0, bi1, wo0, wo1, xhat_hbm, grad_hbm, gain1_ref, shift1_ref, bo_ref, gain_ref, shift_ref,
    act0, slope0, slope1, out_hbm, back_hbm, low_hbm, other_ref, sums_ref,
    acc_ref, act1, xhat_ref, grad_ref, out_ref, back_low, in_sem, out_sem, *, chunk, places,
):
    step = pl.program_id(0)
    rows = low_ref.shape[0]
    half = rows // 2
    width = wi0.shape[1]
    fetches = [pltpu.make_async_copy(xhat_hbm, xhat_ref, in_sem.at[0])]
    for i in range(2):
        source = grad_hbm.at[pl.ds(pl.multiple_of((2 * i + side_ref[0]) * half, half), half), :]
        fetches.append(pltpu.make_async_copy(source, grad_ref.at[i * half : (i + 1) * half, :], in_sem.at[1 + i]))

    @pl.when(step == 0)
    def _():
        for fetch in fetches:
            fetch.start()

    cols = pl.ds(pl.multiple_of(width * step, width), width)
    win = jnp.concatenate([wi0[...], wi1[...]], 1)
    bias = jnp.concatenate([b[cols].reshape(1, width) for b in (bi0, bi1)], 1)
    wout = jnp.concatenate([wo0[...], wo1[...]], 0)
    for first in range(0, rows, chunk):
        at = pl.ds(first, chunk)
        inner = nn(low_ref[at, :], win) + bias
        cdf, bell = gelu_parts(inner)
        active = (inner * cdf).astype(bf)
        slope = (cdf + bell).astype(bf)
        act0[at, :] = active[:, :width]
        act1[at, cols] = active[:, width:]
        slope0[at, :] = slope[:, :width]
        slope1[at, :] = slope[:, width:]
        part = nn(active, wout)

        @pl.when(step == 0)
        def _():
            acc_ref[at, :] = part

        @pl.when(step > 0)
        def _():
            acc_ref[at, :] += part

    @pl.when(step == pl.num_programs(0) - 1)
    def _():
        for fetch in fetches:
            fetch.wait()
        ffn_sum = jnp.zeros((1, D), f32)
        gain_sum = jnp.zeros((1, D), f32)
        shift_sum = jnp.zeros((1, D), f32)
        bias_sum = jnp.zeros((1, D), f32)
        stores = []
        for i, (first, size, index) in enumerate(slots(rows)):
            at = pl.ds(first, size)
            length = slot_length(side_ref, long_ref, short_ref, rows, index)
            usable = lax.broadcasted_iota(jnp.int32, (size, D), 0) < length
            ffn = acc_ref[at, :] + line(bo_ref)
            ffn_sum += jnp.sum(jnp.where(usable, ffn * ffn, 0.0), axis=0, keepdims=True)
            total = xhat_ref[at, :] * line(gain1_ref) + line(shift1_ref) + ffn
            centred = total - jnp.mean(total, axis=-1, keepdims=True)
            dev = lax.rsqrt(jnp.mean(centred * centred, axis=-1, keepdims=True) + eps_norm)
            xhat = centred * dev
            out_ref[at, :] = (xhat * line(gain_ref) + line(shift_ref)).astype(bf)
            cot = jnp.where(usable, grad_ref[at, :].astype(f32), 0.0)
            gain_sum += jnp.sum(cot * xhat, axis=0, keepdims=True)
            shift_sum += jnp.sum(cot, axis=0, keepdims=True)
            u = cot * line(gain_ref)
            slant = jnp.mean(u * xhat, axis=-1, keepdims=True)
            back = dev * (u - jnp.mean(u, axis=-1, keepdims=True) - xhat * slant)
            bias_sum += jnp.sum(back, axis=0, keepdims=True)
            acc_ref[at, :] = back
            back_low[at, :] = back.astype(bf)
            for j, (source, target) in enumerate(((out_ref, out_hbm), (acc_ref, back_hbm), (back_low, low_hbm))):
                store = pltpu.make_async_copy(source.at[at, :], target.at[at, :], out_sem.at[3 * i + j])
                store.start()
                stores.append(store)
        sums_ref[...] = jnp.concatenate([ffn_sum, gain_sum, shift_sum, bias_sum, jnp.zeros((4, D), f32)], 0)
        place_rows(other_ref, tn(back_low[...], act1[...]).astype(bf), places)
        for store in stores:
            store.wait()


def ffn_forward(place, low, wi, bi, wo, xhat, grad, gain1, shift1, bo, gain, shift, places, width=512, chunk=512):
    rows = low.shape[0]
    half = wi[0].shape[1]
    cols = pl.BlockSpec((D, width), lambda i, *_: (0, i))
    tall = pl.BlockSpec((width, D), lambda i, *_: (i, 0))
    act = pl.BlockSpec((rows, width), lambda i, *_: (0, i))
    row = whole((D,))
    count = len(slots(rows))
    return pl.pallas_call(
        lambda *refs: ffn_forward_kernel(*refs, chunk=chunk, places=places),
        out_shape=(shape((rows, half), bf),) * 3
        + (shape((rows, D), bf), shape((rows, D), f32), shape((rows, D), bf), shape((D, half), bf), shape((8, D), f32)),
        grid_spec=pltpu.PrefetchScalarGridSpec(
            num_scalar_prefetch=3,
            grid=(half // width,),
            in_specs=[whole((rows, D)), cols, cols, whole((half,)), whole((half,)), tall, tall, anywhere(), anywhere()] + [row] * 5,
            out_specs=[act] * 3 + [anywhere()] * 3 + [whole((D, half)), whole((8, D))],
            scratch_shapes=[
                pltpu.VMEM((rows, D), f32),
                pltpu.VMEM((rows, half), bf),
                pltpu.VMEM((rows, D), f32),
                pltpu.VMEM((rows, D), bf),
                pltpu.VMEM((rows, D), bf),
                pltpu.VMEM((rows, D), bf),
                pltpu.SemaphoreType.DMA((3,)),
                pltpu.SemaphoreType.DMA((3 * count,)),
            ],
        ),
        name="ffn_forward",
        **settings(40e9, 40),
    )(*place, low, *wi, *bi, *wo, xhat, grad, gain1, shift1, bo, gain, shift)


def outer_weight_kernel(low_ref, act_ref, out_ref, *, places):
    place_rows(out_ref, tn(low_ref[...], act_ref[...]).astype(bf), places)


def outer_weight(low, act, places, width=512):
    rows, half = act.shape
    return pl.pallas_call(
        lambda *refs: outer_weight_kernel(*refs, places=places),
        out_shape=shape((D, half), bf),
        grid=(half // width,),
        in_specs=[whole((rows, D)), pl.BlockSpec((rows, width), lambda i: (0, i))],
        out_specs=pl.BlockSpec((D, width), lambda i: (0, i)),
        name="outer_weight",
        **settings(10e9, 8),
    )(low, act)


def ffn_backward_kernel(
    back_low, slope0, slope1, wo0, wo1, wi0, wi1, low_ref, back_hbm, xhat_hbm, dev_ref, gain_ref,
    own_ref, other_ref, bias0, bias1, first_hbm, low_hbm, sums_ref,
    inner_ref, acc_ref, xhat_ref, first_low, in_sem, out_sem, *, chunk, places,
):
    step = pl.program_id(0)
    rows = low_ref.shape[0]
    half = wi0.shape[1]
    fetches = [
        pltpu.make_async_copy(back_hbm, acc_ref, in_sem.at[0]),
        pltpu.make_async_copy(xhat_hbm, xhat_ref, in_sem.at[1]),
    ]

    @pl.when(step == 0)
    def _():
        for fetch in fetches:
            fetch.start()

    wout = jnp.concatenate([wo0[...], wo1[...]], 0)
    win = jnp.concatenate([wi0[...], wi1[...]], 1)
    total = jnp.zeros((1, 2 * half), f32)
    for first in range(0, rows, chunk):
        at = pl.ds(first, chunk)
        slope = jnp.concatenate([slope0[at, :], slope1[at, :]], 1).astype(f32)
        inner = (nt(back_low[at, :], wout) * slope).astype(bf)
        total += jnp.sum(inner.astype(f32), axis=0, keepdims=True)
        inner_ref[at, :] = inner
    bias0[...] = jnp.broadcast_to(total[:, :half], bias0.shape)
    bias1[...] = jnp.broadcast_to(total[:, half:], bias1.shape)
    place_rows(own_ref, tn(low_ref[...], inner_ref[:, :half]).astype(bf), places)
    place_rows(other_ref, tn(low_ref[...], inner_ref[:, half:]).astype(bf), places)

    @pl.when(step == 0)
    def _():
        for fetch in fetches:
            fetch.wait()

    for first in range(0, rows, chunk):
        at = pl.ds(first, chunk)
        acc_ref[at, :] += nt(inner_ref[at, :], win)

    @pl.when(step == pl.num_programs(0) - 1)
    def _():
        gain_sum = jnp.zeros((1, D), f32)
        shift_sum = jnp.zeros((1, D), f32)
        bias_sum = jnp.zeros((1, D), f32)
        stores = []
        for i, first in enumerate(range(0, rows, chunk)):
            at = pl.ds(first, chunk)
            grad = acc_ref[at, :]
            xhat = xhat_ref[at, :]
            gain_sum += jnp.sum(grad * xhat, axis=0, keepdims=True)
            shift_sum += jnp.sum(grad, axis=0, keepdims=True)
            u = grad * line(gain_ref)
            slant = jnp.mean(u * xhat, axis=-1, keepdims=True)
            out = dev_ref[at, 0:1] * (u - jnp.mean(u, axis=-1, keepdims=True) - xhat * slant)
            bias_sum += jnp.sum(out, axis=0, keepdims=True)
            acc_ref[at, :] = out
            first_low[at, :] = out.astype(bf)
            for j, (source, target) in enumerate(((acc_ref, first_hbm), (first_low, low_hbm))):
                store = pltpu.make_async_copy(source.at[at, :], target.at[at, :], out_sem.at[2 * i + j])
                store.start()
                stores.append(store)
        sums_ref[...] = jnp.concatenate([bias_sum, gain_sum, shift_sum, jnp.zeros((5, D), f32)], 0)
        for store in stores:
            store.wait()


def ffn_backward(back_low, slope, wo, wi, low, back, xhat, dev, gain, places, width=512, chunk=512):
    rows = low.shape[0]
    half = wi[0].shape[1]
    cols = pl.BlockSpec((D, width), lambda i: (0, i))
    tall = pl.BlockSpec((width, D), lambda i: (i, 0))
    act = pl.BlockSpec((rows, width), lambda i: (0, i))
    bias = pl.BlockSpec((8, width), lambda i: (0, i))
    full = whole((rows, D))
    return pl.pallas_call(
        lambda *refs: ffn_backward_kernel(*refs, chunk=chunk, places=places),
        out_shape=(shape((D, half), bf),) * 2
        + (shape((8, half), f32),) * 2
        + (shape((rows, D), f32), shape((rows, D), bf), shape((8, D), f32)),
        grid=(half // width,),
        in_specs=[full, act, act, tall, tall, cols, cols, full, anywhere(), anywhere(), whole((rows, 128)), whole((D,))],
        out_specs=[cols] * 2 + [bias] * 2 + [anywhere()] * 2 + [whole((8, D))],
        scratch_shapes=[
            pltpu.VMEM((rows, 2 * width), bf),
            pltpu.VMEM((rows, D), f32),
            pltpu.VMEM((rows, D), f32),
            pltpu.VMEM((rows, D), bf),
            pltpu.SemaphoreType.DMA((2,)),
            pltpu.SemaphoreType.DMA((2 * (rows // chunk),)),
        ],
        name="ffn_backward",
        **settings(40e9, 36),
    )(back_low, *slope, *wo, *wi, low, back, xhat, dev, gain)


def pair_backward(q, k, v, ctx, inv, grad, es):
    size = q.shape[0]
    lane = lax.broadcasted_iota(jnp.int32, (size, 128), 1)
    low = lane < 64
    one = jnp.ones((), bf)
    zero = jnp.zeros((), bf)
    grad = grad * inv
    prod = grad * ctx.astype(f32)
    grad = grad.astype(bf)
    dss = []
    for h in range(2):
        mine = low if h == 0 else ~low
        base = 64 if h == 0 else 0
        delta = -jnp.sum(jnp.where(mine, prod, 0.0), axis=-1, keepdims=True)
        high = delta.astype(bf)
        rest = (delta - high.astype(f32)).astype(bf)
        gh = jnp.where(mine, grad, jnp.where(lane == base, high, jnp.where(lane == base + 1, rest, zero)))
        dp = nt(gh, jnp.where(mine, v, one))
        dss.append((es[h].astype(f32) * dp).astype(bf))
    dq = jnp.where(low, nn(dss[0], k), nn(dss[1], k))
    q_t = q.T
    g_t = grad.T
    dk = jnp.concatenate([nn(q_t[:64], dss[0]), nn(q_t[64:], dss[1])], 0).T
    dv = jnp.concatenate([nn(g_t[:64], es[0]), nn(g_t[64:], es[1])], 0).T
    return dq.astype(bf), dk.astype(bf), dv.astype(bf)


def attention_backward_kernel(
    side_ref, x0, x1, low_ref, qkv_ref, ctx_ref, inv_ref, el_ref, es_ref, wo0, wo1, sums_a, sums_b, sums_c, bias0, bias1,
    out_ref, own_a, own_b, other_a, other_b, small0, small1, grad_ref, *, places_a, places_b,
):
    step = pl.program_id(0)
    half = x0.shape[0]
    rows = 2 * half
    scale = jnp.asarray(0.125, bf)
    low = low_ref[...]
    grad_ref[...] = nt(low, jnp.concatenate([wo0[...], wo1[...]], 0)).astype(bf)
    for first, size, index in slots(rows):
        at = pl.ds(first, size)
        for p in range(2):
            cols = [slice(256 * i + 128 * p, 256 * i + 128 * p + 128) for i in range(3)]
            q = qkv_ref[at, cols[0]] * scale
            k = qkv_ref[at, cols[1]] * scale
            v = qkv_ref[at, cols[2]]
            if size == LONG:
                es = [el_ref[0, 4 * index + 2 * p + h] for h in range(2)]
            else:
                es = [es_ref[0, 4 * (index - half // LONG) + 2 * p + h] for h in range(2)]
            grads = pair_backward(q, k, v, ctx_ref[at, cols[0]], inv_ref[at, cols[0]], grad_ref[at, cols[0]].astype(f32), es)
            for i in range(3):
                out_ref[at, cols[i]] = grads[i]
    packed = out_ref[...]
    wide = (tn(x0[...], packed[:half]) + tn(x1[...], packed[half:])).astype(bf)
    tail = tn(low, ctx_ref[...]).astype(bf)
    for side, (ref_a, ref_b) in enumerate(((own_a, own_b), (other_a, other_b))):
        pieces = [wide[:, 256 * i + 128 * side : 256 * i + 128 * side + 128] for i in range(3)]
        pieces.append(tail[:, 128 * side : 128 * side + 128])
        place_rows(ref_a, jnp.concatenate(pieces[:2], 1), places_a)
        place_rows(ref_b, jnp.concatenate(pieces[2:], 1), places_b)

    @pl.when(step == 0)
    def _():
        for ref, bias in ((small0, bias0), (small1, bias1)):
            ref[0:3, :] = sums_b[1:4, :]
            ref[3:6, :] = sums_c[0:3, :]
            ref[6:8, :] = sums_a[0:2, :]
            ref[8:9, :] = sums_b[0:1, :]
            ref[9:10, :] = sums_a[2:3, :]
            for i in range(bias.shape[1] // D):
                ref[10 + i : 11 + i, :] = bias[0:1, D * i : D * i + D]
            ref[12:16, :] = jnp.zeros((4, D), f32)

    sums = jnp.sum(packed.astype(f32), axis=0, keepdims=True)
    for side, ref in enumerate((small0, small1)):
        for i in range(2):
            start = pl.multiple_of(i * (D // 2) + 128 * step, 128)
            ref[12:13, pl.ds(start, 128)] = sums[:, 512 * i + 128 * side : 512 * i + 128 * side + 128]


def attention_backward(place, tokens, low, qkv, ctx, inv, e_long, e_short, wo, sums, bias, places_a, places_b):
    half = tokens.shape[0] // 4
    rows = 2 * half
    steps = ctx.shape[1] // 256
    tall = pl.BlockSpec((128, D), lambda i, *_: (i, 0))

    def part(height, width):
        return pl.BlockSpec((height, width), lambda i, *_: (0, i))

    return pl.pallas_call(
        lambda *refs: attention_backward_kernel(*refs, places_a=places_a, places_b=places_b),
        out_shape=(shape((rows, 768 * steps), bf),) + (shape((D, 256 * steps), bf),) * 4 + (shape((16, D), f32),) * 2,
        grid_spec=pltpu.PrefetchScalarGridSpec(
            num_scalar_prefetch=1,
            grid=(steps,),
            in_specs=[
                pl.BlockSpec((half, D), lambda i, side, *_: (side[0], 0)),
                pl.BlockSpec((half, D), lambda i, side, *_: (2 + side[0], 0)),
                whole((rows, D)),
                part(rows, 768),
                part(rows, 256),
                part(rows, 256),
                pl.BlockSpec((1,) + e_long.shape[1:], lambda i, *_: (i, 0, 0, 0)),
                pl.BlockSpec((1,) + e_short.shape[1:], lambda i, *_: (i, 0, 0, 0)),
                tall,
                tall,
            ]
            + [whole((8, D))] * 3
            + [whole(bias[0].shape)] * 2,
            out_specs=[part(rows, 768)] + [part(D, 256)] * 4 + [whole((16, D))] * 2,
            scratch_shapes=[pltpu.VMEM((rows, 256), bf)],
        ),
        name="attention_backward",
        **settings(1e6, 29),
    )(place[0], tokens, tokens, low, qkv, ctx, inv, e_long, e_short, *wo, *sums, *bias)


def tokens_backward_kernel(first_ref, packed_ref, wq0, wq1, wk0, wk1, wv0, wv1, out_ref):
    total = first_ref[...]
    for i in range(packed_ref.shape[1] // 768):
        weights = jnp.concatenate([w[:, 128 * i : 128 * i + 128] for w in (wq0, wq1, wk0, wk1, wv0, wv1)], 1)
        total += nt(packed_ref[:, 768 * i : 768 * i + 768], weights)
    out_ref[...] = total.astype(bf)


def tokens_backward(first, packed, wq, wk, wv):
    rows = first.shape[0]
    chunk = 512
    return pl.pallas_call(
        tokens_backward_kernel,
        out_shape=shape((rows, D), bf),
        grid=(rows // chunk,),
        in_specs=[pl.BlockSpec((chunk, D), lambda i: (i, 0)), pl.BlockSpec((chunk, packed.shape[1]), lambda i: (i, 0))]
        + [whole(wq[0].shape)] * 6,
        out_specs=pl.BlockSpec((chunk, D), lambda i: (i, 0)),
        name="tokens_backward",
        **settings(1e6, 16),
    )(first, packed, *wq, *wk, *wv)


def join_kernel(side_ref, own_ref, other_ref, out_ref, buffer_ref, in_sems, out_sems):
    half = own_ref.shape[0] // 2
    fetches = []
    stores = []
    for i, ref in enumerate((own_ref, other_ref)):
        for j in range(2):
            n = 2 * i + j
            block = 2 * j + (side_ref[0] if i == 0 else 1 - side_ref[0])
            target = out_ref.at[pl.ds(pl.multiple_of(block * half, half), half), :]
            place = buffer_ref.at[n * half : (n + 1) * half, :]
            fetches.append(pltpu.make_async_copy(ref.at[j * half : (j + 1) * half, :], place, in_sems.at[n]))
            stores.append(pltpu.make_async_copy(place, target, out_sems.at[n]))
    for fetch in fetches:
        fetch.start()
    for fetch, store in zip(fetches, stores):
        fetch.wait()
        store.start()
    for store in stores:
        store.wait()


def join_rows(place, own, other):
    return pl.pallas_call(
        join_kernel,
        out_shape=shape((2 * own.shape[0], D), own.dtype),
        grid_spec=pltpu.PrefetchScalarGridSpec(
            num_scalar_prefetch=1,
            grid=(1,),
            in_specs=[anywhere(), anywhere()],
            out_specs=anywhere(),
            scratch_shapes=[
                pltpu.VMEM((2 * own.shape[0], D), own.dtype),
                pltpu.SemaphoreType.DMA((4,)),
                pltpu.SemaphoreType.DMA((4,)),
            ],
        ),
        name="join_rows",
        **settings(1e6, 8),
    )(place[0], own, other)


def finish_kernel(keep_a, recv_a, keep_b, recv_b, query_ref, key_ref, value_ref, output_ref):
    pairs = []
    for keep, recv in ((keep_a, recv_a), (keep_b, recv_b)):
        total = keep[...].astype(f32) + recv[...].astype(f32)
        for i in range(2):
            blocks = [total[:, 256 * j + 128 * i : 256 * j + 128 * i + 128] for j in range(total.shape[1] // 256)]
            pairs.append(jnp.concatenate(blocks, 1))
    query_ref[...] = pairs[0]
    key_ref[...] = pairs[1]
    value_ref[...] = pairs[2]
    output_ref[...] = pairs[3]


def finish(pair_a, pair_b):
    rows, columns = pair_a[0].shape
    width = columns // 2
    return pl.pallas_call(
        finish_kernel,
        out_shape=(shape((rows, width), f32),) * 4,
        name="finish",
        **settings(1e6, 2),
    )(*pair_a, *pair_b)


def swap_tensor(value):
    return lax.ppermute(value, "tensor", [(0, 1), (1, 0)])


def dp_bits():
    count = lax.axis_size("dp")
    bits = []
    while (1 << len(bits)) < count:
        bits.append(1 << len(bits))
    return count, bits


def swap_dp(value, bit):
    count, _ = dp_bits()
    return lax.ppermute(value, "dp", [(i, i ^ bit) for i in range(count)])


def after(value, *others):
    return lax.optimization_barrier((value,) + others)[0]


def places_of(order):
    count, bits = dp_bits()
    out = []
    for i in range(count):
        position = 0
        for bit in order:
            position = 2 * position + (i // bit) % 2
        out.append(position)
    return out


def sorted_rows(value, places):
    size = value.shape[0] // len(places)
    source = [places.index(p) for p in range(len(places))]
    return jnp.concatenate([value[i * size : (i + 1) * size] for i in source], 0)


class RowScatter:
    def __init__(self, own, other, order, placed):
        if not placed:
            own, other = [sorted_rows(v, places_of(order)) for v in (own, other)]
        self.pair, self.order = ((own, other), list(order))
        self.split()

    def pick(self, side):
        size = self.pair[0].shape[0] // 2
        a, b = [lax.dynamic_slice_in_dim(v, side * size, size, 0).astype(f32) for v in self.pair]
        return (a + b).astype(bf)

    def split(self):
        mine = (lax.axis_index("dp") // self.order[0]) % 2
        self.send, self.keep = (self.pick(1 - mine), self.pick(mine))

    def step(self, *gates):
        keep = after(self.keep, *gates) if gates else self.keep
        self.pair = (keep, swap_dp(self.send, self.order.pop(0)))
        if self.order:
            self.split()

    def total(self):
        return self.pair[0].astype(f32) + self.pair[1].astype(f32)

    def ready(self):
        return self.send if self.order else self.pair[1]


def near_groups():
    count, bits = dp_bits()
    near = 1 << (len(bits) // 2)
    return [[i * near + j for j in range(near)] for i in range(count // near)]


def places_near():
    _, bits = dp_bits()
    cut = len(bits) // 2
    return places_of(bits[:cut][::-1] + bits[cut:][::-1])


def scatter_near(own, other, placed, gated):
    total = (own.astype(f32) + other.astype(f32)).astype(bf)
    if not placed:
        total = sorted_rows(total, places_near())
    total, gated = lax.optimization_barrier((total, gated))
    groups = near_groups()
    return gated, lax.psum_scatter(total, "dp", scatter_dimension=0, axis_index_groups=groups, tiled=True)


def scatter_far(total):
    groups = [list(g) for g in zip(*near_groups())]
    return lax.psum_scatter(total, "dp", scatter_dimension=0, axis_index_groups=groups, tiled=True)


def local(
    tokens,
    long_lengths,
    short_lengths,
    query_weight,
    query_bias,
    key_weight,
    value_weight,
    value_bias,
    output_weight,
    output_bias,
    first_gain,
    first_shift,
    inner_weight,
    inner_bias,
    outer_weight_here,
    outer_bias,
    second_gain,
    second_shift,
    out_grad,
):
    count, bits = dp_bits()
    order_a, order_b = (bits, bits[1::-1] + bits[2:])
    placed = D % (16 * count) == 0
    places_a, places_b, places_n = [
        p if placed else None for p in (places_of(order_a), places_of(order_b), places_near())
    ]
    width = query_weight.shape[1]
    place = (lax.axis_index("tensor").reshape(1), long_lengths, short_lengths)
    bq, bv, bi, wq, wk, wv, wo, wi, w2 = [
        (v, swap_tensor(v))
        for v in (
            query_bias,
            value_bias,
            inner_bias,
            query_weight,
            key_weight,
            value_weight,
            output_weight,
            inner_weight,
            outer_weight_here,
        )
    ]
    qkv, ctx, inv, e_long, e_short, xhat, dev, low, sums_a = attention_forward(
        place, tokens, wq, wk, wv, bq, bv, wo, output_bias, first_gain, first_shift
    )
    act, slope0, slope1, block_own, back, back_low, outer_other, sums_b = ffn_forward(
        place, low, wi, bi, w2, xhat, out_grad, first_gain, first_shift, outer_bias, second_gain, second_shift, places_n
    )
    outer_other = swap_tensor(outer_other)
    outer_own = outer_weight(back_low, act, places_n)
    block_other = swap_tensor(block_own)
    back_low, outer_near = scatter_near(outer_own, outer_other, placed, back_low)
    back_low = after(back_low, block_other)
    inner_own, inner_other, bias0, bias1, first, first_low, sums_c = ffn_backward(
        back_low, (slope0, slope1), w2, wi, low, back, xhat, dev, first_gain, places_n
    )
    first_low, inner_near = scatter_near(inner_own, swap_tensor(inner_other), placed, first_low)
    packed, own_a, own_b, other_a, other_b, small, small_other = attention_backward(
        place, tokens, first_low, qkv, ctx, inv, e_long, e_short, wo, (sums_a, sums_b, sums_c), (bias0, bias1), places_a, places_b
    )
    own_a, own_b, other_a, other_b, packed, small, small_other, block_own = lax.optimization_barrier(
        (own_a, own_b, other_a, other_b, packed, small, small_other, block_own, outer_near)
    )[:8]
    parts = [
        RowScatter(own_a, swap_tensor(other_a), order_a, placed),
        RowScatter(own_b, swap_tensor(other_b), order_b, placed),
    ]
    small = after(small, parts[0].send, parts[1].send) + swap_tensor(small_other)
    packed = after(packed, small)
    tokens_own = tokens_backward(first, packed, wq, wk, wv)
    small = after(small, tokens_own) + swap_dp(small, bits[0])
    gates = [tokens_own]
    for i in range(len(bits)):
        for part in parts:
            part.step(small, *gates)
        ready = [part.ready() for part in parts]
        if i + 1 < len(bits):
            small = after(small, *ready) + swap_dp(small, bits[i + 1])
        gates = []
        if i == 0:
            tokens_own = after(tokens_own, *ready)
            tokens_other = swap_tensor(tokens_own)
            inner_near = after(inner_near, small)
            ffn_rows = scatter_far(jnp.concatenate([inner_near, outer_near], 1)).astype(f32)
            block_out = join_rows(place, after(block_own, small), block_other)
            gates = [block_out]
        if i == 1:
            tokens_grad = join_rows(place, after(tokens_own, small), tokens_other)
            gates = [tokens_grad]
    query_grad, key_grad, value_grad, output_grad = finish(parts[0].pair, parts[1].pair)
    sums = jnp.sum(small[6:9], axis=1)
    rms = jnp.sqrt(sums / (small[9, 0] * D))
    return (
        block_out,
        tokens_grad,
        query_grad,
        small[12, :width],
        key_grad,
        value_grad,
        small[12, width:],
        output_grad.T,
        small[3],
        small[4],
        small[5],
        ffn_rows[:, : inner_near.shape[1]],
        small[10:12].reshape(-1),
        ffn_rows[:, inner_near.shape[1] :].T,
        small[2],
        small[0],
        small[1],
        rms[0],
        rms[1],
        rms[2],
    )


def solution(mesh):
    return jax.shard_map(
        local,
        mesh=mesh,
        in_specs=(
            P("dp", None),
            P("dp"),
            P("dp"),
            P(None, "tensor"),
            P("tensor"),
            P(None, "tensor"),
            P(None, "tensor"),
            P("tensor"),
            P("tensor", None),
            P(),
            P(),
            P(),
            P(None, "tensor"),
            P("tensor"),
            P("tensor", None),
            P(),
            P(),
            P(),
            P("dp", None),
        ),
        out_specs=(
            P("dp", None),
            P("dp", None),
            P("dp", "tensor"),
            P("tensor"),
            P("dp", "tensor"),
            P("dp", "tensor"),
            P("tensor"),
            P("tensor", "dp"),
            P(),
            P(),
            P(),
            P("dp", "tensor"),
            P("tensor"),
            P("tensor", "dp"),
            P(),
            P(),
            P(),
            P(),
            P(),
            P(),
        ),
        check_vma=False,
    )
```

```python
import jax
import jax.numpy as jnp
from jax import lax
from jax.experimental import pallas as pl
from jax.experimental.pallas import tpu as pltpu
from jax.sharding import PartitionSpec as P

D = 768
LONG = 512
SHORT = 256
eps_norm = 1e-05
bf = jnp.bfloat16
f32 = jnp.float32
shape = jax.ShapeDtypeStruct


def nt(a, b):
    return lax.dot_general(a, b, (((1,), (1,)), ((), ())), preferred_element_type=f32)


def nn(a, b):
    return lax.dot_general(a, b, (((1,), (0,)), ((), ())), preferred_element_type=f32)


def tn(a, b):
    return lax.dot_general(a, b, (((0,), (0,)), ((), ())), preferred_element_type=f32)


def whole(dims):
    return pl.BlockSpec(dims, lambda *_: (0,) * len(dims))


def anywhere():
    return pl.BlockSpec(memory_space=pl.ANY)


def settings(flops, mebibytes):
    return dict(
        compiler_params=pltpu.CompilerParams(vmem_limit_bytes=mebibytes << 20),
        cost_estimate=pl.CostEstimate(flops=int(flops), bytes_accessed=int(1e6), transcendentals=0),
    )


def line(ref):
    return ref[...].reshape(1, ref.shape[0])


def slots(rows):
    longs = rows // 2 // LONG
    shorts = rows // 2 // SHORT
    out = [(i * LONG, LONG, i) for i in range(longs)]
    return out + [(rows // 2 + i * SHORT, SHORT, longs + i) for i in range(shorts)]


def slot_length(side_ref, long_ref, short_ref, rows, index):
    longs = rows // 2 // LONG
    shorts = rows // 2 // SHORT
    if index < longs:
        return long_ref[side_ref[0] * longs + index]
    return short_ref[side_ref[0] * shorts + index - longs]


def place_rows(ref, value, places):
    if places is None:
        ref[...] = value
        return
    size = value.shape[0] // len(places)
    for i, p in enumerate(places):
        ref[p * size : (p + 1) * size, :] = value[i * size : (i + 1) * size, :]


def pair_forward(length, q, k, v, put):
    size = q.shape[0]
    lane = lax.broadcasted_iota(jnp.int32, (size, 128), 1)
    low = lane < 64
    pos = lax.broadcasted_iota(jnp.int32, (size, 128), 0)
    bias = jnp.where(pos < length, 0.0, -1e30).astype(bf)
    one = jnp.ones((), bf)
    zero = jnp.zeros((), bf)
    es = []
    for h in range(2):
        mine = low if h == 0 else ~low
        flag = lane == (64 if h == 0 else 0)
        qh = jnp.where(mine, q, jnp.where(flag, one, zero))
        kh = jnp.where(mine, k, jnp.where(flag, bias, zero))
        s = nt(qh, kh)
        m = jnp.max(s, axis=-1, keepdims=True)
        e = jnp.exp(s - m).astype(bf)
        put(h, e)
        es.append(e)
    here = jnp.where(low, one, zero)
    there = jnp.where(low, zero, one)
    both = [jnp.concatenate([v * here, here], 1), jnp.concatenate([v * there, there], 1)]
    out = nn(jnp.concatenate(es, 1), jnp.concatenate(both, 0))
    inv = 1.0 / out[:, 128:]
    return out[:, :128] * inv, inv


def attention_forward_kernel(
    side_ref, long_ref, short_ref,
    x0, x1, wq0, wq1, wk0, wk1, wv0, wv1, bq0, bq1, bv0, bv1, wo0, wo1, bo_ref, gain_ref, shift_ref,
    qkv_ref, ctx_ref, inv_ref, el_ref, es_ref, xhat_ref, dev_ref, low_ref, sums_ref, acc_ref,
):
    step = pl.program_id(0)
    half = x0.shape[0]
    rows = 2 * half
    zero = jnp.zeros((1, 256), f32)
    cols = pl.ds(pl.multiple_of(128 * step, 128), 128)
    weights = jnp.concatenate([w[...] for w in (wq0, wq1, wk0, wk1, wv0, wv1)], 1)
    bias = [b[cols].reshape(1, 128) for b in (bq0, bq1, bv0, bv1)]
    bias = jnp.concatenate(bias[:2] + [zero] + bias[2:], 1)
    for i, x in enumerate((x0, x1)):
        qkv_ref[i * half : (i + 1) * half, :] = (nn(x[...], weights) + bias).astype(bf)
    scale = jnp.asarray(0.125, bf)
    for first, size, index in slots(rows):
        at = pl.ds(first, size)
        length = slot_length(side_ref, long_ref, short_ref, rows, index)
        for p in range(2):
            q = qkv_ref[at, 128 * p : 128 * p + 128] * scale
            k = qkv_ref[at, 256 + 128 * p : 384 + 128 * p]
            v = qkv_ref[at, 512 + 128 * p : 640 + 128 * p]

            def put(h, e, p=p, size=size, index=index):
                if size == LONG:
                    el_ref[0, 4 * index + 2 * p + h] = e
                else:
                    es_ref[0, 4 * (index - half // LONG) + 2 * p + h] = e

            ctx, inv = pair_forward(length, q, k, v, put)
            ctx_ref[at, 128 * p : 128 * p + 128] = ctx.astype(bf)
            inv_ref[at, 128 * p : 128 * p + 128] = inv
    part = nn(ctx_ref[...], jnp.concatenate([wo0[...], wo1[...]], 0))

    @pl.when(step == 0)
    def _():
        acc_ref[...] = part

    @pl.when(step > 0)
    def _():
        acc_ref[...] += part

    @pl.when(step == pl.num_programs(0) - 1)
    def _():
        resid = jnp.zeros((1, D), f32)
        attn = jnp.zeros((1, D), f32)
        count = jnp.zeros((), jnp.int32)
        for first, size, index in slots(rows):
            at = pl.ds(first, size)
            length = slot_length(side_ref, long_ref, short_ref, rows, index)
            count += length
            usable = lax.broadcasted_iota(jnp.int32, (size, D), 0) < length
            branch = acc_ref[at, :] + line(bo_ref)
            source = x0[at, :] if first < half else x1[first - half : first - half + size, :]
            total = source.astype(f32) + branch
            resid += jnp.sum(jnp.where(usable, total * total, 0.0), axis=0, keepdims=True)
            attn += jnp.sum(jnp.where(usable, branch * branch, 0.0), axis=0, keepdims=True)
            centred = total - jnp.mean(total, axis=-1, keepdims=True)
            dev = lax.rsqrt(jnp.mean(centred * centred, axis=-1, keepdims=True) + eps_norm)
            xhat = centred * dev
            xhat_ref[at, :] = xhat
            dev_ref[at, :] = jnp.broadcast_to(dev, (size, 128))
            low_ref[at, :] = (xhat * line(gain_ref) + line(shift_ref)).astype(bf)
        count = jnp.full((1, D), count, jnp.int32).astype(f32)
        sums_ref[...] = jnp.concatenate([resid, attn, count, jnp.zeros((5, D), f32)], 0)


def attention_forward(place, tokens, wq, wk, wv, bq, bv, wo, bo, gain, shift):
    half = tokens.shape[0] // 4
    rows = 2 * half
    width = wq[0].shape[1]
    steps = width // 128
    longs = half // LONG
    shorts = half // SHORT
    wide = pl.BlockSpec((D, 128), lambda i, *_: (0, i))
    tall = pl.BlockSpec((128, D), lambda i, *_: (i, 0))

    def part(columns):
        return pl.BlockSpec((rows, columns), lambda i, *_: (0, i))

    return pl.pallas_call(
        attention_forward_kernel,
        out_shape=(
            shape((rows, steps * 768), bf),
            shape((rows, steps * 256), bf),
            shape((rows, steps * 256), f32),
            shape((steps, 4 * longs, LONG, LONG), bf),
            shape((steps, 4 * shorts, SHORT, SHORT), bf),
            shape((rows, D), f32),
            shape((rows, 128), f32),
            shape((rows, D), bf),
            shape((8, D), f32),
        ),
        grid_spec=pltpu.PrefetchScalarGridSpec(
            num_scalar_prefetch=3,
            grid=(steps,),
            in_specs=[
                pl.BlockSpec((half, D), lambda i, side, *_: (side[0], 0)),
                pl.BlockSpec((half, D), lambda i, side, *_: (2 + side[0], 0)),
            ]
            + [wide] * 6
            + [whole((width,))] * 4
            + [tall] * 2
            + [whole((D,))] * 3,
            out_specs=[
                part(768),
                part(256),
                part(256),
                pl.BlockSpec((1, 4 * longs, LONG, LONG), lambda i, *_: (i, 0, 0, 0)),
                pl.BlockSpec((1, 4 * shorts, SHORT, SHORT), lambda i, *_: (i, 0, 0, 0)),
                whole((rows, D)),
                whole((rows, 128)),
                whole((rows, D)),
                whole((8, D)),
            ],
            scratch_shapes=[pltpu.VMEM((rows, D), f32)],
        ),
        name="attention_forward",
        **settings(40e9, 58),
    )(*place, tokens, tokens, *wq, *wk, *wv, *bq, *bv, *wo, bo, gain, shift)


def gelu_parts(v):
    cdf = 0.5 * (1.0 + lax.erf(v * 0.7071067811865476))
    return cdf, v * (0.3989422804014327 * jnp.exp(-0.5 * (v * v)))


def ffn_forward_kernel(
    side_ref, long_ref, short_ref,
    low_ref, wi0, wi1, bi0, bi1, wo0, wo1, xhat_hbm, grad_hbm, gain1_ref, shift1_ref, bo_ref, gain_ref, shift_ref,
    act0, slope0, slope1, out_hbm, back_hbm, low_hbm, other_ref, sums_ref,
    acc_ref, act1, xhat_ref, grad_ref, out_ref, back_low, in_sem, out_sem, *, chunk, places,
):
    step = pl.program_id(0)
    rows = low_ref.shape[0]
    half = rows // 2
    width = wi0.shape[1]
    fetches = [pltpu.make_async_copy(xhat_hbm, xhat_ref, in_sem.at[0])]
    for i in range(2):
        source = grad_hbm.at[pl.ds(pl.multiple_of((2 * i + side_ref[0]) * half, half), half), :]
        fetches.append(pltpu.make_async_copy(source, grad_ref.at[i * half : (i + 1) * half, :], in_sem.at[1 + i]))

    @pl.when(step == 0)
    def _():
        for fetch in fetches:
            fetch.start()

    cols = pl.ds(pl.multiple_of(width * step, width), width)
    win = jnp.concatenate([wi0[...], wi1[...]], 1)
    bias = jnp.concatenate([b[cols].reshape(1, width) for b in (bi0, bi1)], 1)
    wout = jnp.concatenate([wo0[...], wo1[...]], 0)
    for first in range(0, rows, chunk):
        at = pl.ds(first, chunk)
        inner = nn(low_ref[at, :], win) + bias
        cdf, bell = gelu_parts(inner)
        active = (inner * cdf).astype(bf)
        slope = (cdf + bell).astype(bf)
        act0[at, :] = active[:, :width]
        act1[at, cols] = active[:, width:]
        slope0[at, :] = slope[:, :width]
        slope1[at, :] = slope[:, width:]
        part = nn(active, wout)

        @pl.when(step == 0)
        def _():
            acc_ref[at, :] = part

        @pl.when(step > 0)
        def _():
            acc_ref[at, :] += part

    @pl.when(step == pl.num_programs(0) - 1)
    def _():
        for fetch in fetches:
            fetch.wait()
        ffn_sum = jnp.zeros((1, D), f32)
        gain_sum = jnp.zeros((1, D), f32)
        shift_sum = jnp.zeros((1, D), f32)
        bias_sum = jnp.zeros((1, D), f32)
        stores = []
        for i, (first, size, index) in enumerate(slots(rows)):
            at = pl.ds(first, size)
            length = slot_length(side_ref, long_ref, short_ref, rows, index)
            usable = lax.broadcasted_iota(jnp.int32, (size, D), 0) < length
            ffn = acc_ref[at, :] + line(bo_ref)
            ffn_sum += jnp.sum(jnp.where(usable, ffn * ffn, 0.0), axis=0, keepdims=True)
            total = xhat_ref[at, :] * line(gain1_ref) + line(shift1_ref) + ffn
            centred = total - jnp.mean(total, axis=-1, keepdims=True)
            dev = lax.rsqrt(jnp.mean(centred * centred, axis=-1, keepdims=True) + eps_norm)
            xhat = centred * dev
            out_ref[at, :] = (xhat * line(gain_ref) + line(shift_ref)).astype(bf)
            cot = jnp.where(usable, grad_ref[at, :].astype(f32), 0.0)
            gain_sum += jnp.sum(cot * xhat, axis=0, keepdims=True)
            shift_sum += jnp.sum(cot, axis=0, keepdims=True)
            u = cot * line(gain_ref)
            slant = jnp.mean(u * xhat, axis=-1, keepdims=True)
            back = dev * (u - jnp.mean(u, axis=-1, keepdims=True) - xhat * slant)
            bias_sum += jnp.sum(back, axis=0, keepdims=True)
            acc_ref[at, :] = back
            back_low[at, :] = back.astype(bf)
            for j, (source, target) in enumerate(((out_ref, out_hbm), (acc_ref, back_hbm), (back_low, low_hbm))):
                store = pltpu.make_async_copy(source.at[at, :], target.at[at, :], out_sem.at[3 * i + j])
                store.start()
                stores.append(store)
        sums_ref[...] = jnp.concatenate([ffn_sum, gain_sum, shift_sum, bias_sum, jnp.zeros((4, D), f32)], 0)
        place_rows(other_ref, tn(back_low[...], act1[...]).astype(bf), places)
        for store in stores:
            store.wait()


def ffn_forward(place, low, wi, bi, wo, xhat, grad, gain1, shift1, bo, gain, shift, places, width=512, chunk=512):
    rows = low.shape[0]
    half = wi[0].shape[1]
    cols = pl.BlockSpec((D, width), lambda i, *_: (0, i))
    tall = pl.BlockSpec((width, D), lambda i, *_: (i, 0))
    act = pl.BlockSpec((rows, width), lambda i, *_: (0, i))
    row = whole((D,))
    count = len(slots(rows))
    return pl.pallas_call(
        lambda *refs: ffn_forward_kernel(*refs, chunk=chunk, places=places),
        out_shape=(shape((rows, half), bf),) * 3
        + (shape((rows, D), bf), shape((rows, D), f32), shape((rows, D), bf), shape((D, half), bf), shape((8, D), f32)),
        grid_spec=pltpu.PrefetchScalarGridSpec(
            num_scalar_prefetch=3,
            grid=(half // width,),
            in_specs=[whole((rows, D)), cols, cols, whole((half,)), whole((half,)), tall, tall, anywhere(), anywhere()] + [row] * 5,
            out_specs=[act] * 3 + [anywhere()] * 3 + [whole((D, half)), whole((8, D))],
            scratch_shapes=[
                pltpu.VMEM((rows, D), f32),
                pltpu.VMEM((rows, half), bf),
                pltpu.VMEM((rows, D), f32),
                pltpu.VMEM((rows, D), bf),
                pltpu.VMEM((rows, D), bf),
                pltpu.VMEM((rows, D), bf),
                pltpu.SemaphoreType.DMA((3,)),
                pltpu.SemaphoreType.DMA((3 * count,)),
            ],
        ),
        name="ffn_forward",
        **settings(40e9, 58),
    )(*place, low, *wi, *bi, *wo, xhat, grad, gain1, shift1, bo, gain, shift)


def outer_weight_kernel(low_ref, act_ref, out_ref, *, places):
    place_rows(out_ref, tn(low_ref[...], act_ref[...]).astype(bf), places)


def outer_weight(low, act, places, width=512):
    rows, half = act.shape
    return pl.pallas_call(
        lambda *refs: outer_weight_kernel(*refs, places=places),
        out_shape=shape((D, half), bf),
        grid=(half // width,),
        in_specs=[whole((rows, D)), pl.BlockSpec((rows, width), lambda i: (0, i))],
        out_specs=pl.BlockSpec((D, width), lambda i: (0, i)),
        name="outer_weight",
        **settings(10e9, 8),
    )(low, act)


def ffn_backward_kernel(
    back_low, slope0, slope1, wo0, wo1, wi0, wi1, low_ref, back_hbm, xhat_hbm, dev_ref, gain_ref,
    own_ref, other_ref, bias0, bias1, first_hbm, low_hbm, sums_ref,
    inner_ref, acc_ref, xhat_ref, first_low, in_sem, out_sem, *, chunk, places,
):
    step = pl.program_id(0)
    rows = low_ref.shape[0]
    half = wi0.shape[1]
    fetches = [
        pltpu.make_async_copy(back_hbm, acc_ref, in_sem.at[0]),
        pltpu.make_async_copy(xhat_hbm, xhat_ref, in_sem.at[1]),
    ]

    @pl.when(step == 0)
    def _():
        for fetch in fetches:
            fetch.start()

    wout = jnp.concatenate([wo0[...], wo1[...]], 0)
    win = jnp.concatenate([wi0[...], wi1[...]], 1)
    total = jnp.zeros((1, 2 * half), f32)
    for first in range(0, rows, chunk):
        at = pl.ds(first, chunk)
        slope = jnp.concatenate([slope0[at, :], slope1[at, :]], 1).astype(f32)
        inner = (nt(back_low[at, :], wout) * slope).astype(bf)
        total += jnp.sum(inner.astype(f32), axis=0, keepdims=True)
        inner_ref[at, :] = inner
    bias0[...] = jnp.broadcast_to(total[:, :half], bias0.shape)
    bias1[...] = jnp.broadcast_to(total[:, half:], bias1.shape)
    place_rows(own_ref, tn(low_ref[...], inner_ref[:, :half]).astype(bf), places)
    place_rows(other_ref, tn(low_ref[...], inner_ref[:, half:]).astype(bf), places)

    @pl.when(step == 0)
    def _():
        for fetch in fetches:
            fetch.wait()

    for first in range(0, rows, chunk):
        at = pl.ds(first, chunk)
        acc_ref[at, :] += nt(inner_ref[at, :], win)

    @pl.when(step == pl.num_programs(0) - 1)
    def _():
        gain_sum = jnp.zeros((1, D), f32)
        shift_sum = jnp.zeros((1, D), f32)
        bias_sum = jnp.zeros((1, D), f32)
        stores = []
        for i, first in enumerate(range(0, rows, chunk)):
            at = pl.ds(first, chunk)
            grad = acc_ref[at, :]
            xhat = xhat_ref[at, :]
            gain_sum += jnp.sum(grad * xhat, axis=0, keepdims=True)
            shift_sum += jnp.sum(grad, axis=0, keepdims=True)
            u = grad * line(gain_ref)
            slant = jnp.mean(u * xhat, axis=-1, keepdims=True)
            out = dev_ref[at, 0:1] * (u - jnp.mean(u, axis=-1, keepdims=True) - xhat * slant)
            bias_sum += jnp.sum(out, axis=0, keepdims=True)
            acc_ref[at, :] = out
            first_low[at, :] = out.astype(bf)
            for j, (source, target) in enumerate(((acc_ref, first_hbm), (first_low, low_hbm))):
                store = pltpu.make_async_copy(source.at[at, :], target.at[at, :], out_sem.at[2 * i + j])
                store.start()
                stores.append(store)
        sums_ref[...] = jnp.concatenate([bias_sum, gain_sum, shift_sum, jnp.zeros((5, D), f32)], 0)
        for store in stores:
            store.wait()


def ffn_backward(back_low, slope, wo, wi, low, back, xhat, dev, gain, places, width=512, chunk=512):
    rows = low.shape[0]
    half = wi[0].shape[1]
    cols = pl.BlockSpec((D, width), lambda i: (0, i))
    tall = pl.BlockSpec((width, D), lambda i: (i, 0))
    act = pl.BlockSpec((rows, width), lambda i: (0, i))
    bias = pl.BlockSpec((8, width), lambda i: (0, i))
    full = whole((rows, D))
    return pl.pallas_call(
        lambda *refs: ffn_backward_kernel(*refs, chunk=chunk, places=places),
        out_shape=(shape((D, half), bf),) * 2
        + (shape((8, half), f32),) * 2
        + (shape((rows, D), f32), shape((rows, D), bf), shape((8, D), f32)),
        grid=(half // width,),
        in_specs=[full, act, act, tall, tall, cols, cols, full, anywhere(), anywhere(), whole((rows, 128)), whole((D,))],
        out_specs=[cols] * 2 + [bias] * 2 + [anywhere()] * 2 + [whole((8, D))],
        scratch_shapes=[
            pltpu.VMEM((rows, 2 * width), bf),
            pltpu.VMEM((rows, D), f32),
            pltpu.VMEM((rows, D), f32),
            pltpu.VMEM((rows, D), bf),
            pltpu.SemaphoreType.DMA((2,)),
            pltpu.SemaphoreType.DMA((2 * (rows // chunk),)),
        ],
        name="ffn_backward",
        **settings(40e9, 58),
    )(back_low, *slope, *wo, *wi, low, back, xhat, dev, gain)


def pair_backward(q, k, v, ctx, inv, grad, es):
    size = q.shape[0]
    lane = lax.broadcasted_iota(jnp.int32, (size, 128), 1)
    low = lane < 64
    one = jnp.ones((), bf)
    zero = jnp.zeros((), bf)
    grad = grad * inv
    prod = grad * ctx.astype(f32)
    grad = grad.astype(bf)
    dss = []
    for h in range(2):
        mine = low if h == 0 else ~low
        base = 64 if h == 0 else 0
        delta = -jnp.sum(jnp.where(mine, prod, 0.0), axis=-1, keepdims=True)
        high = delta.astype(bf)
        rest = (delta - high.astype(f32)).astype(bf)
        gh = jnp.where(mine, grad, jnp.where(lane == base, high, jnp.where(lane == base + 1, rest, zero)))
        dp = nt(gh, jnp.where(mine, v, one))
        dss.append((es[h].astype(f32) * dp).astype(bf))
    dq = jnp.where(low, nn(dss[0], k), nn(dss[1], k))
    q_t = q.T
    g_t = grad.T
    dk = jnp.concatenate([nn(q_t[:64], dss[0]), nn(q_t[64:], dss[1])], 0).T
    dv = jnp.concatenate([nn(g_t[:64], es[0]), nn(g_t[64:], es[1])], 0).T
    return dq.astype(bf), dk.astype(bf), dv.astype(bf)


def attention_backward_kernel(
    side_ref, x0, x1, low_ref, qkv_ref, ctx_ref, inv_ref, el_ref, es_ref, wo0, wo1, sums_a, sums_b, sums_c, bias0, bias1,
    out_ref, own_a, own_b, other_a, other_b, small0, small1, grad_ref, *, places_a, places_b,
):
    step = pl.program_id(0)
    half = x0.shape[0]
    rows = 2 * half
    scale = jnp.asarray(0.125, bf)
    low = low_ref[...]
    grad_ref[...] = nt(low, jnp.concatenate([wo0[...], wo1[...]], 0)).astype(bf)
    for first, size, index in slots(rows):
        at = pl.ds(first, size)
        for p in range(2):
            cols = [slice(256 * i + 128 * p, 256 * i + 128 * p + 128) for i in range(3)]
            q = qkv_ref[at, cols[0]] * scale
            k = qkv_ref[at, cols[1]] * scale
            v = qkv_ref[at, cols[2]]
            if size == LONG:
                es = [el_ref[0, 4 * index + 2 * p + h] for h in range(2)]
            else:
                es = [es_ref[0, 4 * (index - half // LONG) + 2 * p + h] for h in range(2)]
            grads = pair_backward(q, k, v, ctx_ref[at, cols[0]], inv_ref[at, cols[0]], grad_ref[at, cols[0]].astype(f32), es)
            for i in range(3):
                out_ref[at, cols[i]] = grads[i]
    packed = out_ref[...]
    wide = (tn(x0[...], packed[:half]) + tn(x1[...], packed[half:])).astype(bf)
    tail = tn(low, ctx_ref[...]).astype(bf)
    for side, (ref_a, ref_b) in enumerate(((own_a, own_b), (other_a, other_b))):
        pieces = [wide[:, 256 * i + 128 * side : 256 * i + 128 * side + 128] for i in range(3)]
        pieces.append(tail[:, 128 * side : 128 * side + 128])
        place_rows(ref_a, jnp.concatenate(pieces[:2], 1), places_a)
        place_rows(ref_b, jnp.concatenate(pieces[2:], 1), places_b)

    @pl.when(step == 0)
    def _():
        for ref, bias in ((small0, bias0), (small1, bias1)):
            ref[0:3, :] = sums_b[1:4, :]
            ref[3:6, :] = sums_c[0:3, :]
            ref[6:8, :] = sums_a[0:2, :]
            ref[8:9, :] = sums_b[0:1, :]
            ref[9:10, :] = sums_a[2:3, :]
            for i in range(bias.shape[1] // D):
                ref[10 + i : 11 + i, :] = bias[0:1, D * i : D * i + D]
            ref[12:16, :] = jnp.zeros((4, D), f32)

    sums = jnp.sum(packed.astype(f32), axis=0, keepdims=True)
    for side, ref in enumerate((small0, small1)):
        for i in range(2):
            start = pl.multiple_of(i * (D // 2) + 128 * step, 128)
            ref[12:13, pl.ds(start, 128)] = sums[:, 512 * i + 128 * side : 512 * i + 128 * side + 128]


def attention_backward(place, tokens, low, qkv, ctx, inv, e_long, e_short, wo, sums, bias, places_a, places_b):
    half = tokens.shape[0] // 4
    rows = 2 * half
    steps = ctx.shape[1] // 256
    tall = pl.BlockSpec((128, D), lambda i, *_: (i, 0))

    def part(height, width):
        return pl.BlockSpec((height, width), lambda i, *_: (0, i))

    return pl.pallas_call(
        lambda *refs: attention_backward_kernel(*refs, places_a=places_a, places_b=places_b),
        out_shape=(shape((rows, 768 * steps), bf),) + (shape((D, 256 * steps), bf),) * 4 + (shape((16, D), f32),) * 2,
        grid_spec=pltpu.PrefetchScalarGridSpec(
            num_scalar_prefetch=1,
            grid=(steps,),
            in_specs=[
                pl.BlockSpec((half, D), lambda i, side, *_: (side[0], 0)),
                pl.BlockSpec((half, D), lambda i, side, *_: (2 + side[0], 0)),
                whole((rows, D)),
                part(rows, 768),
                part(rows, 256),
                part(rows, 256),
                pl.BlockSpec((1,) + e_long.shape[1:], lambda i, *_: (i, 0, 0, 0)),
                pl.BlockSpec((1,) + e_short.shape[1:], lambda i, *_: (i, 0, 0, 0)),
                tall,
                tall,
            ]
            + [whole((8, D))] * 3
            + [whole(bias[0].shape)] * 2,
            out_specs=[part(rows, 768)] + [part(D, 256)] * 4 + [whole((16, D))] * 2,
            scratch_shapes=[pltpu.VMEM((rows, 256), bf)],
        ),
        name="attention_backward",
        **settings(1e6, 58),
    )(place[0], tokens, tokens, low, qkv, ctx, inv, e_long, e_short, *wo, *sums, *bias)


def tokens_backward_kernel(first_ref, packed_ref, wq0, wq1, wk0, wk1, wv0, wv1, out_ref):
    total = first_ref[...]
    for i in range(packed_ref.shape[1] // 768):
        weights = jnp.concatenate([w[:, 128 * i : 128 * i + 128] for w in (wq0, wq1, wk0, wk1, wv0, wv1)], 1)
        total += nt(packed_ref[:, 768 * i : 768 * i + 768], weights)
    out_ref[...] = total.astype(bf)


def tokens_backward(first, packed, wq, wk, wv):
    rows = first.shape[0]
    chunk = 512
    return pl.pallas_call(
        tokens_backward_kernel,
        out_shape=shape((rows, D), bf),
        grid=(rows // chunk,),
        in_specs=[pl.BlockSpec((chunk, D), lambda i: (i, 0)), pl.BlockSpec((chunk, packed.shape[1]), lambda i: (i, 0))]
        + [whole(wq[0].shape)] * 6,
        out_specs=pl.BlockSpec((chunk, D), lambda i: (i, 0)),
        name="tokens_backward",
        **settings(1e6, 16),
    )(first, packed, *wq, *wk, *wv)


def join_kernel(side_ref, own_ref, other_ref, out_ref, buffer_ref, in_sems, out_sems):
    half = own_ref.shape[0] // 2
    fetches = []
    stores = []
    for i, ref in enumerate((own_ref, other_ref)):
        for j in range(2):
            n = 2 * i + j
            block = 2 * j + (side_ref[0] if i == 0 else 1 - side_ref[0])
            target = out_ref.at[pl.ds(pl.multiple_of(block * half, half), half), :]
            place = buffer_ref.at[n * half : (n + 1) * half, :]
            fetches.append(pltpu.make_async_copy(ref.at[j * half : (j + 1) * half, :], place, in_sems.at[n]))
            stores.append(pltpu.make_async_copy(place, target, out_sems.at[n]))
    for fetch in fetches:
        fetch.start()
    for fetch, store in zip(fetches, stores):
        fetch.wait()
        store.start()
    for store in stores:
        store.wait()


def join_rows(place, own, other):
    return pl.pallas_call(
        join_kernel,
        out_shape=shape((2 * own.shape[0], D), own.dtype),
        grid_spec=pltpu.PrefetchScalarGridSpec(
            num_scalar_prefetch=1,
            grid=(1,),
            in_specs=[anywhere(), anywhere()],
            out_specs=anywhere(),
            scratch_shapes=[
                pltpu.VMEM((2 * own.shape[0], D), own.dtype),
                pltpu.SemaphoreType.DMA((4,)),
                pltpu.SemaphoreType.DMA((4,)),
            ],
        ),
        name="join_rows",
        **settings(1e6, 4),
    )(place[0], own, other)


def split_terms(value):
    high = value.astype(bf)
    return high, (value - high.astype(f32)).astype(bf)


def exchange_kernel(mine_ref, *refs, chains, count, merge, step):
    ins, outs = (refs[:count], refs[count:])
    small_ref, news = (outs[-1], outs[:-1])
    small_in, small_from, small_at = chains[0][5:]
    if small_at is None:
        small = ins[small_in][...] + ins[small_from][...]
    else:
        got = ins[small_from][small_at : small_at + 32, :].astype(f32)
        small = ins[small_in][...] + (got[:16] + got[16:])
    small_ref[...] = small
    base = 0
    for i, (keep, k0, recv, r0, rows, *_) in enumerate(chains):
        half = rows // 2
        send_ref, keep_ref = (news[0], news[1]) if merge else (news[2 * i], news[2 * i + 1])
        for ref, side in ((send_ref, 1 - mine_ref[2 * step + i]), (keep_ref, mine_ref[2 * step + i])):
            at = side * half
            mine = ins[keep][pl.ds(pl.multiple_of(k0 + at, 16), half), :].astype(f32)
            sent = ins[recv][pl.ds(pl.multiple_of(r0 + at, 16), half), :].astype(f32)
            ref[base : base + half, :] = (mine + sent).astype(bf)
        base = base + half if merge else 0
        if i == len(chains) - 1 or (not merge and i == 0):
            if i == 0 or merge:
                end = base if merge else half
                high, rest = split_terms(small)
                send_ref[end : end + 16, :] = high
                send_ref[end + 16 : end + 32, :] = rest


def exchange(mine, arrays, chains, merge, step):
    columns = arrays[0].shape[1]
    halves = [chain[4] // 2 for chain in chains]
    if merge:
        outs = [shape((sum(halves) + 32, columns), bf), shape((sum(halves), columns), bf)]
    else:
        outs = []
        for i, half in enumerate(halves):
            outs += [shape((half + (32 if i == 0 else 0), columns), bf), shape((half, columns), bf)]
    outs.append(shape((16, D), f32))
    return pl.pallas_call(
        lambda *refs: exchange_kernel(*refs, chains=chains, count=len(arrays), merge=merge, step=step),
        out_shape=tuple(outs),
        grid_spec=pltpu.PrefetchScalarGridSpec(
            num_scalar_prefetch=1,
            grid=(1,),
            in_specs=[whole(v.shape) for v in arrays],
            out_specs=[whole(v.shape) for v in outs],
        ),
        name="exchange",
        **settings(1e6, 8),
    )(mine, *arrays)


def finish_kernel(keep_ref, recv_ref, small_in, query_ref, key_ref, value_ref, output_ref, small_ref):
    rows = keep_ref.shape[0]
    total = keep_ref[...].astype(f32) + recv_ref[0:rows, :].astype(f32)
    outs = (query_ref, key_ref, value_ref, output_ref)
    for n, ref in enumerate(outs):
        part = total[(n // 2) * (rows // 2) : (n // 2 + 1) * (rows // 2)]
        for j in range(total.shape[1] // 256):
            ref[:, 128 * j : 128 * j + 128] = part[:, 256 * j + 128 * (n % 2) : 256 * j + 128 * (n % 2) + 128]
    got = recv_ref[rows : rows + 32, :].astype(f32)
    small_ref[...] = small_in[...] + (got[:16] + got[16:])


def finish(keep, recv, small):
    rows, columns = keep.shape
    outs = (shape((rows // 2, columns // 2), f32),) * 4 + (shape((16, D), f32),)
    return pl.pallas_call(
        finish_kernel,
        out_shape=outs,
        grid=(1,),
        in_specs=[whole(v.shape) for v in (keep, recv, small)],
        out_specs=[whole(v.shape) for v in outs],
        name="finish",
        **settings(1e6, 2),
    )(keep, recv, small)


def swap_tensor(value):
    return lax.ppermute(value, "tensor", [(0, 1), (1, 0)])


def dp_bits():
    count = lax.axis_size("dp")
    bits = []
    while (1 << len(bits)) < count:
        bits.append(1 << len(bits))
    return count, bits


def swap_dp(value, bit):
    count, _ = dp_bits()
    return lax.ppermute(value, "dp", [(i, i ^ bit) for i in range(count)])


def after(value, *others):
    return lax.optimization_barrier((value,) + others)[0]


def places_of(order):
    count, bits = dp_bits()
    out = []
    for i in range(count):
        position = 0
        for bit in order:
            position = 2 * position + (i // bit) % 2
        out.append(position)
    return out


def sorted_rows(value, places):
    size = value.shape[0] // len(places)
    source = [places.index(p) for p in range(len(places))]
    return jnp.concatenate([value[i * size : (i + 1) * size] for i in source], 0)


class RowScatter:
    def __init__(self, own, other, order, placed):
        if not placed:
            own, other = [sorted_rows(v, places_of(order)) for v in (own, other)]
        self.pair, self.order = ((own, other), list(order))
        self.split()

    def pick(self, side):
        size = self.pair[0].shape[0] // 2
        a, b = [lax.dynamic_slice_in_dim(v, side * size, size, 0).astype(f32) for v in self.pair]
        return (a + b).astype(bf)

    def split(self):
        mine = (lax.axis_index("dp") // self.order[0]) % 2
        self.send, self.keep = (self.pick(1 - mine), self.pick(mine))

    def step(self, *gates):
        keep = after(self.keep, *gates) if gates else self.keep
        self.pair = (keep, swap_dp(self.send, self.order.pop(0)))
        if self.order:
            self.split()

    def total(self):
        return self.pair[0].astype(f32) + self.pair[1].astype(f32)

    def ready(self):
        return self.send if self.order else self.pair[1]


def local(
    tokens,
    long_lengths,
    short_lengths,
    query_weight,
    query_bias,
    key_weight,
    value_weight,
    value_bias,
    output_weight,
    output_bias,
    first_gain,
    first_shift,
    inner_weight,
    inner_bias,
    outer_weight_here,
    outer_bias,
    second_gain,
    second_shift,
    out_grad,
):
    count, bits = dp_bits()
    order_a, order_b = (bits, bits[1::-1] + bits[2:])
    placed = D % (16 * count) == 0
    places_a, places_b = [places_of(order) if placed else None for order in (order_a, order_b)]
    width = query_weight.shape[1]
    place = (lax.axis_index("tensor").reshape(1), long_lengths, short_lengths)
    mine = (lax.axis_index("dp") // jnp.array([v for pair in zip(order_a, order_b) for v in pair], jnp.int32)) % 2
    bq, bv, bi, wq, wk, wv, wo, wi, w2 = [
        (v, swap_tensor(v))
        for v in (
            query_bias,
            value_bias,
            inner_bias,
            query_weight,
            key_weight,
            value_weight,
            output_weight,
            inner_weight,
            outer_weight_here,
        )
    ]
    qkv, ctx, inv, e_long, e_short, xhat, dev, low, sums_a = attention_forward(
        place, tokens, wq, wk, wv, bq, bv, wo, output_bias, first_gain, first_shift
    )
    act, slope0, slope1, block_own, back, back_low, outer_other, sums_b = ffn_forward(
        place, low, wi, bi, w2, xhat, out_grad, first_gain, first_shift, outer_bias, second_gain, second_shift, places_a
    )
    outer_other = swap_tensor(outer_other)
    outer = RowScatter(outer_weight(back_low, act, places_a), outer_other, order_a, placed)
    block_other = swap_tensor(block_own)
    back_low = after(back_low, outer.send, block_other)
    order_i = bits[:1] + bits[2:3] + bits[1:2] + bits[3:]
    inner_own, inner_other, bias0, bias1, first, first_low, sums_c = ffn_backward(
        back_low, (slope0, slope1), w2, wi, low, back, xhat, dev, first_gain, places_of(order_i) if placed else None
    )
    outer.step(sums_c)
    inner_own, inner_other, first_low, first = lax.optimization_barrier(
        (inner_own, inner_other, first_low, first, outer.send)
    )[:4]
    inner = RowScatter(inner_own, swap_tensor(inner_other), order_i, placed)
    first_low = after(first_low, inner.send)
    packed, own_a, own_b, other_a, other_b, small, small_other = attention_backward(
        place, tokens, first_low, qkv, ctx, inv, e_long, e_short, wo, (sums_a, sums_b, sums_c), (bias0, bias1), places_a, places_b
    )
    outer.step(small)
    inner.step(small)
    other_a, other_b, small_other = [swap_tensor(after(v, outer.send)) for v in (other_a, other_b, small_other)]
    own_a, own_b, packed, small, block_own = lax.optimization_barrier(
        (own_a, own_b, packed, small, block_own, outer.send, inner.send)
    )[:5]
    def advance(step, *gates):
        for chain in (outer, inner):
            if chain.order:
                chain.step(*gates)

    if placed:
        chains = [(0, 0, 1, 0, D, 4, 5, None), (2, 0, 3, 0, D)]
        send_a, keep_a, send_b, keep_b, small = exchange(mine, (own_a, other_a, own_b, other_b, small, small_other), chains, False, 0)
        packed = after(packed, send_a)
        tokens_own = tokens_backward(first, packed, wq, wk, wv)
        recv_a, recv_b = (swap_dp(send_a, order_a[0]), swap_dp(send_b, order_b[0]))
        outer.step(tokens_own)
        keep_a = after(keep_a, tokens_own, outer.ready())
        rows = D // 2
        chains = [(0, 0, 1, 0, rows, 4, 1, rows), (2, 0, 3, 0, rows)]
        send_a, keep_a, send_b, keep_b, small = exchange(mine, (keep_a, recv_a, keep_b, recv_b, small), chains, False, 1)
        tokens_own, block_own = lax.optimization_barrier((tokens_own, block_own, send_a))[:2]
        tokens_other = swap_tensor(tokens_own)
        block_out = join_rows(place, block_own, block_other)
        recv_a, recv_b = (swap_dp(send_a, order_a[1]), swap_dp(send_b, order_b[1]))
        inner.step(send_a)
        keep_a = after(keep_a, block_out)
        rows = D // 4
        chains = [(0, 0, 1, 0, rows, 4, 1, rows), (2, 0, 3, 0, rows)]
        send, keep, small = exchange(mine, (keep_a, recv_a, keep_b, recv_b, small), chains, True, 2)
        tokens_grad = join_rows(place, after(tokens_own, send), tokens_other)
        for step in range(2, len(bits) - 1):
            recv = swap_dp(send, order_a[step])
            advance(step, send)
            keep = after(keep, tokens_grad) if step == 2 else keep
            rows = keep.shape[0] // 2
            chains = [(0, 0, 1, 0, rows, 2, 1, 2 * rows), (0, rows, 1, rows, rows)]
            send, keep, small = exchange(mine, (keep, recv, small), chains, True, step + 1)
        recv = swap_dp(send, order_a[-1])
        while outer.order or inner.order:
            advance(0, send)
        query_grad, key_grad, value_grad, output_grad, small = finish(keep, recv, small)
    else:
        parts = [RowScatter(own_a, other_a, order_a, placed), RowScatter(own_b, other_b, order_b, placed)]
        small = small + small_other
        tokens_own = tokens_backward(first, packed, wq, wk, wv)
        tokens_grad = join_rows(place, tokens_own, swap_tensor(tokens_own))
        block_out = join_rows(place, block_own, block_other)
        for bit in bits:
            small = small + swap_dp(small, bit)
            for chain in [outer, inner] + parts:
                if chain.order:
                    chain.step()
        part_a, part_b = [part.total().reshape(D // count, -1, 2, 128) for part in parts]
        query_grad, key_grad, value_grad, output_grad = [
            v[:, :, i].reshape(-1, width) for v in (part_a, part_b) for i in range(2)
        ]
    sums = jnp.sum(small[6:9], axis=1)
    rms = jnp.sqrt(sums / (small[9, 0] * D))
    return (
        block_out,
        tokens_grad,
        query_grad,
        small[12, :width],
        key_grad,
        value_grad,
        small[12, width:],
        output_grad.T,
        small[3],
        small[4],
        small[5],
        inner.total(),
        small[10:12].reshape(-1),
        outer.total().T,
        small[2],
        small[0],
        small[1],
        rms[0],
        rms[1],
        rms[2],
    )


def solution(mesh):
    return jax.shard_map(
        local,
        mesh=mesh,
        in_specs=(
            P("dp", None),
            P("dp"),
            P("dp"),
            P(None, "tensor"),
            P("tensor"),
            P(None, "tensor"),
            P(None, "tensor"),
            P("tensor"),
            P("tensor", None),
            P(),
            P(),
            P(),
            P(None, "tensor"),
            P("tensor"),
            P("tensor", None),
            P(),
            P(),
            P(),
            P("dp", None),
        ),
        out_specs=(
            P("dp", None),
            P("dp", None),
            P("dp", "tensor"),
            P("tensor"),
            P("dp", "tensor"),
            P("dp", "tensor"),
            P("tensor"),
            P("tensor", "dp"),
            P(),
            P(),
            P(),
            P("dp", "tensor"),
            P("tensor"),
            P("tensor", "dp"),
            P(),
            P(),
            P(),
            P(),
            P(),
            P(),
        ),
        check_vma=False,
    )
```

```python
import jax
import jax.numpy as jnp
from jax import lax
from jax.experimental import pallas as pl
from jax.experimental.pallas import tpu as pltpu
from jax.sharding import PartitionSpec as P

D = 768
LONG = 512
SHORT = 256
eps_norm = 1e-05
bf = jnp.bfloat16
f32 = jnp.float32
shape = jax.ShapeDtypeStruct


def nt(a, b):
    return lax.dot_general(a, b, (((1,), (1,)), ((), ())), preferred_element_type=f32)


def nn(a, b):
    return lax.dot_general(a, b, (((1,), (0,)), ((), ())), preferred_element_type=f32)


def tn(a, b):
    return lax.dot_general(a, b, (((0,), (0,)), ((), ())), preferred_element_type=f32)


def whole(dims):
    return pl.BlockSpec(dims, lambda *_: (0,) * len(dims))


def anywhere():
    return pl.BlockSpec(memory_space=pl.ANY)


def settings(flops, mebibytes):
    return dict(
        compiler_params=pltpu.CompilerParams(vmem_limit_bytes=mebibytes << 20),
        cost_estimate=pl.CostEstimate(flops=int(flops), bytes_accessed=int(1e6), transcendentals=0),
    )


def line(ref):
    return ref[...].reshape(1, ref.shape[0])


def slots(rows):
    longs = rows // 2 // LONG
    shorts = rows // 2 // SHORT
    out = [(i * LONG, LONG, i) for i in range(longs)]
    return out + [(rows // 2 + i * SHORT, SHORT, longs + i) for i in range(shorts)]


def slot_length(side_ref, long_ref, short_ref, rows, index):
    longs = rows // 2 // LONG
    shorts = rows // 2 // SHORT
    if index < longs:
        return long_ref[side_ref[0] * longs + index]
    return short_ref[side_ref[0] * shorts + index - longs]


def place_rows(ref, value, places):
    if places is None:
        ref[...] = value
        return
    size = value.shape[0] // len(places)
    for i, p in enumerate(places):
        ref[p * size : (p + 1) * size, :] = value[i * size : (i + 1) * size, :]


def pair_forward(length, q, k, v, put):
    size = q.shape[0]
    lane = lax.broadcasted_iota(jnp.int32, (size, 128), 1)
    low = lane < 64
    pos = lax.broadcasted_iota(jnp.int32, (size, 128), 0)
    bias = jnp.where(pos < length, 0.0, -1e30).astype(bf)
    one = jnp.ones((), bf)
    zero = jnp.zeros((), bf)
    es = []
    for h in range(2):
        mine = low if h == 0 else ~low
        flag = lane == (64 if h == 0 else 0)
        qh = jnp.where(mine, q, jnp.where(flag, one, zero))
        kh = jnp.where(mine, k, jnp.where(flag, bias, zero))
        s = nt(qh, kh)
        m = jnp.max(s, axis=-1, keepdims=True)
        e = jnp.exp(s - m).astype(bf)
        put(h, e)
        es.append(e)
    here = jnp.where(low, one, zero)
    there = jnp.where(low, zero, one)
    both = [jnp.concatenate([v * here, here], 1), jnp.concatenate([v * there, there], 1)]
    out = nn(jnp.concatenate(es, 1), jnp.concatenate(both, 0))
    inv = 1.0 / out[:, 128:]
    return out[:, :128] * inv, inv


def attention_forward_kernel(
    side_ref, long_ref, short_ref,
    x0, x1, wq0, wq1, wk0, wk1, wv0, wv1, bq0, bq1, bv0, bv1, wo0, wo1, bo_ref, gain_ref, shift_ref,
    qkv_ref, ctx_ref, inv_ref, el_ref, es_ref, xhat_ref, dev_ref, low_ref, sums_ref, acc_ref,
):
    step = pl.program_id(0)
    half = x0.shape[0]
    rows = 2 * half
    zero = jnp.zeros((1, 256), f32)
    cols = pl.ds(pl.multiple_of(128 * step, 128), 128)
    weights = jnp.concatenate([w[...] for w in (wq0, wq1, wk0, wk1, wv0, wv1)], 1)
    bias = [b[cols].reshape(1, 128) for b in (bq0, bq1, bv0, bv1)]
    bias = jnp.concatenate(bias[:2] + [zero] + bias[2:], 1)
    for i, x in enumerate((x0, x1)):
        qkv_ref[i * half : (i + 1) * half, :] = (nn(x[...], weights) + bias).astype(bf)
    scale = jnp.asarray(0.125, bf)
    for first, size, index in slots(rows):
        at = pl.ds(first, size)
        length = slot_length(side_ref, long_ref, short_ref, rows, index)
        for p in range(2):
            q = qkv_ref[at, 128 * p : 128 * p + 128] * scale
            k = qkv_ref[at, 256 + 128 * p : 384 + 128 * p]
            v = qkv_ref[at, 512 + 128 * p : 640 + 128 * p]

            def put(h, e, p=p, size=size, index=index):
                if size == LONG:
                    el_ref[0, 4 * index + 2 * p + h] = e
                else:
                    es_ref[0, 4 * (index - half // LONG) + 2 * p + h] = e

            ctx, inv = pair_forward(length, q, k, v, put)
            ctx_ref[at, 128 * p : 128 * p + 128] = ctx.astype(bf)
            inv_ref[at, 128 * p : 128 * p + 128] = inv
    part = nn(ctx_ref[...], jnp.concatenate([wo0[...], wo1[...]], 0))

    @pl.when(step == 0)
    def _():
        acc_ref[...] = part

    @pl.when(step > 0)
    def _():
        acc_ref[...] += part

    @pl.when(step == pl.num_programs(0) - 1)
    def _():
        resid = jnp.zeros((1, D), f32)
        attn = jnp.zeros((1, D), f32)
        count = jnp.zeros((), jnp.int32)
        for first, size, index in slots(rows):
            at = pl.ds(first, size)
            length = slot_length(side_ref, long_ref, short_ref, rows, index)
            count += length
            usable = lax.broadcasted_iota(jnp.int32, (size, D), 0) < length
            branch = acc_ref[at, :] + line(bo_ref)
            source = x0[at, :] if first < half else x1[first - half : first - half + size, :]
            total = source.astype(f32) + branch
            resid += jnp.sum(jnp.where(usable, total * total, 0.0), axis=0, keepdims=True)
            attn += jnp.sum(jnp.where(usable, branch * branch, 0.0), axis=0, keepdims=True)
            centred = total - jnp.mean(total, axis=-1, keepdims=True)
            dev = lax.rsqrt(jnp.mean(centred * centred, axis=-1, keepdims=True) + eps_norm)
            xhat = centred * dev
            xhat_ref[at, :] = xhat
            dev_ref[at, :] = jnp.broadcast_to(dev, (size, 128))
            low_ref[at, :] = (xhat * line(gain_ref) + line(shift_ref)).astype(bf)
        count = jnp.full((1, D), count, jnp.int32).astype(f32)
        sums_ref[...] = jnp.concatenate([resid, attn, count, jnp.zeros((5, D), f32)], 0)


def attention_forward(place, tokens, wq, wk, wv, bq, bv, wo, bo, gain, shift):
    half = tokens.shape[0] // 4
    rows = 2 * half
    width = wq[0].shape[1]
    steps = width // 128
    longs = half // LONG
    shorts = half // SHORT
    wide = pl.BlockSpec((D, 128), lambda i, *_: (0, i))
    tall = pl.BlockSpec((128, D), lambda i, *_: (i, 0))

    def part(columns):
        return pl.BlockSpec((rows, columns), lambda i, *_: (0, i))

    return pl.pallas_call(
        attention_forward_kernel,
        out_shape=(
            shape((rows, steps * 768), bf),
            shape((rows, steps * 256), bf),
            shape((rows, steps * 256), f32),
            shape((steps, 4 * longs, LONG, LONG), bf),
            shape((steps, 4 * shorts, SHORT, SHORT), bf),
            shape((rows, D), f32),
            shape((rows, 128), f32),
            shape((rows, D), bf),
            shape((8, D), f32),
        ),
        grid_spec=pltpu.PrefetchScalarGridSpec(
            num_scalar_prefetch=3,
            grid=(steps,),
            in_specs=[
                pl.BlockSpec((half, D), lambda i, side, *_: (side[0], 0)),
                pl.BlockSpec((half, D), lambda i, side, *_: (2 + side[0], 0)),
            ]
            + [wide] * 6
            + [whole((width,))] * 4
            + [tall] * 2
            + [whole((D,))] * 3,
            out_specs=[
                part(768),
                part(256),
                part(256),
                pl.BlockSpec((1, 4 * longs, LONG, LONG), lambda i, *_: (i, 0, 0, 0)),
                pl.BlockSpec((1, 4 * shorts, SHORT, SHORT), lambda i, *_: (i, 0, 0, 0)),
                whole((rows, D)),
                whole((rows, 128)),
                whole((rows, D)),
                whole((8, D)),
            ],
            scratch_shapes=[pltpu.VMEM((rows, D), f32)],
        ),
        name="attention_forward",
        **settings(40e9, 58),
    )(*place, tokens, tokens, *wq, *wk, *wv, *bq, *bv, *wo, bo, gain, shift)


def gelu_parts(v):
    cdf = 0.5 * (1.0 + lax.erf(v * 0.7071067811865476))
    return cdf, v * (0.3989422804014327 * jnp.exp(-0.5 * (v * v)))


def ffn_forward_kernel(
    side_ref, long_ref, short_ref,
    low_ref, wi0, wi1, bi0, bi1, wo0, wo1, xhat_hbm, grad_hbm, gain1_ref, shift1_ref, bo_ref, gain_ref, shift_ref,
    act0, slope0, slope1, out_hbm, back_hbm, low_hbm, other_ref, sums_ref,
    acc_ref, act1, xhat_ref, grad_ref, out_ref, back_low, in_sem, out_sem, *, chunk, places,
):
    step = pl.program_id(0)
    rows = low_ref.shape[0]
    half = rows // 2
    width = wi0.shape[1]
    fetches = [pltpu.make_async_copy(xhat_hbm, xhat_ref, in_sem.at[0])]
    for i in range(2):
        source = grad_hbm.at[pl.ds(pl.multiple_of((2 * i + side_ref[0]) * half, half), half), :]
        fetches.append(pltpu.make_async_copy(source, grad_ref.at[i * half : (i + 1) * half, :], in_sem.at[1 + i]))

    @pl.when(step == 0)
    def _():
        for fetch in fetches:
            fetch.start()

    cols = pl.ds(pl.multiple_of(width * step, width), width)
    win = jnp.concatenate([wi0[...], wi1[...]], 1)
    bias = jnp.concatenate([b[cols].reshape(1, width) for b in (bi0, bi1)], 1)
    wout = jnp.concatenate([wo0[...], wo1[...]], 0)
    for first in range(0, rows, chunk):
        at = pl.ds(first, chunk)
        inner = nn(low_ref[at, :], win) + bias
        cdf, bell = gelu_parts(inner)
        active = (inner * cdf).astype(bf)
        slope = (cdf + bell).astype(bf)
        act0[at, :] = active[:, :width]
        act1[at, cols] = active[:, width:]
        slope0[at, :] = slope[:, :width]
        slope1[at, :] = slope[:, width:]
        part = nn(active, wout)

        @pl.when(step == 0)
        def _():
            acc_ref[at, :] = part

        @pl.when(step > 0)
        def _():
            acc_ref[at, :] += part

    @pl.when(step == pl.num_programs(0) - 1)
    def _():
        for fetch in fetches:
            fetch.wait()
        ffn_sum = jnp.zeros((1, D), f32)
        gain_sum = jnp.zeros((1, D), f32)
        shift_sum = jnp.zeros((1, D), f32)
        bias_sum = jnp.zeros((1, D), f32)
        stores = []
        for i, (first, size, index) in enumerate(slots(rows)):
            at = pl.ds(first, size)
            length = slot_length(side_ref, long_ref, short_ref, rows, index)
            usable = lax.broadcasted_iota(jnp.int32, (size, D), 0) < length
            ffn = acc_ref[at, :] + line(bo_ref)
            ffn_sum += jnp.sum(jnp.where(usable, ffn * ffn, 0.0), axis=0, keepdims=True)
            total = xhat_ref[at, :] * line(gain1_ref) + line(shift1_ref) + ffn
            centred = total - jnp.mean(total, axis=-1, keepdims=True)
            dev = lax.rsqrt(jnp.mean(centred * centred, axis=-1, keepdims=True) + eps_norm)
            xhat = centred * dev
            out_ref[at, :] = (xhat * line(gain_ref) + line(shift_ref)).astype(bf)
            cot = jnp.where(usable, grad_ref[at, :].astype(f32), 0.0)
            gain_sum += jnp.sum(cot * xhat, axis=0, keepdims=True)
            shift_sum += jnp.sum(cot, axis=0, keepdims=True)
            u = cot * line(gain_ref)
            slant = jnp.mean(u * xhat, axis=-1, keepdims=True)
            back = dev * (u - jnp.mean(u, axis=-1, keepdims=True) - xhat * slant)
            bias_sum += jnp.sum(back, axis=0, keepdims=True)
            acc_ref[at, :] = back
            back_low[at, :] = back.astype(bf)
            for j, (source, target) in enumerate(((out_ref, out_hbm), (acc_ref, back_hbm), (back_low, low_hbm))):
                store = pltpu.make_async_copy(source.at[at, :], target.at[at, :], out_sem.at[3 * i + j])
                store.start()
                stores.append(store)
        sums_ref[...] = jnp.concatenate([ffn_sum, gain_sum, shift_sum, bias_sum, jnp.zeros((4, D), f32)], 0)
        place_rows(other_ref, tn(back_low[...], act1[...]).astype(bf), places)
        for store in stores:
            store.wait()


def ffn_forward(place, low, wi, bi, wo, xhat, grad, gain1, shift1, bo, gain, shift, places, width=512, chunk=512):
    rows = low.shape[0]
    half = wi[0].shape[1]
    cols = pl.BlockSpec((D, width), lambda i, *_: (0, i))
    tall = pl.BlockSpec((width, D), lambda i, *_: (i, 0))
    act = pl.BlockSpec((rows, width), lambda i, *_: (0, i))
    row = whole((D,))
    count = len(slots(rows))
    return pl.pallas_call(
        lambda *refs: ffn_forward_kernel(*refs, chunk=chunk, places=places),
        out_shape=(shape((rows, half), bf),) * 3
        + (shape((rows, D), bf), shape((rows, D), f32), shape((rows, D), bf), shape((D, half), bf), shape((8, D), f32)),
        grid_spec=pltpu.PrefetchScalarGridSpec(
            num_scalar_prefetch=3,
            grid=(half // width,),
            in_specs=[whole((rows, D)), cols, cols, whole((half,)), whole((half,)), tall, tall, anywhere(), anywhere()] + [row] * 5,
            out_specs=[act] * 3 + [anywhere()] * 3 + [whole((D, half)), whole((8, D))],
            scratch_shapes=[
                pltpu.VMEM((rows, D), f32),
                pltpu.VMEM((rows, half), bf),
                pltpu.VMEM((rows, D), f32),
                pltpu.VMEM((rows, D), bf),
                pltpu.VMEM((rows, D), bf),
                pltpu.VMEM((rows, D), bf),
                pltpu.SemaphoreType.DMA((3,)),
                pltpu.SemaphoreType.DMA((3 * count,)),
            ],
        ),
        name="ffn_forward",
        **settings(40e9, 58),
    )(*place, low, *wi, *bi, *wo, xhat, grad, gain1, shift1, bo, gain, shift)


def outer_weight_kernel(low_ref, act_ref, out_ref, *, places):
    place_rows(out_ref, tn(low_ref[...], act_ref[...]).astype(bf), places)


def outer_weight(low, act, places, width=512):
    rows, half = act.shape
    return pl.pallas_call(
        lambda *refs: outer_weight_kernel(*refs, places=places),
        out_shape=shape((D, half), bf),
        grid=(half // width,),
        in_specs=[whole((rows, D)), pl.BlockSpec((rows, width), lambda i: (0, i))],
        out_specs=pl.BlockSpec((D, width), lambda i: (0, i)),
        name="outer_weight",
        **settings(10e9, 8),
    )(low, act)


def ffn_backward_kernel(
    back_low, slope0, slope1, wo0, wo1, wi0, wi1, low_ref, back_hbm, xhat_hbm, dev_ref, gain_ref,
    own_ref, other_ref, bias0, bias1, first_hbm, low_hbm, sums_ref,
    inner_ref, acc_ref, xhat_ref, first_low, in_sem, out_sem, *, chunk, places,
):
    step = pl.program_id(0)
    rows = low_ref.shape[0]
    half = wi0.shape[1]
    fetches = [
        pltpu.make_async_copy(back_hbm, acc_ref, in_sem.at[0]),
        pltpu.make_async_copy(xhat_hbm, xhat_ref, in_sem.at[1]),
    ]

    @pl.when(step == 0)
    def _():
        for fetch in fetches:
            fetch.start()

    wout = jnp.concatenate([wo0[...], wo1[...]], 0)
    win = jnp.concatenate([wi0[...], wi1[...]], 1)
    total = jnp.zeros((1, 2 * half), f32)
    for first in range(0, rows, chunk):
        at = pl.ds(first, chunk)
        slope = jnp.concatenate([slope0[at, :], slope1[at, :]], 1).astype(f32)
        inner = (nt(back_low[at, :], wout) * slope).astype(bf)
        total += jnp.sum(inner.astype(f32), axis=0, keepdims=True)
        inner_ref[at, :] = inner
    bias0[...] = jnp.broadcast_to(total[:, :half], bias0.shape)
    bias1[...] = jnp.broadcast_to(total[:, half:], bias1.shape)
    place_rows(own_ref, tn(low_ref[...], inner_ref[:, :half]).astype(bf), places)
    place_rows(other_ref, tn(low_ref[...], inner_ref[:, half:]).astype(bf), places)

    @pl.when(step == 0)
    def _():
        for fetch in fetches:
            fetch.wait()

    for first in range(0, rows, chunk):
        at = pl.ds(first, chunk)
        acc_ref[at, :] += nt(inner_ref[at, :], win)

    @pl.when(step == pl.num_programs(0) - 1)
    def _():
        gain_sum = jnp.zeros((1, D), f32)
        shift_sum = jnp.zeros((1, D), f32)
        bias_sum = jnp.zeros((1, D), f32)
        stores = []
        for i, first in enumerate(range(0, rows, chunk)):
            at = pl.ds(first, chunk)
            grad = acc_ref[at, :]
            xhat = xhat_ref[at, :]
            gain_sum += jnp.sum(grad * xhat, axis=0, keepdims=True)
            shift_sum += jnp.sum(grad, axis=0, keepdims=True)
            u = grad * line(gain_ref)
            slant = jnp.mean(u * xhat, axis=-1, keepdims=True)
            out = dev_ref[at, 0:1] * (u - jnp.mean(u, axis=-1, keepdims=True) - xhat * slant)
            bias_sum += jnp.sum(out, axis=0, keepdims=True)
            acc_ref[at, :] = out
            first_low[at, :] = out.astype(bf)
            for j, (source, target) in enumerate(((acc_ref, first_hbm), (first_low, low_hbm))):
                store = pltpu.make_async_copy(source.at[at, :], target.at[at, :], out_sem.at[2 * i + j])
                store.start()
                stores.append(store)
        sums_ref[...] = jnp.concatenate([bias_sum, gain_sum, shift_sum, jnp.zeros((5, D), f32)], 0)
        for store in stores:
            store.wait()


def ffn_backward(back_low, slope, wo, wi, low, back, xhat, dev, gain, places, width=512, chunk=512):
    rows = low.shape[0]
    half = wi[0].shape[1]
    cols = pl.BlockSpec((D, width), lambda i: (0, i))
    tall = pl.BlockSpec((width, D), lambda i: (i, 0))
    act = pl.BlockSpec((rows, width), lambda i: (0, i))
    bias = pl.BlockSpec((8, width), lambda i: (0, i))
    full = whole((rows, D))
    return pl.pallas_call(
        lambda *refs: ffn_backward_kernel(*refs, chunk=chunk, places=places),
        out_shape=(shape((D, half), bf),) * 2
        + (shape((8, half), f32),) * 2
        + (shape((rows, D), f32), shape((rows, D), bf), shape((8, D), f32)),
        grid=(half // width,),
        in_specs=[full, act, act, tall, tall, cols, cols, full, anywhere(), anywhere(), whole((rows, 128)), whole((D,))],
        out_specs=[cols] * 2 + [bias] * 2 + [anywhere()] * 2 + [whole((8, D))],
        scratch_shapes=[
            pltpu.VMEM((rows, 2 * width), bf),
            pltpu.VMEM((rows, D), f32),
            pltpu.VMEM((rows, D), f32),
            pltpu.VMEM((rows, D), bf),
            pltpu.SemaphoreType.DMA((2,)),
            pltpu.SemaphoreType.DMA((2 * (rows // chunk),)),
        ],
        name="ffn_backward",
        **settings(40e9, 58),
    )(back_low, *slope, *wo, *wi, low, back, xhat, dev, gain)


def pair_backward(q, k, v, ctx, inv, grad, es):
    size = q.shape[0]
    lane = lax.broadcasted_iota(jnp.int32, (size, 128), 1)
    low = lane < 64
    one = jnp.ones((), bf)
    zero = jnp.zeros((), bf)
    grad = grad * inv
    prod = grad * ctx.astype(f32)
    grad = grad.astype(bf)
    dss = []
    for h in range(2):
        mine = low if h == 0 else ~low
        base = 64 if h == 0 else 0
        delta = -jnp.sum(jnp.where(mine, prod, 0.0), axis=-1, keepdims=True)
        high = delta.astype(bf)
        rest = (delta - high.astype(f32)).astype(bf)
        gh = jnp.where(mine, grad, jnp.where(lane == base, high, jnp.where(lane == base + 1, rest, zero)))
        dp = nt(gh, jnp.where(mine, v, one))
        dss.append((es[h].astype(f32) * dp).astype(bf))
    dq = jnp.where(low, nn(dss[0], k), nn(dss[1], k))
    q_t = q.T
    g_t = grad.T
    dk = jnp.concatenate([nn(q_t[:64], dss[0]), nn(q_t[64:], dss[1])], 0).T
    dv = jnp.concatenate([nn(g_t[:64], es[0]), nn(g_t[64:], es[1])], 0).T
    return dq.astype(bf), dk.astype(bf), dv.astype(bf)


def attention_backward_kernel(
    side_ref, x0, x1, low_ref, qkv_ref, ctx_ref, inv_ref, el_ref, es_ref, wo0, wo1, sums_a, sums_b, sums_c, bias0, bias1,
    out_ref, own_a, own_b, other_a, other_b, small0, small1, grad_ref, *, places_a, places_b,
):
    step = pl.program_id(0)
    half = x0.shape[0]
    rows = 2 * half
    scale = jnp.asarray(0.125, bf)
    low = low_ref[...]
    grad_ref[...] = nt(low, jnp.concatenate([wo0[...], wo1[...]], 0)).astype(bf)
    for first, size, index in slots(rows):
        at = pl.ds(first, size)
        for p in range(2):
            cols = [slice(256 * i + 128 * p, 256 * i + 128 * p + 128) for i in range(3)]
            q = qkv_ref[at, cols[0]] * scale
            k = qkv_ref[at, cols[1]] * scale
            v = qkv_ref[at, cols[2]]
            if size == LONG:
                es = [el_ref[0, 4 * index + 2 * p + h] for h in range(2)]
            else:
                es = [es_ref[0, 4 * (index - half // LONG) + 2 * p + h] for h in range(2)]
            grads = pair_backward(q, k, v, ctx_ref[at, cols[0]], inv_ref[at, cols[0]], grad_ref[at, cols[0]].astype(f32), es)
            for i in range(3):
                out_ref[at, cols[i]] = grads[i]
    packed = out_ref[...]
    wide = (tn(x0[...], packed[:half]) + tn(x1[...], packed[half:])).astype(bf)
    tail = tn(low, ctx_ref[...]).astype(bf)
    for side, (ref_a, ref_b) in enumerate(((own_a, own_b), (other_a, other_b))):
        pieces = [wide[:, 256 * i + 128 * side : 256 * i + 128 * side + 128] for i in range(3)]
        pieces.append(tail[:, 128 * side : 128 * side + 128])
        place_rows(ref_a, jnp.concatenate(pieces[:2], 1), places_a)
        place_rows(ref_b, jnp.concatenate(pieces[2:], 1), places_b)

    @pl.when(step == 0)
    def _():
        for ref, bias in ((small0, bias0), (small1, bias1)):
            ref[0:3, :] = sums_b[1:4, :]
            ref[3:6, :] = sums_c[0:3, :]
            ref[6:8, :] = sums_a[0:2, :]
            ref[8:9, :] = sums_b[0:1, :]
            high = jnp.floor(sums_a[2:3, :] * (1.0 / 256.0))
            ref[9:10, :] = high
            for i in range(bias.shape[1] // D):
                ref[10 + i : 11 + i, :] = bias[0:1, D * i : D * i + D]
            ref[12:16, :] = jnp.zeros((4, D), f32)
            ref[13:14, :] = sums_a[2:3, :] - 256.0 * high

    sums = jnp.sum(packed.astype(f32), axis=0, keepdims=True)
    for side, ref in enumerate((small0, small1)):
        for i in range(2):
            start = pl.multiple_of(i * (D // 2) + 128 * step, 128)
            ref[12:13, pl.ds(start, 128)] = sums[:, 512 * i + 128 * side : 512 * i + 128 * side + 128]


def attention_backward(place, tokens, low, qkv, ctx, inv, e_long, e_short, wo, sums, bias, places_a, places_b):
    half = tokens.shape[0] // 4
    rows = 2 * half
    steps = ctx.shape[1] // 256
    tall = pl.BlockSpec((128, D), lambda i, *_: (i, 0))

    def part(height, width):
        return pl.BlockSpec((height, width), lambda i, *_: (0, i))

    return pl.pallas_call(
        lambda *refs: attention_backward_kernel(*refs, places_a=places_a, places_b=places_b),
        out_shape=(shape((rows, 768 * steps), bf),) + (shape((D, 256 * steps), bf),) * 4 + (shape((16, D), f32),) * 2,
        grid_spec=pltpu.PrefetchScalarGridSpec(
            num_scalar_prefetch=1,
            grid=(steps,),
            in_specs=[
                pl.BlockSpec((half, D), lambda i, side, *_: (side[0], 0)),
                pl.BlockSpec((half, D), lambda i, side, *_: (2 + side[0], 0)),
                whole((rows, D)),
                part(rows, 768),
                part(rows, 256),
                part(rows, 256),
                pl.BlockSpec((1,) + e_long.shape[1:], lambda i, *_: (i, 0, 0, 0)),
                pl.BlockSpec((1,) + e_short.shape[1:], lambda i, *_: (i, 0, 0, 0)),
                tall,
                tall,
            ]
            + [whole((8, D))] * 3
            + [whole(bias[0].shape)] * 2,
            out_specs=[part(rows, 768)] + [part(D, 256)] * 4 + [whole((16, D))] * 2,
            scratch_shapes=[pltpu.VMEM((rows, 256), bf)],
        ),
        name="attention_backward",
        **settings(1e6, 58),
    )(place[0], tokens, tokens, low, qkv, ctx, inv, e_long, e_short, *wo, *sums, *bias)


def tokens_backward_kernel(first_ref, packed_ref, wq0, wq1, wk0, wk1, wv0, wv1, out_ref):
    total = first_ref[...]
    for i in range(packed_ref.shape[1] // 768):
        weights = jnp.concatenate([w[:, 128 * i : 128 * i + 128] for w in (wq0, wq1, wk0, wk1, wv0, wv1)], 1)
        total += nt(packed_ref[:, 768 * i : 768 * i + 768], weights)
    out_ref[...] = total.astype(bf)


def tokens_backward(first, packed, wq, wk, wv):
    rows = first.shape[0]
    chunk = 512
    return pl.pallas_call(
        tokens_backward_kernel,
        out_shape=shape((rows, D), bf),
        grid=(rows // chunk,),
        in_specs=[pl.BlockSpec((chunk, D), lambda i: (i, 0)), pl.BlockSpec((chunk, packed.shape[1]), lambda i: (i, 0))]
        + [whole(wq[0].shape)] * 6,
        out_specs=pl.BlockSpec((chunk, D), lambda i: (i, 0)),
        name="tokens_backward",
        **settings(1e6, 16),
    )(first, packed, *wq, *wk, *wv)


def join_kernel(side_ref, own_ref, other_ref, out_ref, buffer_ref, in_sems, out_sems):
    half = own_ref.shape[0] // 2
    fetches = []
    stores = []
    for i, ref in enumerate((own_ref, other_ref)):
        for j in range(2):
            n = 2 * i + j
            block = 2 * j + (side_ref[0] if i == 0 else 1 - side_ref[0])
            target = out_ref.at[pl.ds(pl.multiple_of(block * half, half), half), :]
            place = buffer_ref.at[n * half : (n + 1) * half, :]
            fetches.append(pltpu.make_async_copy(ref.at[j * half : (j + 1) * half, :], place, in_sems.at[n]))
            stores.append(pltpu.make_async_copy(place, target, out_sems.at[n]))
    for fetch in fetches:
        fetch.start()
    for fetch, store in zip(fetches, stores):
        fetch.wait()
        store.start()
    for store in stores:
        store.wait()


def join_rows(place, own, other):
    return pl.pallas_call(
        join_kernel,
        out_shape=shape((2 * own.shape[0], D), own.dtype),
        grid_spec=pltpu.PrefetchScalarGridSpec(
            num_scalar_prefetch=1,
            grid=(1,),
            in_specs=[anywhere(), anywhere()],
            out_specs=anywhere(),
            scratch_shapes=[
                pltpu.VMEM((2 * own.shape[0], D), own.dtype),
                pltpu.SemaphoreType.DMA((4,)),
                pltpu.SemaphoreType.DMA((4,)),
            ],
        ),
        name="join_rows",
        **settings(1e6, 4),
    )(place[0], own, other)


def exchange_kernel(mine_ref, *refs, chains, small, count, merge, step):
    ins, outs = (refs[:count], refs[count:])
    if small is not None:
        kept, source, first = small
        arrived = ins[source][...] if first is None else ins[source][first : first + 16, :].astype(f32)
        sums = ins[kept][...] + arrived
        outs[-1][...] = sums
    base = 0
    for i, (keep, k0, recv, r0, rows) in enumerate(chains):
        half = rows // 2
        send_ref, keep_ref = (outs[0], outs[1]) if merge else (outs[2 * i], outs[2 * i + 1])
        for ref, side in ((send_ref, 1 - mine_ref[2 * step + i]), (keep_ref, mine_ref[2 * step + i])):
            at = side * half
            mine = ins[keep][pl.ds(pl.multiple_of(k0 + at, 16), half), :].astype(f32)
            sent = ins[recv][pl.ds(pl.multiple_of(r0 + at, 16), half), :].astype(f32)
            ref[base : base + half, :] = (mine + sent).astype(bf)
        end = base + half
        base = end if merge else 0
        if small is not None and i == (len(chains) - 1 if merge else 0):
            send_ref[end : end + 16, :] = sums.astype(bf)


def exchange(mine, arrays, chains, small, merge, step):
    columns = arrays[0].shape[1]
    halves = [chain[4] // 2 for chain in chains]
    extra = 0 if small is None else 16
    if merge:
        outs = [shape((sum(halves) + extra, columns), bf), shape((sum(halves), columns), bf)]
    else:
        outs = []
        for i, half in enumerate(halves):
            outs += [shape((half + (extra if i == 0 else 0), columns), bf), shape((half, columns), bf)]
    if small is not None:
        outs.append(shape((16, D), f32))
    return pl.pallas_call(
        lambda *refs: exchange_kernel(
            *refs, chains=chains, small=small, count=len(arrays), merge=merge, step=step
        ),
        out_shape=tuple(outs),
        grid_spec=pltpu.PrefetchScalarGridSpec(
            num_scalar_prefetch=1,
            grid=(1,),
            in_specs=[whole(v.shape) for v in arrays],
            out_specs=[whole(v.shape) for v in outs],
        ),
        name="exchange",
        **settings(1e6, 8),
    )(mine, *arrays)


def finish_kernel(keep_ref, recv_ref, small_in, *outs):
    rows = keep_ref.shape[0]
    total = keep_ref[...].astype(f32) + recv_ref[0:rows, :].astype(f32)
    for n, ref in enumerate(outs[:4]):
        part = total[(n // 2) * (rows // 2) : (n // 2 + 1) * (rows // 2)]
        for j in range(total.shape[1] // 256):
            ref[:, 128 * j : 128 * j + 128] = part[:, 256 * j + 128 * (n % 2) : 256 * j + 128 * (n % 2) + 128]
    small = small_in[...] + recv_ref[rows : rows + 16, :].astype(f32)
    for n in range(6):
        outs[4 + n][...] = small[n].reshape(D)
    inner_ref, query_ref, value_ref = outs[10:13]
    for i in range(inner_ref.shape[0] // D):
        inner_ref[D * i : D * i + D] = small[10 + i].reshape(D)
    half = query_ref.shape[0]
    query_ref[...] = small[12:13, :half].reshape(half)
    value_ref[...] = small[12:13, half:].reshape(half)
    count = small[9:10, 0:1] * 256.0 + small[13:14, 0:1]
    for n in range(3):
        outs[13 + n][...] = jnp.sqrt(jnp.sum(small[6 + n : 7 + n], axis=1, keepdims=True) / (count * D))


def finish(keep, recv, small, units):
    rows, columns = keep.shape
    half = columns // 2
    outs = [shape((rows // 2, half), f32)] * 4 + [shape((D,), f32)] * 6
    outs += [shape((units,), f32), shape((half,), f32), shape((half,), f32)] + [shape((1, 1), f32)] * 3
    return pl.pallas_call(
        finish_kernel,
        out_shape=tuple(outs),
        grid=(1,),
        in_specs=[whole(v.shape) for v in (keep, recv, small)],
        out_specs=[whole(v.shape) for v in outs],
        name="finish",
        **settings(1e6, 2),
    )(keep, recv, small)


def swap_tensor(value):
    return lax.ppermute(value, "tensor", [(0, 1), (1, 0)])


def dp_bits():
    count = lax.axis_size("dp")
    bits = []
    while (1 << len(bits)) < count:
        bits.append(1 << len(bits))
    return count, bits


def swap_dp(value, bit):
    count, _ = dp_bits()
    return lax.ppermute(value, "dp", [(i, i ^ bit) for i in range(count)])


def after(value, *others):
    return lax.optimization_barrier((value,) + others)[0]


def places_of(order):
    count, bits = dp_bits()
    out = []
    for i in range(count):
        position = 0
        for bit in order:
            position = 2 * position + (i // bit) % 2
        out.append(position)
    return out


def sorted_rows(value, places):
    size = value.shape[0] // len(places)
    source = [places.index(p) for p in range(len(places))]
    return jnp.concatenate([value[i * size : (i + 1) * size] for i in source], 0)


class RowScatter:
    def __init__(self, own, other, order, placed):
        if not placed:
            own, other = [sorted_rows(v, places_of(order)) for v in (own, other)]
        self.pair, self.order = ((own, other), list(order))
        self.split()

    def pick(self, side):
        size = self.pair[0].shape[0] // 2
        a, b = [lax.dynamic_slice_in_dim(v, side * size, size, 0).astype(f32) for v in self.pair]
        return (a + b).astype(bf)

    def resume(self, keep, recv, used):
        self.pair, self.order = ((keep, recv), self.order[used:])
        self.split()

    def split(self):
        mine = (lax.axis_index("dp") // self.order[0]) % 2
        self.send, self.keep = (self.pick(1 - mine), self.pick(mine))

    def step(self, *gates):
        keep = after(self.keep, *gates) if gates else self.keep
        self.pair = (keep, swap_dp(self.send, self.order[0]))
        self.order = self.order[1:]
        if self.order:
            self.split()

    def total(self):
        return self.pair[0].astype(f32) + self.pair[1].astype(f32)

    def ready(self):
        return self.send if self.order else self.pair[1]


def local(
    tokens,
    long_lengths,
    short_lengths,
    query_weight,
    query_bias,
    key_weight,
    value_weight,
    value_bias,
    output_weight,
    output_bias,
    first_gain,
    first_shift,
    inner_weight,
    inner_bias,
    outer_weight_here,
    outer_bias,
    second_gain,
    second_shift,
    out_grad,
):
    count, bits = dp_bits()
    order_a, order_b = (bits, bits[1::-1] + bits[2:])
    order_o = bits
    order_i = bits[:1] + bits[2:3] + bits[1:2] + bits[3:]
    placed = D % (16 * count) == 0
    places_a, places_b, places_o, places_i = [
        places_of(order) if placed else None for order in (order_a, order_b, order_o, order_i)
    ]
    width = query_weight.shape[1]
    place = (lax.axis_index("tensor").reshape(1), long_lengths, short_lengths)
    mine = (lax.axis_index("dp") // jnp.array([v for pair in zip(order_a, order_b) for v in pair], jnp.int32)) % 2
    bq, bv, bi, wq, wk, wv, wo, wi, w2 = [
        (v, swap_tensor(v))
        for v in (
            query_bias,
            value_bias,
            inner_bias,
            query_weight,
            key_weight,
            value_weight,
            output_weight,
            inner_weight,
            outer_weight_here,
        )
    ]
    qkv, ctx, inv, e_long, e_short, xhat, dev, low, sums_a = attention_forward(
        place, tokens, wq, wk, wv, bq, bv, wo, output_bias, first_gain, first_shift
    )
    act, slope0, slope1, block_own, back, back_low, outer_other, sums_b = ffn_forward(
        place, low, wi, bi, w2, xhat, out_grad, first_gain, first_shift, outer_bias, second_gain, second_shift, places_o
    )
    outer_other = swap_tensor(outer_other)
    outer = RowScatter(outer_weight(back_low, act, places_o), outer_other, order_o, placed)
    block_other = swap_tensor(block_own)
    back_low = after(back_low, outer.send, block_other)
    inner_own, inner_other, bias0, bias1, first, first_low, sums_c = ffn_backward(
        back_low, (slope0, slope1), w2, wi, low, back, xhat, dev, first_gain, places_i
    )
    outer.step(sums_c)
    inner_own, inner_other, first_low, first = lax.optimization_barrier(
        (inner_own, inner_other, first_low, first, outer.send)
    )[:4]
    inner = RowScatter(inner_own, swap_tensor(inner_other), order_i, placed)
    first_low = after(first_low, inner.send)
    packed, own_a, own_b, other_a, other_b, small, small_other = attention_backward(
        place, tokens, first_low, qkv, ctx, inv, e_long, e_short, wo, (sums_a, sums_b, sums_c), (bias0, bias1), places_a, places_b
    )
    outer.step(small)
    other_a, other_b, small_other = [swap_tensor(after(v, outer.pair[1])) for v in (other_a, other_b, small_other)]
    inner.step(small)
    own_a, own_b, packed, small, block_own = lax.optimization_barrier(
        (own_a, own_b, packed, small, block_own, outer.pair[1], inner.pair[1])
    )[:5]

    def advance(*gates):
        for chain in (outer, inner):
            if chain.order:
                chain.step(*gates)

    if placed:
        rows = outer.pair[0].shape[0]
        chains = [(0, 0, 1, 0, rows), (2, 0, 3, 0, 2 * rows)]
        send_o, keep_o, send_i, keep_i = exchange(mine, (*outer.pair, *inner.pair), chains, None, False, 2)
        recv_o = swap_dp(send_o, order_o[2])
        own_a = after(own_a, send_o)
        chains = [(0, 0, 1, 0, D), (2, 0, 3, 0, D)]
        send_a, keep_a, send_b, keep_b, small = exchange(mine, (own_a, other_a, own_b, other_b, small, small_other), chains, (4, 5, None), False, 0)
        block_out = join_rows(place, after(block_own, send_a), block_other)
        recv_i = swap_dp(after(send_i, send_a, recv_o), order_i[1])
        outer.resume(after(keep_o, block_out), recv_o, 1)
        packed = after(packed, send_a, block_out, outer.send)
        tokens_own = tokens_backward(first, packed, wq, wk, wv)
        recv_a, recv_b = (swap_dp(send_a, order_a[0]), swap_dp(send_b, order_b[0]))
        keep_a = after(keep_a, tokens_own)
        rows = D // 2
        chains = [(0, 0, 1, 0, rows), (2, 0, 3, 0, rows)]
        send_a, keep_a, send_b, keep_b, small = exchange(mine, (keep_a, recv_a, keep_b, recv_b, small), chains, (4, 1, rows), False, 1)
        tokens_own = after(tokens_own, send_a)
        tokens_other = swap_tensor(tokens_own)
        recv_a, recv_b = (swap_dp(send_a, order_a[1]), swap_dp(send_b, order_b[1]))
        inner.resume(after(keep_i, send_a), recv_i, 1)
        rows = D // 4
        chains = [(0, 0, 1, 0, rows), (2, 0, 3, 0, rows)]
        send, keep, small = exchange(mine, (keep_a, recv_a, keep_b, recv_b, small), chains, (4, 1, rows), True, 2)
        for step in range(2, len(bits) - 1):
            recv = swap_dp(send, order_a[step])
            advance(send)
            rows = keep.shape[0] // 2
            chains = [(0, 0, 1, 0, rows), (0, rows, 1, rows, rows)]
            send, keep, small = exchange(mine, (keep, recv, small), chains, (2, 1, 2 * rows), True, step + 1)
        recv = swap_dp(send, order_a[-1])
        while outer.order or inner.order:
            advance(send)
        tokens_grad = join_rows(place, after(tokens_own, send), tokens_other)
        results = finish(after(keep, tokens_grad), recv, small, inner_bias.shape[0])
        query_grad, key_grad, value_grad, output_grad = results[:4]
        sums = list(results[4:13])
        rms = [v.reshape(()) for v in results[13:]]
    else:
        parts = [RowScatter(own_a, other_a, order_a, placed), RowScatter(own_b, other_b, order_b, placed)]
        small = small + small_other
        tokens_own = tokens_backward(first, packed, wq, wk, wv)
        tokens_grad = join_rows(place, tokens_own, swap_tensor(tokens_own))
        block_out = join_rows(place, block_own, block_other)
        for bit in bits:
            small = small + swap_dp(small, bit)
            for chain in [outer, inner] + parts:
                if chain.order:
                    chain.step()
        part_a, part_b = [part.total().reshape(D // count, -1, 2, 128) for part in parts]
        query_grad, key_grad, value_grad, output_grad = [
            v[:, :, i].reshape(-1, width) for v in (part_a, part_b) for i in range(2)
        ]
        sums = [small[i] for i in range(6)] + [small[10:12].reshape(-1), small[12, :width], small[12, width:]]
        squares = jnp.sum(small[6:9], axis=1)
        rms = jnp.sqrt(squares / ((small[9, 0] * 256.0 + small[13, 0]) * D))
    return (
        block_out,
        tokens_grad,
        query_grad,
        sums[7],
        key_grad,
        value_grad,
        sums[8],
        output_grad.T,
        sums[3],
        sums[4],
        sums[5],
        inner.total(),
        sums[6],
        outer.total().T,
        sums[2],
        sums[0],
        sums[1],
        rms[0],
        rms[1],
        rms[2],
    )


def solution(mesh):
    return jax.shard_map(
        local,
        mesh=mesh,
        in_specs=(
            P("dp", None),
            P("dp"),
            P("dp"),
            P(None, "tensor"),
            P("tensor"),
            P(None, "tensor"),
            P(None, "tensor"),
            P("tensor"),
            P("tensor", None),
            P(),
            P(),
            P(),
            P(None, "tensor"),
            P("tensor"),
            P("tensor", None),
            P(),
            P(),
            P(),
            P("dp", None),
        ),
        out_specs=(
            P("dp", None),
            P("dp", None),
            P("dp", "tensor"),
            P("tensor"),
            P("dp", "tensor"),
            P("dp", "tensor"),
            P("tensor"),
            P("tensor", "dp"),
            P(),
            P(),
            P(),
            P("dp", "tensor"),
            P("tensor"),
            P("tensor", "dp"),
            P(),
            P(),
            P(),
            P(),
            P(),
            P(),
        ),
        check_vma=False,
    )
```

```python
import jax
import jax.numpy as jnp
from jax import lax
from jax.experimental import pallas as pl
from jax.experimental.pallas import tpu as pltpu
from jax.sharding import PartitionSpec as P

D = 768
LONG = 512
SHORT = 256
eps_norm = 1e-05
bf = jnp.bfloat16
f32 = jnp.float32
shape = jax.ShapeDtypeStruct


def nt(a, b):
    return lax.dot_general(a, b, (((1,), (1,)), ((), ())), preferred_element_type=f32)


def nn(a, b):
    return lax.dot_general(a, b, (((1,), (0,)), ((), ())), preferred_element_type=f32)


def tn(a, b):
    return lax.dot_general(a, b, (((0,), (0,)), ((), ())), preferred_element_type=f32)


def whole(dims):
    return pl.BlockSpec(dims, lambda *_: (0,) * len(dims))


def anywhere():
    return pl.BlockSpec(memory_space=pl.ANY)


def settings(flops, mebibytes):
    return dict(
        compiler_params=pltpu.CompilerParams(vmem_limit_bytes=mebibytes << 20),
        cost_estimate=pl.CostEstimate(flops=int(flops), bytes_accessed=int(1e6), transcendentals=0),
    )


def line(ref):
    return ref[...].reshape(1, ref.shape[0])


def slots(rows):
    longs = rows // 2 // LONG
    shorts = rows // 2 // SHORT
    out = [(i * LONG, LONG, i) for i in range(longs)]
    return out + [(rows // 2 + i * SHORT, SHORT, longs + i) for i in range(shorts)]


def slot_length(side_ref, long_ref, short_ref, rows, index):
    longs = rows // 2 // LONG
    shorts = rows // 2 // SHORT
    if index < longs:
        return long_ref[side_ref[0] * longs + index]
    return short_ref[side_ref[0] * shorts + index - longs]


def place_rows(ref, value, places):
    if places is None:
        ref[...] = value
        return
    size = value.shape[0] // len(places)
    for i, p in enumerate(places):
        ref[p * size : (p + 1) * size, :] = value[i * size : (i + 1) * size, :]


def pair_forward(length, q, k, v, put):
    size = q.shape[0]
    lane = lax.broadcasted_iota(jnp.int32, (size, 128), 1)
    low = lane < 64
    pos = lax.broadcasted_iota(jnp.int32, (size, 128), 0)
    bias = jnp.where(pos < length, 0.0, -1e30).astype(bf)
    one = jnp.ones((), bf)
    zero = jnp.zeros((), bf)
    es = []
    for h in range(2):
        mine = low if h == 0 else ~low
        flag = lane == (64 if h == 0 else 0)
        qh = jnp.where(mine, q, jnp.where(flag, one, zero))
        kh = jnp.where(mine, k, jnp.where(flag, bias, zero))
        s = nt(qh, kh)
        m = jnp.max(s, axis=-1, keepdims=True)
        e = jnp.exp(s - m).astype(bf)
        put(h, e)
        es.append(e)
    here = jnp.where(low, one, zero)
    there = jnp.where(low, zero, one)
    both = [jnp.concatenate([v * here, here], 1), jnp.concatenate([v * there, there], 1)]
    out = nn(jnp.concatenate(es, 1), jnp.concatenate(both, 0))
    inv = 1.0 / out[:, 128:]
    return out[:, :128] * inv, inv


def attention_forward_kernel(
    side_ref, long_ref, short_ref,
    x0, x1, wq0, wq1, wk0, wk1, wv0, wv1, bq0, bq1, bv0, bv1, wo0, wo1, bo_ref, gain_ref, shift_ref,
    qkv_ref, ctx_ref, inv_ref, el_ref, es_ref, xhat_ref, dev_ref, low_ref, sums_ref, acc_ref, all_ref,
):
    step = pl.program_id(0)
    half = x0.shape[0]
    rows = 2 * half
    zero = jnp.zeros((1, 256), f32)
    cols = pl.ds(pl.multiple_of(128 * step, 128), 128)
    weights = jnp.concatenate([w[...] for w in (wq0, wq1, wk0, wk1, wv0, wv1)], 1)
    bias = [b[cols].reshape(1, 128) for b in (bq0, bq1, bv0, bv1)]
    bias = jnp.concatenate(bias[:2] + [zero] + bias[2:], 1)
    for i, x in enumerate((x0, x1)):
        qkv_ref[i * half : (i + 1) * half, :] = (nn(x[...], weights) + bias).astype(bf)
    scale = jnp.asarray(0.125, bf)
    for first, size, index in slots(rows):
        at = pl.ds(first, size)
        length = slot_length(side_ref, long_ref, short_ref, rows, index)
        for p in range(2):
            q = qkv_ref[at, 128 * p : 128 * p + 128] * scale
            k = qkv_ref[at, 256 + 128 * p : 384 + 128 * p]
            v = qkv_ref[at, 512 + 128 * p : 640 + 128 * p]

            def put(h, e, p=p, size=size, index=index):
                if size == LONG:
                    el_ref[0, 4 * index + 2 * p + h] = e
                else:
                    es_ref[0, 4 * (index - half // LONG) + 2 * p + h] = e

            ctx, inv = pair_forward(length, q, k, v, put)
            ctx_ref[at, 128 * p : 128 * p + 128] = ctx.astype(bf)
            inv_ref[at, 128 * p : 128 * p + 128] = inv
    all_ref[:, pl.ds(pl.multiple_of(256 * step, 256), 256)] = ctx_ref[...]

    @pl.when(step == pl.num_programs(0) - 1)
    def _():
        parts = []
        for i in range(0, wo0.shape[0], 128):
            parts += [wo0[i : i + 128, :], wo1[i : i + 128, :]]
        acc_ref[...] = nn(all_ref[...], jnp.concatenate(parts, 0))
        resid = jnp.zeros((1, D), f32)
        attn = jnp.zeros((1, D), f32)
        count = jnp.zeros((), jnp.int32)
        for first, size, index in slots(rows):
            at = pl.ds(first, size)
            length = slot_length(side_ref, long_ref, short_ref, rows, index)
            count += length
            usable = lax.broadcasted_iota(jnp.int32, (size, D), 0) < length
            branch = acc_ref[at, :] + line(bo_ref)
            source = x0[at, :] if first < half else x1[first - half : first - half + size, :]
            total = source.astype(f32) + branch
            resid += jnp.sum(jnp.where(usable, total * total, 0.0), axis=0, keepdims=True)
            attn += jnp.sum(jnp.where(usable, branch * branch, 0.0), axis=0, keepdims=True)
            centred = total - jnp.mean(total, axis=-1, keepdims=True)
            dev = lax.rsqrt(jnp.mean(centred * centred, axis=-1, keepdims=True) + eps_norm)
            xhat = centred * dev
            xhat_ref[at, :] = xhat
            dev_ref[at, :] = jnp.broadcast_to(dev, (size, 128))
            low_ref[at, :] = (xhat * line(gain_ref) + line(shift_ref)).astype(bf)
        count = jnp.full((1, D), count, jnp.int32).astype(f32)
        sums_ref[...] = jnp.concatenate([resid, attn, count, jnp.zeros((5, D), f32)], 0)


def attention_forward(place, tokens, wq, wk, wv, bq, bv, wo, bo, gain, shift):
    half = tokens.shape[0] // 4
    rows = 2 * half
    width = wq[0].shape[1]
    steps = width // 128
    longs = half // LONG
    shorts = half // SHORT
    wide = pl.BlockSpec((D, 128), lambda i, *_: (0, i))

    def part(columns):
        return pl.BlockSpec((rows, columns), lambda i, *_: (0, i))

    return pl.pallas_call(
        attention_forward_kernel,
        out_shape=(
            shape((rows, steps * 768), bf),
            shape((rows, steps * 256), bf),
            shape((rows, steps * 256), f32),
            shape((steps, 4 * longs, LONG, LONG), bf),
            shape((steps, 4 * shorts, SHORT, SHORT), bf),
            shape((rows, D), f32),
            shape((rows, 128), f32),
            shape((rows, D), bf),
            shape((8, D), f32),
        ),
        grid_spec=pltpu.PrefetchScalarGridSpec(
            num_scalar_prefetch=3,
            grid=(steps,),
            in_specs=[
                pl.BlockSpec((half, D), lambda i, side, *_: (side[0], 0)),
                pl.BlockSpec((half, D), lambda i, side, *_: (2 + side[0], 0)),
            ]
            + [wide] * 6
            + [whole((width,))] * 4
            + [whole((width, D))] * 2
            + [whole((D,))] * 3,
            out_specs=[
                part(768),
                part(256),
                part(256),
                pl.BlockSpec((1, 4 * longs, LONG, LONG), lambda i, *_: (i, 0, 0, 0)),
                pl.BlockSpec((1, 4 * shorts, SHORT, SHORT), lambda i, *_: (i, 0, 0, 0)),
                whole((rows, D)),
                whole((rows, 128)),
                whole((rows, D)),
                whole((8, D)),
            ],
            scratch_shapes=[pltpu.VMEM((rows, D), f32), pltpu.VMEM((rows, 2 * width), bf)],
        ),
        name="attention_forward",
        **settings(40e9, 58),
    )(*place, tokens, tokens, *wq, *wk, *wv, *bq, *bv, *wo, bo, gain, shift)


def gelu_parts(v):
    cdf = 0.5 * (1.0 + lax.erf(v * 0.7071067811865476))
    return cdf, v * (0.3989422804014327 * jnp.exp(-0.5 * (v * v)))


def ffn_forward_kernel(
    side_ref, long_ref, short_ref,
    low_ref, wi0, wi1, bi0, bi1, wo0, wo1, xhat_hbm, grad_hbm, gain1_ref, shift1_ref, bo_ref, gain_ref, shift_ref,
    act0, slope0, slope1, out_hbm, back_hbm, low_hbm, other_ref, sums_ref,
    acc_ref, act1, xhat_ref, grad_ref, out_ref, back_low, in_sem, out_sem, *, chunk, places,
):
    step = pl.program_id(0)
    rows = low_ref.shape[0]
    half = rows // 2
    width = wi0.shape[1]
    fetches = [pltpu.make_async_copy(xhat_hbm, xhat_ref, in_sem.at[0])]
    for i in range(2):
        source = grad_hbm.at[pl.ds(pl.multiple_of((2 * i + side_ref[0]) * half, half), half), :]
        fetches.append(pltpu.make_async_copy(source, grad_ref.at[i * half : (i + 1) * half, :], in_sem.at[1 + i]))

    @pl.when(step == 0)
    def _():
        for fetch in fetches:
            fetch.start()

    cols = pl.ds(pl.multiple_of(width * step, width), width)
    win = jnp.concatenate([wi0[...], wi1[...]], 1)
    bias = jnp.concatenate([b[cols].reshape(1, width) for b in (bi0, bi1)], 1)
    wout = jnp.concatenate([wo0[...], wo1[...]], 0)
    for first in range(0, rows, chunk):
        at = pl.ds(first, chunk)
        inner = nn(low_ref[at, :], win) + bias
        cdf, bell = gelu_parts(inner)
        active = (inner * cdf).astype(bf)
        slope = (cdf + bell).astype(bf)
        act0[at, :] = active[:, :width]
        act1[at, cols] = active[:, width:]
        slope0[at, :] = slope[:, :width]
        slope1[at, :] = slope[:, width:]
        part = nn(active, wout)

        @pl.when(step == 0)
        def _():
            acc_ref[at, :] = part

        @pl.when(step > 0)
        def _():
            acc_ref[at, :] += part

    @pl.when(step == pl.num_programs(0) - 1)
    def _():
        for fetch in fetches:
            fetch.wait()
        ffn_sum = jnp.zeros((1, D), f32)
        gain_sum = jnp.zeros((1, D), f32)
        shift_sum = jnp.zeros((1, D), f32)
        bias_sum = jnp.zeros((1, D), f32)
        stores = []
        for i, (first, size, index) in enumerate(slots(rows)):
            at = pl.ds(first, size)
            length = slot_length(side_ref, long_ref, short_ref, rows, index)
            usable = lax.broadcasted_iota(jnp.int32, (size, D), 0) < length
            ffn = acc_ref[at, :] + line(bo_ref)
            ffn_sum += jnp.sum(jnp.where(usable, ffn * ffn, 0.0), axis=0, keepdims=True)
            total = xhat_ref[at, :] * line(gain1_ref) + line(shift1_ref) + ffn
            centred = total - jnp.mean(total, axis=-1, keepdims=True)
            dev = lax.rsqrt(jnp.mean(centred * centred, axis=-1, keepdims=True) + eps_norm)
            xhat = centred * dev
            out_ref[at, :] = (xhat * line(gain_ref) + line(shift_ref)).astype(bf)
            cot = jnp.where(usable, grad_ref[at, :].astype(f32), 0.0)
            gain_sum += jnp.sum(cot * xhat, axis=0, keepdims=True)
            shift_sum += jnp.sum(cot, axis=0, keepdims=True)
            u = cot * line(gain_ref)
            slant = jnp.mean(u * xhat, axis=-1, keepdims=True)
            back = dev * (u - jnp.mean(u, axis=-1, keepdims=True) - xhat * slant)
            bias_sum += jnp.sum(back, axis=0, keepdims=True)
            acc_ref[at, :] = back
            back_low[at, :] = back.astype(bf)
            for j, (source, target) in enumerate(((out_ref, out_hbm), (acc_ref, back_hbm), (back_low, low_hbm))):
                store = pltpu.make_async_copy(source.at[at, :], target.at[at, :], out_sem.at[3 * i + j])
                store.start()
                stores.append(store)
        sums_ref[...] = jnp.concatenate([ffn_sum, gain_sum, shift_sum, bias_sum, jnp.zeros((4, D), f32)], 0)
        place_rows(other_ref, tn(back_low[...], act1[...]).astype(bf), places)
        for store in stores:
            store.wait()


def ffn_forward(place, low, wi, bi, wo, xhat, grad, gain1, shift1, bo, gain, shift, places, width=512, chunk=512):
    rows = low.shape[0]
    half = wi[0].shape[1]
    cols = pl.BlockSpec((D, width), lambda i, *_: (0, i))
    tall = pl.BlockSpec((width, D), lambda i, *_: (i, 0))
    act = pl.BlockSpec((rows, width), lambda i, *_: (0, i))
    row = whole((D,))
    count = len(slots(rows))
    return pl.pallas_call(
        lambda *refs: ffn_forward_kernel(*refs, chunk=chunk, places=places),
        out_shape=(shape((rows, half), bf),) * 3
        + (shape((rows, D), bf), shape((rows, D), f32), shape((rows, D), bf), shape((D, half), bf), shape((8, D), f32)),
        grid_spec=pltpu.PrefetchScalarGridSpec(
            num_scalar_prefetch=3,
            grid=(half // width,),
            in_specs=[whole((rows, D)), cols, cols, whole((half,)), whole((half,)), tall, tall, anywhere(), anywhere()] + [row] * 5,
            out_specs=[act] * 3 + [anywhere()] * 3 + [whole((D, half)), whole((8, D))],
            scratch_shapes=[
                pltpu.VMEM((rows, D), f32),
                pltpu.VMEM((rows, half), bf),
                pltpu.VMEM((rows, D), f32),
                pltpu.VMEM((rows, D), bf),
                pltpu.VMEM((rows, D), bf),
                pltpu.VMEM((rows, D), bf),
                pltpu.SemaphoreType.DMA((3,)),
                pltpu.SemaphoreType.DMA((3 * count,)),
            ],
        ),
        name="ffn_forward",
        **settings(40e9, 58),
    )(*place, low, *wi, *bi, *wo, xhat, grad, gain1, shift1, bo, gain, shift)


def outer_weight_kernel(low_ref, act_ref, out_ref, *, places):
    place_rows(out_ref, tn(low_ref[...], act_ref[...]).astype(bf), places)


def outer_weight(low, act, places, width=512):
    rows, half = act.shape
    return pl.pallas_call(
        lambda *refs: outer_weight_kernel(*refs, places=places),
        out_shape=shape((D, half), bf),
        grid=(half // width,),
        in_specs=[whole((rows, D)), pl.BlockSpec((rows, width), lambda i: (0, i))],
        out_specs=pl.BlockSpec((D, width), lambda i: (0, i)),
        name="outer_weight",
        **settings(10e9, 8),
    )(low, act)


def ffn_backward_kernel(
    back_low, slope0, slope1, wo0, wo1, wi0, wi1, low_ref, back_hbm, xhat_hbm, dev_ref, gain_ref,
    own_ref, other_ref, bias0, bias1, first_hbm, low_hbm, sums_ref,
    inner_ref, acc_ref, xhat_ref, first_low, in_sem, out_sem, *, chunk, places,
):
    step = pl.program_id(0)
    rows = low_ref.shape[0]
    half = wi0.shape[1]
    fetches = [
        pltpu.make_async_copy(back_hbm, acc_ref, in_sem.at[0]),
        pltpu.make_async_copy(xhat_hbm, xhat_ref, in_sem.at[1]),
    ]

    @pl.when(step == 0)
    def _():
        for fetch in fetches:
            fetch.start()

    wout = jnp.concatenate([wo0[...], wo1[...]], 0)
    win = jnp.concatenate([wi0[...], wi1[...]], 1)
    total = jnp.zeros((1, 2 * half), f32)
    for first in range(0, rows, chunk):
        at = pl.ds(first, chunk)
        slope = jnp.concatenate([slope0[at, :], slope1[at, :]], 1).astype(f32)
        inner = (nt(back_low[at, :], wout) * slope).astype(bf)
        total += jnp.sum(inner.astype(f32), axis=0, keepdims=True)
        inner_ref[at, :] = inner
    bias0[...] = jnp.broadcast_to(total[:, :half], bias0.shape)
    bias1[...] = jnp.broadcast_to(total[:, half:], bias1.shape)
    place_rows(own_ref, tn(low_ref[...], inner_ref[:, :half]).astype(bf), places)
    place_rows(other_ref, tn(low_ref[...], inner_ref[:, half:]).astype(bf), places)

    @pl.when(step == 0)
    def _():
        for fetch in fetches:
            fetch.wait()

    for first in range(0, rows, chunk):
        at = pl.ds(first, chunk)
        acc_ref[at, :] += nt(inner_ref[at, :], win)

    @pl.when(step == pl.num_programs(0) - 1)
    def _():
        gain_sum = jnp.zeros((1, D), f32)
        shift_sum = jnp.zeros((1, D), f32)
        bias_sum = jnp.zeros((1, D), f32)
        stores = []
        for i, first in enumerate(range(0, rows, chunk)):
            at = pl.ds(first, chunk)
            grad = acc_ref[at, :]
            xhat = xhat_ref[at, :]
            gain_sum += jnp.sum(grad * xhat, axis=0, keepdims=True)
            shift_sum += jnp.sum(grad, axis=0, keepdims=True)
            u = grad * line(gain_ref)
            slant = jnp.mean(u * xhat, axis=-1, keepdims=True)
            out = dev_ref[at, 0:1] * (u - jnp.mean(u, axis=-1, keepdims=True) - xhat * slant)
            bias_sum += jnp.sum(out, axis=0, keepdims=True)
            acc_ref[at, :] = out
            first_low[at, :] = out.astype(bf)
            for j, (source, target) in enumerate(((acc_ref, first_hbm), (first_low, low_hbm))):
                store = pltpu.make_async_copy(source.at[at, :], target.at[at, :], out_sem.at[2 * i + j])
                store.start()
                stores.append(store)
        sums_ref[...] = jnp.concatenate([bias_sum, gain_sum, shift_sum, jnp.zeros((5, D), f32)], 0)
        for store in stores:
            store.wait()


def ffn_backward(back_low, slope, wo, wi, low, back, xhat, dev, gain, places, width=512, chunk=512):
    rows = low.shape[0]
    half = wi[0].shape[1]
    cols = pl.BlockSpec((D, width), lambda i: (0, i))
    tall = pl.BlockSpec((width, D), lambda i: (i, 0))
    act = pl.BlockSpec((rows, width), lambda i: (0, i))
    bias = pl.BlockSpec((8, width), lambda i: (0, i))
    full = whole((rows, D))
    return pl.pallas_call(
        lambda *refs: ffn_backward_kernel(*refs, chunk=chunk, places=places),
        out_shape=(shape((D, half), bf),) * 2
        + (shape((8, half), f32),) * 2
        + (shape((rows, D), f32), shape((rows, D), bf), shape((8, D), f32)),
        grid=(half // width,),
        in_specs=[full, act, act, tall, tall, cols, cols, full, anywhere(), anywhere(), whole((rows, 128)), whole((D,))],
        out_specs=[cols] * 2 + [bias] * 2 + [anywhere()] * 2 + [whole((8, D))],
        scratch_shapes=[
            pltpu.VMEM((rows, 2 * width), bf),
            pltpu.VMEM((rows, D), f32),
            pltpu.VMEM((rows, D), f32),
            pltpu.VMEM((rows, D), bf),
            pltpu.SemaphoreType.DMA((2,)),
            pltpu.SemaphoreType.DMA((2 * (rows // chunk),)),
        ],
        name="ffn_backward",
        **settings(40e9, 58),
    )(back_low, *slope, *wo, *wi, low, back, xhat, dev, gain)


def pair_backward(q, k, v, ctx, inv, grad, es):
    size = q.shape[0]
    lane = lax.broadcasted_iota(jnp.int32, (size, 128), 1)
    low = lane < 64
    one = jnp.ones((), bf)
    zero = jnp.zeros((), bf)
    grad = grad * inv
    prod = grad * ctx.astype(f32)
    grad = grad.astype(bf)
    dss = []
    for h in range(2):
        mine = low if h == 0 else ~low
        base = 64 if h == 0 else 0
        delta = -jnp.sum(jnp.where(mine, prod, 0.0), axis=-1, keepdims=True)
        high = delta.astype(bf)
        rest = (delta - high.astype(f32)).astype(bf)
        gh = jnp.where(mine, grad, jnp.where(lane == base, high, jnp.where(lane == base + 1, rest, zero)))
        dp = nt(gh, jnp.where(mine, v, one))
        dss.append((es[h].astype(f32) * dp).astype(bf))
    dq = jnp.where(low, nn(dss[0], k), nn(dss[1], k))
    q_t = q.T
    g_t = grad.T
    dk = jnp.concatenate([nn(q_t[:64], dss[0]), nn(q_t[64:], dss[1])], 0).T
    dv = jnp.concatenate([nn(g_t[:64], es[0]), nn(g_t[64:], es[1])], 0).T
    return dq.astype(bf), dk.astype(bf), dv.astype(bf)


def attention_backward_kernel(
    side_ref, x0, x1, low_ref, qkv_ref, ctx_ref, inv_ref, el_ref, es_ref, wo0, wo1, sums_a, sums_b, sums_c, bias0, bias1,
    out_ref, own_a, own_b, other_a, other_b, small0, small1, grad_ref, *, places_a, places_b,
):
    step = pl.program_id(0)
    half = x0.shape[0]
    rows = 2 * half
    scale = jnp.asarray(0.125, bf)
    low = low_ref[...]
    grad_ref[...] = nt(low, jnp.concatenate([wo0[...], wo1[...]], 0)).astype(bf)
    for first, size, index in slots(rows):
        at = pl.ds(first, size)
        for p in range(2):
            cols = [slice(256 * i + 128 * p, 256 * i + 128 * p + 128) for i in range(3)]
            q = qkv_ref[at, cols[0]] * scale
            k = qkv_ref[at, cols[1]] * scale
            v = qkv_ref[at, cols[2]]
            if size == LONG:
                es = [el_ref[0, 4 * index + 2 * p + h] for h in range(2)]
            else:
                es = [es_ref[0, 4 * (index - half // LONG) + 2 * p + h] for h in range(2)]
            grads = pair_backward(q, k, v, ctx_ref[at, cols[0]], inv_ref[at, cols[0]], grad_ref[at, cols[0]].astype(f32), es)
            for i in range(3):
                out_ref[at, cols[i]] = grads[i]
    packed = out_ref[...]
    wide = (tn(x0[...], packed[:half]) + tn(x1[...], packed[half:])).astype(bf)
    tail = tn(low, ctx_ref[...]).astype(bf)
    for side, (ref_a, ref_b) in enumerate(((own_a, own_b), (other_a, other_b))):
        pieces = [wide[:, 256 * i + 128 * side : 256 * i + 128 * side + 128] for i in range(3)]
        pieces.append(tail[:, 128 * side : 128 * side + 128])
        place_rows(ref_a, jnp.concatenate(pieces[:2], 1), places_a)
        place_rows(ref_b, jnp.concatenate(pieces[2:], 1), places_b)

    @pl.when(step == 0)
    def _():
        for ref, bias in ((small0, bias0), (small1, bias1)):
            ref[0:3, :] = sums_b[1:4, :]
            ref[3:6, :] = sums_c[0:3, :]
            ref[6:8, :] = sums_a[0:2, :]
            ref[8:9, :] = sums_b[0:1, :]
            high = jnp.floor(sums_a[2:3, :] * (1.0 / 256.0))
            ref[9:10, :] = high
            for i in range(bias.shape[1] // D):
                ref[10 + i : 11 + i, :] = bias[0:1, D * i : D * i + D]
            ref[12:16, :] = jnp.zeros((4, D), f32)
            ref[13:14, :] = sums_a[2:3, :] - 256.0 * high

    sums = jnp.sum(packed.astype(f32), axis=0, keepdims=True)
    for side, ref in enumerate((small0, small1)):
        for i in range(2):
            start = pl.multiple_of(i * (D // 2) + 128 * step, 128)
            ref[12:13, pl.ds(start, 128)] = sums[:, 512 * i + 128 * side : 512 * i + 128 * side + 128]


def attention_backward(place, tokens, low, qkv, ctx, inv, e_long, e_short, wo, sums, bias, places_a, places_b):
    half = tokens.shape[0] // 4
    rows = 2 * half
    steps = ctx.shape[1] // 256
    tall = pl.BlockSpec((128, D), lambda i, *_: (i, 0))

    def part(height, width):
        return pl.BlockSpec((height, width), lambda i, *_: (0, i))

    return pl.pallas_call(
        lambda *refs: attention_backward_kernel(*refs, places_a=places_a, places_b=places_b),
        out_shape=(shape((rows, 768 * steps), bf),) + (shape((D, 256 * steps), bf),) * 4 + (shape((16, D), f32),) * 2,
        grid_spec=pltpu.PrefetchScalarGridSpec(
            num_scalar_prefetch=1,
            grid=(steps,),
            in_specs=[
                pl.BlockSpec((half, D), lambda i, side, *_: (side[0], 0)),
                pl.BlockSpec((half, D), lambda i, side, *_: (2 + side[0], 0)),
                whole((rows, D)),
                part(rows, 768),
                part(rows, 256),
                part(rows, 256),
                pl.BlockSpec((1,) + e_long.shape[1:], lambda i, *_: (i, 0, 0, 0)),
                pl.BlockSpec((1,) + e_short.shape[1:], lambda i, *_: (i, 0, 0, 0)),
                tall,
                tall,
            ]
            + [whole((8, D))] * 3
            + [whole(bias[0].shape)] * 2,
            out_specs=[part(rows, 768)] + [part(D, 256)] * 4 + [whole((16, D))] * 2,
            scratch_shapes=[pltpu.VMEM((rows, 256), bf)],
        ),
        name="attention_backward",
        **settings(1e6, 58),
    )(place[0], tokens, tokens, low, qkv, ctx, inv, e_long, e_short, *wo, *sums, *bias)


def tokens_backward_kernel(first_ref, packed_ref, wq0, wq1, wk0, wk1, wv0, wv1, out_ref):
    total = first_ref[...]
    for i in range(packed_ref.shape[1] // 768):
        weights = jnp.concatenate([w[:, 128 * i : 128 * i + 128] for w in (wq0, wq1, wk0, wk1, wv0, wv1)], 1)
        total += nt(packed_ref[:, 768 * i : 768 * i + 768], weights)
    out_ref[...] = total.astype(bf)


def tokens_backward(first, packed, wq, wk, wv):
    rows = first.shape[0]
    chunk = 512
    return pl.pallas_call(
        tokens_backward_kernel,
        out_shape=shape((rows, D), bf),
        grid=(rows // chunk,),
        in_specs=[pl.BlockSpec((chunk, D), lambda i: (i, 0)), pl.BlockSpec((chunk, packed.shape[1]), lambda i: (i, 0))]
        + [whole(wq[0].shape)] * 6,
        out_specs=pl.BlockSpec((chunk, D), lambda i: (i, 0)),
        name="tokens_backward",
        **settings(1e6, 16),
    )(first, packed, *wq, *wk, *wv)


def join_kernel(side_ref, own_ref, other_ref, out_ref, buffer_ref, in_sems, out_sems):
    half = own_ref.shape[0] // 2
    fetches = []
    stores = []
    for i, ref in enumerate((own_ref, other_ref)):
        for j in range(2):
            n = 2 * i + j
            block = 2 * j + (side_ref[0] if i == 0 else 1 - side_ref[0])
            target = out_ref.at[pl.ds(pl.multiple_of(block * half, half), half), :]
            place = buffer_ref.at[n * half : (n + 1) * half, :]
            fetches.append(pltpu.make_async_copy(ref.at[j * half : (j + 1) * half, :], place, in_sems.at[n]))
            stores.append(pltpu.make_async_copy(place, target, out_sems.at[n]))
    for fetch in fetches:
        fetch.start()
    for fetch, store in zip(fetches, stores):
        fetch.wait()
        store.start()
    for store in stores:
        store.wait()


def join_rows(place, own, other):
    return pl.pallas_call(
        join_kernel,
        out_shape=shape((2 * own.shape[0], D), own.dtype),
        grid_spec=pltpu.PrefetchScalarGridSpec(
            num_scalar_prefetch=1,
            grid=(1,),
            in_specs=[anywhere(), anywhere()],
            out_specs=anywhere(),
            scratch_shapes=[
                pltpu.VMEM((2 * own.shape[0], D), own.dtype),
                pltpu.SemaphoreType.DMA((4,)),
                pltpu.SemaphoreType.DMA((4,)),
            ],
        ),
        name="join_rows",
        **settings(1e6, 4),
    )(place[0], own, other)


def exchange_kernel(mine_ref, *refs, chains, small, count, merge, step):
    ins, outs = (refs[:count], refs[count:])
    if small is not None:
        kept, source, first = small
        arrived = ins[source][...] if first is None else ins[source][first : first + 16, :].astype(f32)
        sums = ins[kept][...] + arrived
        sums = sums.astype(bf)
        outs[-1][...] = sums.astype(f32)
    base = 0
    for i, (keep, k0, recv, r0, rows) in enumerate(chains):
        half = rows // 2
        send_ref, keep_ref = (outs[0], outs[1]) if merge else (outs[2 * i], outs[2 * i + 1])
        for ref, side in ((send_ref, 1 - mine_ref[2 * step + i]), (keep_ref, mine_ref[2 * step + i])):
            at = side * half
            mine = ins[keep][pl.ds(pl.multiple_of(k0 + at, 16), half), :].astype(f32)
            sent = ins[recv][pl.ds(pl.multiple_of(r0 + at, 16), half), :].astype(f32)
            ref[base : base + half, :] = (mine + sent).astype(bf)
        end = base + half
        base = end if merge else 0
        if small is not None and i == (len(chains) - 1 if merge else 0):
            send_ref[end : end + 16, :] = sums


def exchange(mine, arrays, chains, small, merge, step):
    columns = arrays[0].shape[1]
    halves = [chain[4] // 2 for chain in chains]
    extra = 0 if small is None else 16
    if merge:
        outs = [shape((sum(halves) + extra, columns), bf), shape((sum(halves), columns), bf)]
    else:
        outs = []
        for i, half in enumerate(halves):
            kind = shape
            outs += [kind((half + (extra if i == 0 else 0), columns), bf), kind((half, columns), bf)]
    if small is not None:
        outs.append(shape((16, D), f32))
    return pl.pallas_call(
        lambda *refs: exchange_kernel(
            *refs, chains=chains, small=small, count=len(arrays), merge=merge, step=step
        ),
        out_shape=tuple(outs),
        grid_spec=pltpu.PrefetchScalarGridSpec(
            num_scalar_prefetch=1,
            grid=(1,),
            in_specs=[whole(v.shape) for v in arrays],
            out_specs=[whole(v.shape) for v in outs],
        ),
        name="exchange",
        **settings(1e6, 8),
    )(mine, *arrays)


def finish_kernel(keep_ref, recv_ref, small_in, *outs):
    rows = keep_ref.shape[0]
    total = keep_ref[...].astype(f32) + recv_ref[0:rows, :].astype(f32)
    for n, ref in enumerate(outs[:4]):
        part = total[(n // 2) * (rows // 2) : (n // 2 + 1) * (rows // 2)]
        for j in range(total.shape[1] // 256):
            ref[:, 128 * j : 128 * j + 128] = part[:, 256 * j + 128 * (n % 2) : 256 * j + 128 * (n % 2) + 128]
    small = small_in[...] + recv_ref[rows : rows + 16, :].astype(f32)
    for n in range(6):
        outs[4 + n][...] = small[n].reshape(D)
    inner_ref, query_ref, value_ref = outs[10:13]
    for i in range(inner_ref.shape[0] // D):
        inner_ref[D * i : D * i + D] = small[10 + i].reshape(D)
    half = query_ref.shape[0]
    query_ref[...] = small[12:13, :half].reshape(half)
    value_ref[...] = small[12:13, half:].reshape(half)
    count = small[9:10, 0:1] * 256.0 + small[13:14, 0:1]
    for n in range(3):
        outs[13 + n][...] = jnp.sqrt(jnp.sum(small[6 + n : 7 + n], axis=1, keepdims=True) / (count * D))


def finish(keep, recv, small, units):
    rows, columns = keep.shape
    half = columns // 2
    outs = [shape((rows // 2, half), f32)] * 4 + [shape((D,), f32)] * 6
    outs += [shape((units,), f32), shape((half,), f32), shape((half,), f32)] + [shape((1, 1), f32)] * 3
    return pl.pallas_call(
        finish_kernel,
        out_shape=tuple(outs),
        grid=(1,),
        in_specs=[whole(v.shape) for v in (keep, recv, small)],
        out_specs=[whole(v.shape) for v in outs],
        name="finish",
        **settings(1e6, 2),
    )(keep, recv, small)


def swap_tensor(value):
    return lax.ppermute(value, "tensor", [(0, 1), (1, 0)])


def dp_bits():
    count = lax.axis_size("dp")
    bits = []
    while (1 << len(bits)) < count:
        bits.append(1 << len(bits))
    return count, bits


def swap_dp(value, bit):
    count, _ = dp_bits()
    return lax.ppermute(value, "dp", [(i, i ^ bit) for i in range(count)])


def after(value, *others):
    return lax.optimization_barrier((value,) + others)[0]


def places_of(order):
    count, bits = dp_bits()
    out = []
    for i in range(count):
        position = 0
        for bit in order:
            position = 2 * position + (i // bit) % 2
        out.append(position)
    return out


def sorted_rows(value, places):
    size = value.shape[0] // len(places)
    source = [places.index(p) for p in range(len(places))]
    return jnp.concatenate([value[i * size : (i + 1) * size] for i in source], 0)


class RowScatter:
    def __init__(self, own, other, order, placed):
        if not placed:
            own, other = [sorted_rows(v, places_of(order)) for v in (own, other)]
        self.pair, self.order = ((own, other), list(order))
        self.split()

    def pick(self, side):
        size = self.pair[0].shape[0] // 2
        a, b = [lax.dynamic_slice_in_dim(v, side * size, size, 0).astype(f32) for v in self.pair]
        return (a + b).astype(bf)

    def resume(self, keep, recv, used):
        self.pair, self.order = ((keep, recv), self.order[used:])
        self.split()

    def split(self):
        mine = (lax.axis_index("dp") // self.order[0]) % 2
        self.send, self.keep = (self.pick(1 - mine), self.pick(mine))

    def step(self, *gates):
        keep = after(self.keep, *gates) if gates else self.keep
        self.pair = (keep, swap_dp(self.send, self.order[0]))
        self.order = self.order[1:]
        if self.order:
            self.split()

    def total(self):
        return self.pair[0].astype(f32) + self.pair[1].astype(f32)

    def ready(self):
        return self.send if self.order else self.pair[1]


def local(
    tokens,
    long_lengths,
    short_lengths,
    query_weight,
    query_bias,
    key_weight,
    value_weight,
    value_bias,
    output_weight,
    output_bias,
    first_gain,
    first_shift,
    inner_weight,
    inner_bias,
    outer_weight_here,
    outer_bias,
    second_gain,
    second_shift,
    out_grad,
):
    count, bits = dp_bits()
    order_a, order_b = (bits, bits[1::-1] + bits[2:])
    order_o = bits
    order_i = bits[:1] + bits[2:3] + bits[1:2] + bits[3:]
    placed = D % (16 * count) == 0
    places_a, places_b, places_o, places_i = [
        places_of(order) if placed else None for order in (order_a, order_b, order_o, order_i)
    ]
    width = query_weight.shape[1]
    place = (lax.axis_index("tensor").reshape(1), long_lengths, short_lengths)
    mine = (lax.axis_index("dp") // jnp.array([v for pair in zip(order_a, order_b) for v in pair], jnp.int32)) % 2
    bq, bv, bi, wq, wk, wv, wo, wi, w2 = [
        (v, swap_tensor(v))
        for v in (
            query_bias,
            value_bias,
            inner_bias,
            query_weight,
            key_weight,
            value_weight,
            output_weight,
            inner_weight,
            outer_weight_here,
        )
    ]
    qkv, ctx, inv, e_long, e_short, xhat, dev, low, sums_a = attention_forward(
        place, tokens, wq, wk, wv, bq, bv, wo, output_bias, first_gain, first_shift
    )
    act, slope0, slope1, block_own, back, back_low, outer_other, sums_b = ffn_forward(
        place, low, wi, bi, w2, xhat, out_grad, first_gain, first_shift, outer_bias, second_gain, second_shift, places_o
    )
    outer_other = swap_tensor(outer_other)
    outer = RowScatter(outer_weight(back_low, act, places_o), outer_other, order_o, placed)
    block_other = swap_tensor(block_own)
    back_low = after(back_low, outer.send, block_other)
    inner_own, inner_other, bias0, bias1, first, first_low, sums_c = ffn_backward(
        back_low, (slope0, slope1), w2, wi, low, back, xhat, dev, first_gain, places_i
    )
    outer.step(sums_c)
    inner_own, inner_other, first_low, first = lax.optimization_barrier(
        (inner_own, inner_other, first_low, first, outer.send)
    )[:4]
    inner = RowScatter(inner_own, swap_tensor(inner_other), order_i, placed)
    first_low = after(first_low, inner.send)
    packed, own_a, own_b, other_a, other_b, small, small_other = attention_backward(
        place, tokens, first_low, qkv, ctx, inv, e_long, e_short, wo, (sums_a, sums_b, sums_c), (bias0, bias1), places_a, places_b
    )
    outer.step(small)
    other_a, other_b, small_other = [swap_tensor(after(v, outer.pair[1])) for v in (other_a, other_b, small_other)]
    inner.step(small)
    own_a, own_b, packed, small, block_own = lax.optimization_barrier(
        (own_a, own_b, packed, small, block_own, outer.pair[1], inner.pair[1])
    )[:5]

    def advance(*gates):
        for chain in (outer, inner):
            if chain.order:
                chain.step(*gates)

    if placed:
        rows = outer.pair[0].shape[0]
        chains = [(0, 0, 1, 0, rows), (2, 0, 3, 0, 2 * rows)]
        send_o, keep_o, send_i, keep_i = exchange(mine, (*outer.pair, *inner.pair), chains, None, False, 2)
        recv_o = swap_dp(send_o, order_o[2])
        own_a = after(own_a, send_o)
        chains = [(0, 0, 1, 0, D), (2, 0, 3, 0, D)]
        send_a, keep_a, send_b, keep_b, small = exchange(mine, (own_a, other_a, own_b, other_b, small, small_other), chains, (4, 5, None), False, 0)
        block_out = join_rows(place, after(block_own, send_a), block_other)
        recv_i = swap_dp(after(send_i, send_a, recv_o), order_i[1])
        outer.resume(after(keep_o, block_out), recv_o, 1)
        packed = after(packed, send_a, block_out, outer.send)
        tokens_own = tokens_backward(first, packed, wq, wk, wv)
        recv_a, recv_b = (swap_dp(send_a, order_a[0]), swap_dp(send_b, order_b[0]))
        keep_a = after(keep_a, tokens_own)
        rows = D // 2
        chains = [(0, 0, 1, 0, rows), (2, 0, 3, 0, rows)]
        send_a, keep_a, send_b, keep_b, small = exchange(mine, (keep_a, recv_a, keep_b, recv_b, small), chains, (4, 1, rows), False, 1)
        tokens_own = after(tokens_own, send_a)
        tokens_other = swap_tensor(tokens_own)
        recv_a, recv_b = (swap_dp(send_a, order_a[1]), swap_dp(send_b, order_b[1]))
        inner.resume(after(keep_i, send_a), recv_i, 1)
        rows = D // 4
        chains = [(0, 0, 1, 0, rows), (2, 0, 3, 0, rows)]
        send, keep, small = exchange(mine, (keep_a, recv_a, keep_b, recv_b, small), chains, (4, 1, rows), True, 2)
        for step in range(2, len(bits) - 1):
            recv = swap_dp(send, order_a[step])
            advance(send)
            rows = keep.shape[0] // 2
            chains = [(0, 0, 1, 0, rows), (0, rows, 1, rows, rows)]
            send, keep, small = exchange(mine, (keep, recv, small), chains, (2, 1, 2 * rows), True, step + 1)
        recv = swap_dp(send, order_a[-1])
        while outer.order or inner.order:
            advance(send)
        tokens_grad = join_rows(place, after(tokens_own, send), tokens_other)
        results = finish(after(keep, tokens_grad), recv, small, inner_bias.shape[0])
        query_grad, key_grad, value_grad, output_grad = results[:4]
        sums = list(results[4:13])
        rms = [v.reshape(()) for v in results[13:]]
    else:
        parts = [RowScatter(own_a, other_a, order_a, placed), RowScatter(own_b, other_b, order_b, placed)]
        small = small + small_other
        tokens_own = tokens_backward(first, packed, wq, wk, wv)
        tokens_grad = join_rows(place, tokens_own, swap_tensor(tokens_own))
        block_out = join_rows(place, block_own, block_other)
        for bit in bits:
            small = small + swap_dp(small, bit)
            for chain in [outer, inner] + parts:
                if chain.order:
                    chain.step()
        part_a, part_b = [part.total().reshape(D // count, -1, 2, 128) for part in parts]
        query_grad, key_grad, value_grad, output_grad = [
            v[:, :, i].reshape(-1, width) for v in (part_a, part_b) for i in range(2)
        ]
        sums = [small[i] for i in range(6)] + [small[10:12].reshape(-1), small[12, :width], small[12, width:]]
        squares = jnp.sum(small[6:9], axis=1)
        rms = jnp.sqrt(squares / ((small[9, 0] * 256.0 + small[13, 0]) * D))
    return (
        block_out,
        tokens_grad,
        query_grad,
        sums[7],
        key_grad,
        value_grad,
        sums[8],
        output_grad.T,
        sums[3],
        sums[4],
        sums[5],
        inner.total(),
        sums[6],
        outer.total().T,
        sums[2],
        sums[0],
        sums[1],
        rms[0],
        rms[1],
        rms[2],
    )


def solution(mesh):
    return jax.shard_map(
        local,
        mesh=mesh,
        in_specs=(
            P("dp", None),
            P("dp"),
            P("dp"),
            P(None, "tensor"),
            P("tensor"),
            P(None, "tensor"),
            P(None, "tensor"),
            P("tensor"),
            P("tensor", None),
            P(),
            P(),
            P(),
            P(None, "tensor"),
            P("tensor"),
            P("tensor", None),
            P(),
            P(),
            P(),
            P("dp", None),
        ),
        out_specs=(
            P("dp", None),
            P("dp", None),
            P("dp", "tensor"),
            P("tensor"),
            P("dp", "tensor"),
            P("dp", "tensor"),
            P("tensor"),
            P("tensor", "dp"),
            P(),
            P(),
            P(),
            P("dp", "tensor"),
            P("tensor"),
            P("tensor", "dp"),
            P(),
            P(),
            P(),
            P(),
            P(),
            P(),
        ),
        check_vma=False,
    )
```

```python
import jax
import jax.numpy as jnp
from jax import lax
from jax.experimental import pallas as pl
from jax.experimental.pallas import tpu as pltpu
from jax.sharding import PartitionSpec as P

D = 768
LONG = 512
SHORT = 256
eps_norm = 1e-05
bf = jnp.bfloat16
f32 = jnp.float32
shape = jax.ShapeDtypeStruct


def nt(a, b):
    return lax.dot_general(a, b, (((1,), (1,)), ((), ())), preferred_element_type=f32)


def nn(a, b):
    return lax.dot_general(a, b, (((1,), (0,)), ((), ())), preferred_element_type=f32)


def tn(a, b):
    return lax.dot_general(a, b, (((0,), (0,)), ((), ())), preferred_element_type=f32)


def whole(dims):
    return pl.BlockSpec(dims, lambda *_: (0,) * len(dims))


def anywhere():
    return pl.BlockSpec(memory_space=pl.ANY)


def settings(flops, mebibytes):
    return dict(
        compiler_params=pltpu.CompilerParams(vmem_limit_bytes=mebibytes << 20),
        cost_estimate=pl.CostEstimate(flops=int(flops), bytes_accessed=int(1e6), transcendentals=0),
    )


def line(ref):
    return ref[...].reshape(1, ref.shape[0])


def slots(rows):
    longs = rows // 2 // LONG
    shorts = rows // 2 // SHORT
    out = [(i * LONG, LONG, i) for i in range(longs)]
    return out + [(rows // 2 + i * SHORT, SHORT, longs + i) for i in range(shorts)]


def slot_length(side_ref, long_ref, short_ref, rows, index):
    longs = rows // 2 // LONG
    shorts = rows // 2 // SHORT
    if index < longs:
        return long_ref[side_ref[0] * longs + index]
    return short_ref[side_ref[0] * shorts + index - longs]


def place_rows(ref, value, places):
    if places is None:
        ref[...] = value
        return
    size = value.shape[0] // len(places)
    for i, p in enumerate(places):
        ref[p * size : (p + 1) * size, :] = value[i * size : (i + 1) * size, :]


def pair_forward(length, q, k, v, put):
    size = q.shape[0]
    lane = lax.broadcasted_iota(jnp.int32, (size, 128), 1)
    low = lane < 64
    pos = lax.broadcasted_iota(jnp.int32, (size, 128), 0)
    bias = jnp.where(pos < length, 0.0, -1e30).astype(bf)
    one = jnp.ones((), bf)
    zero = jnp.zeros((), bf)
    es = []
    for h in range(2):
        mine = low if h == 0 else ~low
        flag = lane == (64 if h == 0 else 0)
        qh = jnp.where(mine, q, jnp.where(flag, one, zero))
        kh = jnp.where(mine, k, jnp.where(flag, bias, zero))
        s = nt(qh, kh)
        m = jnp.max(s, axis=-1, keepdims=True)
        e = jnp.exp(s - m).astype(bf)
        put(h, e)
        es.append(e)
    here = jnp.where(low, one, zero)
    there = jnp.where(low, zero, one)
    both = [jnp.concatenate([v * here, here], 1), jnp.concatenate([v * there, there], 1)]
    out = nn(jnp.concatenate(es, 1), jnp.concatenate(both, 0))
    inv = 1.0 / out[:, 128:]
    return out[:, :128] * inv, inv


def attention_forward_kernel(
    side_ref, long_ref, short_ref,
    x0, x1, wq0, wq1, wk0, wk1, wv0, wv1, bias0, bias1, wo0, wo1, bo_ref, gain_ref, shift_ref,
    qkv_ref, ctx_ref, inv_ref, el_ref, es_ref, xhat_ref, dev_ref, low_ref, sums_ref, acc_ref, all_ref,
):
    step = pl.program_id(0)
    half = x0.shape[0]
    rows = 2 * half
    zero = jnp.zeros((1, 256), f32)
    cols = pl.ds(pl.multiple_of(128 * step, 128), 128)
    weights = jnp.concatenate([w[...] for w in (wq0, wq1, wk0, wk1, wv0, wv1)], 1)
    late = pl.ds(pl.multiple_of(wo0.shape[0] + 128 * step, 128), 128)
    bias = [b[at].reshape(1, 128) for at in (cols, late) for b in (bias0, bias1)]
    bias = jnp.concatenate(bias[:2] + [zero] + bias[2:], 1)
    for i, x in enumerate((x0, x1)):
        qkv_ref[i * half : (i + 1) * half, :] = (nn(x[...], weights) + bias).astype(bf)
    scale = jnp.asarray(0.125, bf)
    for first, size, index in slots(rows):
        at = pl.ds(first, size)
        length = slot_length(side_ref, long_ref, short_ref, rows, index)
        for p in range(2):
            q = qkv_ref[at, 128 * p : 128 * p + 128] * scale
            k = qkv_ref[at, 256 + 128 * p : 384 + 128 * p]
            v = qkv_ref[at, 512 + 128 * p : 640 + 128 * p]

            def put(h, e, p=p, size=size, index=index):
                if size == LONG:
                    el_ref[0, 4 * index + 2 * p + h] = e
                else:
                    es_ref[0, 4 * (index - half // LONG) + 2 * p + h] = e

            ctx, inv = pair_forward(length, q, k, v, put)
            ctx_ref[at, 128 * p : 128 * p + 128] = ctx.astype(bf)
            inv_ref[at, 128 * p : 128 * p + 128] = inv
    all_ref[:, pl.ds(pl.multiple_of(256 * step, 256), 256)] = ctx_ref[...]

    @pl.when(step == pl.num_programs(0) - 1)
    def _():
        parts = []
        for i in range(0, wo0.shape[0], 128):
            parts += [wo0[i : i + 128, :], wo1[i : i + 128, :]]
        acc_ref[...] = nn(all_ref[...], jnp.concatenate(parts, 0))
        resid = jnp.zeros((1, D), f32)
        attn = jnp.zeros((1, D), f32)
        count = jnp.zeros((), jnp.int32)
        for first, size, index in slots(rows):
            at = pl.ds(first, size)
            length = slot_length(side_ref, long_ref, short_ref, rows, index)
            count += length
            usable = lax.broadcasted_iota(jnp.int32, (size, D), 0) < length
            branch = acc_ref[at, :] + line(bo_ref)
            source = x0[at, :] if first < half else x1[first - half : first - half + size, :]
            total = source.astype(f32) + branch
            resid += jnp.sum(jnp.where(usable, total * total, 0.0), axis=0, keepdims=True)
            attn += jnp.sum(jnp.where(usable, branch * branch, 0.0), axis=0, keepdims=True)
            centred = total - jnp.mean(total, axis=-1, keepdims=True)
            dev = lax.rsqrt(jnp.mean(centred * centred, axis=-1, keepdims=True) + eps_norm)
            xhat = centred * dev
            xhat_ref[at, :] = xhat
            dev_ref[at, :] = jnp.broadcast_to(dev, (size, 128))
            low_ref[at, :] = (xhat * line(gain_ref) + line(shift_ref)).astype(bf)
        count = jnp.full((1, D), count, jnp.int32).astype(f32)
        sums_ref[...] = jnp.concatenate([resid, attn, count, jnp.zeros((5, D), f32)], 0)


def attention_forward(place, tokens, wq, wk, wv, bias, wo, bo, gain, shift):
    half = tokens.shape[0] // 4
    rows = 2 * half
    width = wq[0].shape[1]
    steps = width // 128
    longs = half // LONG
    shorts = half // SHORT
    wide = pl.BlockSpec((D, 128), lambda i, *_: (0, i))

    def part(columns):
        return pl.BlockSpec((rows, columns), lambda i, *_: (0, i))

    return pl.pallas_call(
        attention_forward_kernel,
        out_shape=(
            shape((rows, steps * 768), bf),
            shape((rows, steps * 256), bf),
            shape((rows, steps * 256), f32),
            shape((steps, 4 * longs, LONG, LONG), bf),
            shape((steps, 4 * shorts, SHORT, SHORT), bf),
            shape((rows, D), f32),
            shape((rows, 128), f32),
            shape((rows, D), bf),
            shape((8, D), f32),
        ),
        grid_spec=pltpu.PrefetchScalarGridSpec(
            num_scalar_prefetch=3,
            grid=(steps,),
            in_specs=[
                pl.BlockSpec((half, D), lambda i, side, *_: (side[0], 0)),
                pl.BlockSpec((half, D), lambda i, side, *_: (2 + side[0], 0)),
            ]
            + [wide] * 6
            + [whole(bias[0].shape)] * 2
            + [whole((width, D))] * 2
            + [whole((D,))] * 3,
            out_specs=[
                part(768),
                part(256),
                part(256),
                pl.BlockSpec((1, 4 * longs, LONG, LONG), lambda i, *_: (i, 0, 0, 0)),
                pl.BlockSpec((1, 4 * shorts, SHORT, SHORT), lambda i, *_: (i, 0, 0, 0)),
                whole((rows, D)),
                whole((rows, 128)),
                whole((rows, D)),
                whole((8, D)),
            ],
            scratch_shapes=[pltpu.VMEM((rows, D), f32), pltpu.VMEM((rows, 2 * width), bf)],
        ),
        name="attention_forward",
        **settings(40e9, 58),
    )(*place, tokens, tokens, *wq, *wk, *wv, *bias, *wo, bo, gain, shift)


def gelu_parts(v):
    cdf = 0.5 * (1.0 + lax.erf(v * 0.7071067811865476))
    return cdf, v * (0.3989422804014327 * jnp.exp(-0.5 * (v * v)))


def ffn_forward_kernel(
    side_ref, long_ref, short_ref,
    low_ref, wi0, wi1, bi0, bi1, wo0, wo1, xhat_hbm, grad_hbm, gain1_ref, shift1_ref, bo_ref, gain_ref, shift_ref,
    act0, slope0, slope1, out_hbm, back_hbm, low_hbm, other_ref, sums_ref,
    acc_ref, act1, xhat_ref, grad_ref, out_ref, back_low, in_sem, out_sem, *, chunk, places,
):
    step = pl.program_id(0)
    rows = low_ref.shape[0]
    half = rows // 2
    width = wi0.shape[1]
    fetches = [pltpu.make_async_copy(xhat_hbm, xhat_ref, in_sem.at[0])]
    for i in range(2):
        source = grad_hbm.at[pl.ds(pl.multiple_of((2 * i + side_ref[0]) * half, half), half), :]
        fetches.append(pltpu.make_async_copy(source, grad_ref.at[i * half : (i + 1) * half, :], in_sem.at[1 + i]))

    @pl.when(step == 0)
    def _():
        for fetch in fetches:
            fetch.start()

    cols = pl.ds(pl.multiple_of(width * step, width), width)
    place = pl.ds(pl.multiple_of(bi0.shape[0] - act1.shape[1] + width * step, 128), width)
    win = jnp.concatenate([wi0[...], wi1[...]], 1)
    bias = jnp.concatenate([b[place].reshape(1, width) for b in (bi0, bi1)], 1)
    wout = jnp.concatenate([wo0[...], wo1[...]], 0)
    for first in range(0, rows, chunk):
        at = pl.ds(first, chunk)
        inner = nn(low_ref[at, :], win) + bias
        cdf, bell = gelu_parts(inner)
        active = (inner * cdf).astype(bf)
        slope = (cdf + bell).astype(bf)
        act0[at, :] = active[:, :width]
        act1[at, cols] = active[:, width:]
        slope0[at, :] = slope[:, :width]
        slope1[at, :] = slope[:, width:]
        part = nn(active, wout)

        @pl.when(step == 0)
        def _():
            acc_ref[at, :] = part

        @pl.when(step > 0)
        def _():
            acc_ref[at, :] += part

    @pl.when(step == pl.num_programs(0) - 1)
    def _():
        for fetch in fetches:
            fetch.wait()
        ffn_sum = jnp.zeros((1, D), f32)
        gain_sum = jnp.zeros((1, D), f32)
        shift_sum = jnp.zeros((1, D), f32)
        bias_sum = jnp.zeros((1, D), f32)
        stores = []
        for i, (first, size, index) in enumerate(slots(rows)):
            at = pl.ds(first, size)
            length = slot_length(side_ref, long_ref, short_ref, rows, index)
            usable = lax.broadcasted_iota(jnp.int32, (size, D), 0) < length
            ffn = acc_ref[at, :] + line(bo_ref)
            ffn_sum += jnp.sum(jnp.where(usable, ffn * ffn, 0.0), axis=0, keepdims=True)
            total = xhat_ref[at, :] * line(gain1_ref) + line(shift1_ref) + ffn
            centred = total - jnp.mean(total, axis=-1, keepdims=True)
            dev = lax.rsqrt(jnp.mean(centred * centred, axis=-1, keepdims=True) + eps_norm)
            xhat = centred * dev
            out_ref[at, :] = (xhat * line(gain_ref) + line(shift_ref)).astype(bf)
            cot = jnp.where(usable, grad_ref[at, :].astype(f32), 0.0)
            gain_sum += jnp.sum(cot * xhat, axis=0, keepdims=True)
            shift_sum += jnp.sum(cot, axis=0, keepdims=True)
            u = cot * line(gain_ref)
            slant = jnp.mean(u * xhat, axis=-1, keepdims=True)
            back = dev * (u - jnp.mean(u, axis=-1, keepdims=True) - xhat * slant)
            bias_sum += jnp.sum(back, axis=0, keepdims=True)
            acc_ref[at, :] = back
            back_low[at, :] = back.astype(bf)
            for j, (source, target) in enumerate(((out_ref, out_hbm), (acc_ref, back_hbm), (back_low, low_hbm))):
                store = pltpu.make_async_copy(source.at[at, :], target.at[at, :], out_sem.at[3 * i + j])
                store.start()
                stores.append(store)
        sums_ref[...] = jnp.concatenate([ffn_sum, gain_sum, shift_sum, bias_sum, jnp.zeros((4, D), f32)], 0)
        place_rows(other_ref, tn(back_low[...], act1[...]).astype(bf), places)
        for store in stores:
            store.wait()


def ffn_forward(place, low, wi, bi, wo, xhat, grad, gain1, shift1, bo, gain, shift, places, width=512, chunk=512):
    rows = low.shape[0]
    half = wi[0].shape[1]
    cols = pl.BlockSpec((D, width), lambda i, *_: (0, i))
    tall = pl.BlockSpec((width, D), lambda i, *_: (i, 0))
    act = pl.BlockSpec((rows, width), lambda i, *_: (0, i))
    row = whole((D,))
    count = len(slots(rows))
    return pl.pallas_call(
        lambda *refs: ffn_forward_kernel(*refs, chunk=chunk, places=places),
        out_shape=(shape((rows, half), bf),) * 3
        + (shape((rows, D), bf), shape((rows, D), f32), shape((rows, D), bf), shape((D, half), bf), shape((8, D), f32)),
        grid_spec=pltpu.PrefetchScalarGridSpec(
            num_scalar_prefetch=3,
            grid=(half // width,),
            in_specs=[whole((rows, D)), cols, cols, whole(bi[0].shape), whole(bi[1].shape), tall, tall, anywhere(), anywhere()] + [row] * 5,
            out_specs=[act] * 3 + [anywhere()] * 3 + [whole((D, half)), whole((8, D))],
            scratch_shapes=[
                pltpu.VMEM((rows, D), f32),
                pltpu.VMEM((rows, half), bf),
                pltpu.VMEM((rows, D), f32),
                pltpu.VMEM((rows, D), bf),
                pltpu.VMEM((rows, D), bf),
                pltpu.VMEM((rows, D), bf),
                pltpu.SemaphoreType.DMA((3,)),
                pltpu.SemaphoreType.DMA((3 * count,)),
            ],
        ),
        name="ffn_forward",
        **settings(40e9, 58),
    )(*place, low, *wi, *bi, *wo, xhat, grad, gain1, shift1, bo, gain, shift)


def outer_weight_kernel(low_ref, act_ref, out_ref, *, places):
    place_rows(out_ref, tn(low_ref[...], act_ref[...]).astype(bf), places)


def outer_weight(low, act, places, width=512):
    rows, half = act.shape
    return pl.pallas_call(
        lambda *refs: outer_weight_kernel(*refs, places=places),
        out_shape=shape((D, half), bf),
        grid=(half // width,),
        in_specs=[whole((rows, D)), pl.BlockSpec((rows, width), lambda i: (0, i))],
        out_specs=pl.BlockSpec((D, width), lambda i: (0, i)),
        name="outer_weight",
        **settings(10e9, 8),
    )(low, act)


def ffn_backward_kernel(
    back_low, slope0, slope1, wo0, wo1, wi0, wi1, low_ref, back_hbm, xhat_hbm, dev_ref, gain_ref,
    own_ref, other_ref, bias0, bias1, first_hbm, low_hbm, sums_ref,
    inner_ref, acc_ref, xhat_ref, first_low, in_sem, out_sem, *, chunk, places,
):
    step = pl.program_id(0)
    rows = low_ref.shape[0]
    half = wi0.shape[1]
    fetches = [
        pltpu.make_async_copy(back_hbm, acc_ref, in_sem.at[0]),
        pltpu.make_async_copy(xhat_hbm, xhat_ref, in_sem.at[1]),
    ]

    @pl.when(step == 0)
    def _():
        for fetch in fetches:
            fetch.start()

    wout = jnp.concatenate([wo0[...], wo1[...]], 0)
    win = jnp.concatenate([wi0[...], wi1[...]], 1)
    total = jnp.zeros((1, 2 * half), f32)
    for first in range(0, rows, chunk):
        at = pl.ds(first, chunk)
        slope = jnp.concatenate([slope0[at, :], slope1[at, :]], 1).astype(f32)
        inner = (nt(back_low[at, :], wout) * slope).astype(bf)
        total += jnp.sum(inner.astype(f32), axis=0, keepdims=True)
        inner_ref[at, :] = inner
    bias0[...] = jnp.broadcast_to(total[:, :half], bias0.shape)
    bias1[...] = jnp.broadcast_to(total[:, half:], bias1.shape)
    place_rows(own_ref, tn(low_ref[...], inner_ref[:, :half]).astype(bf), places)
    place_rows(other_ref, tn(low_ref[...], inner_ref[:, half:]).astype(bf), places)

    @pl.when(step == 0)
    def _():
        for fetch in fetches:
            fetch.wait()

    for first in range(0, rows, chunk):
        at = pl.ds(first, chunk)
        acc_ref[at, :] += nt(inner_ref[at, :], win)

    @pl.when(step == pl.num_programs(0) - 1)
    def _():
        gain_sum = jnp.zeros((1, D), f32)
        shift_sum = jnp.zeros((1, D), f32)
        bias_sum = jnp.zeros((1, D), f32)
        stores = []
        for i, first in enumerate(range(0, rows, chunk)):
            at = pl.ds(first, chunk)
            grad = acc_ref[at, :]
            xhat = xhat_ref[at, :]
            gain_sum += jnp.sum(grad * xhat, axis=0, keepdims=True)
            shift_sum += jnp.sum(grad, axis=0, keepdims=True)
            u = grad * line(gain_ref)
            slant = jnp.mean(u * xhat, axis=-1, keepdims=True)
            out = dev_ref[at, 0:1] * (u - jnp.mean(u, axis=-1, keepdims=True) - xhat * slant)
            bias_sum += jnp.sum(out, axis=0, keepdims=True)
            acc_ref[at, :] = out
            first_low[at, :] = out.astype(bf)
            for j, (source, target) in enumerate(((acc_ref, first_hbm), (first_low, low_hbm))):
                store = pltpu.make_async_copy(source.at[at, :], target.at[at, :], out_sem.at[2 * i + j])
                store.start()
                stores.append(store)
        sums_ref[...] = jnp.concatenate([bias_sum, gain_sum, shift_sum, jnp.zeros((5, D), f32)], 0)
        for store in stores:
            store.wait()


def ffn_backward(back_low, slope, wo, wi, low, back, xhat, dev, gain, places, width=512, chunk=512):
    rows = low.shape[0]
    half = wi[0].shape[1]
    cols = pl.BlockSpec((D, width), lambda i: (0, i))
    tall = pl.BlockSpec((width, D), lambda i: (i, 0))
    act = pl.BlockSpec((rows, width), lambda i: (0, i))
    bias = pl.BlockSpec((8, width), lambda i: (0, i))
    full = whole((rows, D))
    return pl.pallas_call(
        lambda *refs: ffn_backward_kernel(*refs, chunk=chunk, places=places),
        out_shape=(shape((D, half), bf),) * 2
        + (shape((8, half), f32),) * 2
        + (shape((rows, D), f32), shape((rows, D), bf), shape((8, D), f32)),
        grid=(half // width,),
        in_specs=[full, act, act, tall, tall, cols, cols, full, anywhere(), anywhere(), whole((rows, 128)), whole((D,))],
        out_specs=[cols] * 2 + [bias] * 2 + [anywhere()] * 2 + [whole((8, D))],
        scratch_shapes=[
            pltpu.VMEM((rows, 2 * width), bf),
            pltpu.VMEM((rows, D), f32),
            pltpu.VMEM((rows, D), f32),
            pltpu.VMEM((rows, D), bf),
            pltpu.SemaphoreType.DMA((2,)),
            pltpu.SemaphoreType.DMA((2 * (rows // chunk),)),
        ],
        name="ffn_backward",
        **settings(40e9, 58),
    )(back_low, *slope, *wo, *wi, low, back, xhat, dev, gain)


def pair_backward(q, k, v, ctx, inv, grad, es):
    size = q.shape[0]
    lane = lax.broadcasted_iota(jnp.int32, (size, 128), 1)
    low = lane < 64
    one = jnp.ones((), bf)
    zero = jnp.zeros((), bf)
    grad = grad * inv
    prod = grad * ctx.astype(f32)
    grad = grad.astype(bf)
    dss = []
    for h in range(2):
        mine = low if h == 0 else ~low
        base = 64 if h == 0 else 0
        delta = -jnp.sum(jnp.where(mine, prod, 0.0), axis=-1, keepdims=True)
        high = delta.astype(bf)
        rest = (delta - high.astype(f32)).astype(bf)
        gh = jnp.where(mine, grad, jnp.where(lane == base, high, jnp.where(lane == base + 1, rest, zero)))
        dp = nt(gh, jnp.where(mine, v, one))
        dss.append((es[h].astype(f32) * dp).astype(bf))
    dq = jnp.where(low, nn(dss[0], k), nn(dss[1], k))
    q_t = q.T
    g_t = grad.T
    dk = jnp.concatenate([nn(q_t[:64], dss[0]), nn(q_t[64:], dss[1])], 0).T
    dv = jnp.concatenate([nn(g_t[:64], es[0]), nn(g_t[64:], es[1])], 0).T
    return dq.astype(bf), dk.astype(bf), dv.astype(bf)


def attention_backward_kernel(
    side_ref, x0, x1, low_ref, qkv_ref, ctx_ref, inv_ref, el_ref, es_ref, wo0, wo1, sums_a, sums_b, sums_c, bias0, bias1,
    out_ref, own_a, own_b, other_a, other_b, small0, small1, grad_ref, *, places_a, places_b,
):
    step = pl.program_id(0)
    half = x0.shape[0]
    rows = 2 * half
    scale = jnp.asarray(0.125, bf)
    low = low_ref[...]
    grad_ref[...] = nt(low, jnp.concatenate([wo0[...], wo1[...]], 0)).astype(bf)
    for first, size, index in slots(rows):
        at = pl.ds(first, size)
        for p in range(2):
            cols = [slice(256 * i + 128 * p, 256 * i + 128 * p + 128) for i in range(3)]
            q = qkv_ref[at, cols[0]] * scale
            k = qkv_ref[at, cols[1]] * scale
            v = qkv_ref[at, cols[2]]
            if size == LONG:
                es = [el_ref[0, 4 * index + 2 * p + h] for h in range(2)]
            else:
                es = [es_ref[0, 4 * (index - half // LONG) + 2 * p + h] for h in range(2)]
            grads = pair_backward(q, k, v, ctx_ref[at, cols[0]], inv_ref[at, cols[0]], grad_ref[at, cols[0]].astype(f32), es)
            for i in range(3):
                out_ref[at, cols[i]] = grads[i]
    packed = out_ref[...]
    wide = (tn(x0[...], packed[:half]) + tn(x1[...], packed[half:])).astype(bf)
    tail = tn(low, ctx_ref[...]).astype(bf)
    for side, (ref_a, ref_b) in enumerate(((own_a, own_b), (other_a, other_b))):
        pieces = [wide[:, 256 * i + 128 * side : 256 * i + 128 * side + 128] for i in range(3)]
        pieces.append(tail[:, 128 * side : 128 * side + 128])
        place_rows(ref_a, jnp.concatenate(pieces[:2], 1), places_a)
        place_rows(ref_b, jnp.concatenate(pieces[2:], 1), places_b)

    @pl.when(step == 0)
    def _():
        for ref, bias in ((small0, bias0), (small1, bias1)):
            ref[0:3, :] = sums_b[1:4, :]
            ref[3:6, :] = sums_c[0:3, :]
            ref[6:8, :] = sums_a[0:2, :]
            ref[8:9, :] = sums_b[0:1, :]
            high = jnp.floor(sums_a[2:3, :] * (1.0 / 256.0))
            ref[9:10, :] = high
            for i in range(bias.shape[1] // D):
                ref[10 + i : 11 + i, :] = bias[0:1, D * i : D * i + D]
            ref[12:16, :] = jnp.zeros((4, D), f32)
            ref[13:14, :] = sums_a[2:3, :] - 256.0 * high

    sums = jnp.sum(packed.astype(f32), axis=0, keepdims=True)
    for side, ref in enumerate((small0, small1)):
        for i in range(2):
            start = pl.multiple_of(i * (D // 2) + 128 * step, 128)
            ref[12:13, pl.ds(start, 128)] = sums[:, 512 * i + 128 * side : 512 * i + 128 * side + 128]


def attention_backward(place, tokens, low, qkv, ctx, inv, e_long, e_short, wo, sums, bias, places_a, places_b):
    half = tokens.shape[0] // 4
    rows = 2 * half
    steps = ctx.shape[1] // 256
    tall = pl.BlockSpec((128, D), lambda i, *_: (i, 0))

    def part(height, width):
        return pl.BlockSpec((height, width), lambda i, *_: (0, i))

    return pl.pallas_call(
        lambda *refs: attention_backward_kernel(*refs, places_a=places_a, places_b=places_b),
        out_shape=(shape((rows, 768 * steps), bf),) + (shape((D, 256 * steps), bf),) * 4 + (shape((16, D), f32),) * 2,
        grid_spec=pltpu.PrefetchScalarGridSpec(
            num_scalar_prefetch=1,
            grid=(steps,),
            in_specs=[
                pl.BlockSpec((half, D), lambda i, side, *_: (side[0], 0)),
                pl.BlockSpec((half, D), lambda i, side, *_: (2 + side[0], 0)),
                whole((rows, D)),
                part(rows, 768),
                part(rows, 256),
                part(rows, 256),
                pl.BlockSpec((1,) + e_long.shape[1:], lambda i, *_: (i, 0, 0, 0)),
                pl.BlockSpec((1,) + e_short.shape[1:], lambda i, *_: (i, 0, 0, 0)),
                tall,
                tall,
            ]
            + [whole((8, D))] * 3
            + [whole(bias[0].shape)] * 2,
            out_specs=[part(rows, 768)] + [part(D, 256)] * 4 + [whole((16, D))] * 2,
            scratch_shapes=[pltpu.VMEM((rows, 256), bf)],
        ),
        name="attention_backward",
        **settings(1e6, 58),
    )(place[0], tokens, tokens, low, qkv, ctx, inv, e_long, e_short, *wo, *sums, *bias)


def tokens_backward_kernel(first_ref, packed_ref, wq0, wq1, wk0, wk1, wv0, wv1, out_ref):
    total = first_ref[...]
    for i in range(packed_ref.shape[1] // 768):
        weights = jnp.concatenate([w[:, 128 * i : 128 * i + 128] for w in (wq0, wq1, wk0, wk1, wv0, wv1)], 1)
        total += nt(packed_ref[:, 768 * i : 768 * i + 768], weights)
    out_ref[...] = total.astype(bf)


def tokens_backward(first, packed, wq, wk, wv):
    rows = first.shape[0]
    chunk = 512
    return pl.pallas_call(
        tokens_backward_kernel,
        out_shape=shape((rows, D), bf),
        grid=(rows // chunk,),
        in_specs=[pl.BlockSpec((chunk, D), lambda i: (i, 0)), pl.BlockSpec((chunk, packed.shape[1]), lambda i: (i, 0))]
        + [whole(wq[0].shape)] * 6,
        out_specs=pl.BlockSpec((chunk, D), lambda i: (i, 0)),
        name="tokens_backward",
        **settings(1e6, 16),
    )(first, packed, *wq, *wk, *wv)


def join_kernel(side_ref, own_ref, other_ref, out_ref, buffer_ref, in_sems, out_sems):
    half = own_ref.shape[0] // 2
    fetches = []
    stores = []
    for i, ref in enumerate((own_ref, other_ref)):
        for j in range(2):
            n = 2 * i + j
            block = 2 * j + (side_ref[0] if i == 0 else 1 - side_ref[0])
            target = out_ref.at[pl.ds(pl.multiple_of(block * half, half), half), :]
            place = buffer_ref.at[n * half : (n + 1) * half, :]
            fetches.append(pltpu.make_async_copy(ref.at[j * half : (j + 1) * half, :], place, in_sems.at[n]))
            stores.append(pltpu.make_async_copy(place, target, out_sems.at[n]))
    for fetch in fetches:
        fetch.start()
    for fetch, store in zip(fetches, stores):
        fetch.wait()
        store.start()
    for store in stores:
        store.wait()


def join_rows(place, own, other):
    return pl.pallas_call(
        join_kernel,
        out_shape=shape((2 * own.shape[0], D), own.dtype),
        grid_spec=pltpu.PrefetchScalarGridSpec(
            num_scalar_prefetch=1,
            grid=(1,),
            in_specs=[anywhere(), anywhere()],
            out_specs=anywhere(),
            scratch_shapes=[
                pltpu.VMEM((2 * own.shape[0], D), own.dtype),
                pltpu.SemaphoreType.DMA((4,)),
                pltpu.SemaphoreType.DMA((4,)),
            ],
        ),
        name="join_rows",
        **settings(1e6, 4),
    )(place[0], own, other)


def exchange_kernel(mine_ref, *refs, chains, small, count, merge, step):
    ins, outs = (refs[:count], refs[count:])
    if small is not None:
        kept, source, first = small
        arrived = ins[source][...] if first is None else ins[source][first : first + 16, :].astype(f32)
        sums = ins[kept][...] + arrived
        sums = sums.astype(bf)
        outs[-1][...] = sums.astype(f32)
    base = 0
    for i, (keep, k0, recv, r0, rows) in enumerate(chains):
        half = rows // 2
        send_ref, keep_ref = (outs[0], outs[1]) if merge else (outs[2 * i], outs[2 * i + 1])
        for ref, side in ((send_ref, 1 - mine_ref[2 * step + i]), (keep_ref, mine_ref[2 * step + i])):
            at = side * half
            mine = ins[keep][pl.ds(pl.multiple_of(k0 + at, 16), half), :].astype(f32)
            sent = ins[recv][pl.ds(pl.multiple_of(r0 + at, 16), half), :].astype(f32)
            ref[base : base + half, :] = (mine + sent).astype(bf)
        end = base + half
        base = end if merge else 0
        if small is not None and i == (len(chains) - 1 if merge else 0):
            send_ref[end : end + 16, :] = sums


def exchange(mine, arrays, chains, small, merge, step):
    columns = arrays[0].shape[1]
    halves = [chain[4] // 2 for chain in chains]
    extra = 0 if small is None else 16
    if merge:
        outs = [shape((sum(halves) + extra, columns), bf), shape((sum(halves), columns), bf)]
    else:
        outs = []
        for i, half in enumerate(halves):
            kind = shape
            outs += [kind((half + (extra if i == 0 else 0), columns), bf), kind((half, columns), bf)]
    if small is not None:
        outs.append(shape((16, D), f32))
    return pl.pallas_call(
        lambda *refs: exchange_kernel(
            *refs, chains=chains, small=small, count=len(arrays), merge=merge, step=step
        ),
        out_shape=tuple(outs),
        grid_spec=pltpu.PrefetchScalarGridSpec(
            num_scalar_prefetch=1,
            grid=(1,),
            in_specs=[whole(v.shape) for v in arrays],
            out_specs=[whole(v.shape) for v in outs],
        ),
        name="exchange",
        **settings(1e6, 8),
    )(mine, *arrays)


def finish_kernel(keep_ref, recv_ref, small_in, *outs):
    rows = keep_ref.shape[0]
    total = keep_ref[...].astype(f32) + recv_ref[0:rows, :].astype(f32)
    for n, ref in enumerate(outs[:4]):
        part = total[(n // 2) * (rows // 2) : (n // 2 + 1) * (rows // 2)]
        for j in range(total.shape[1] // 256):
            ref[:, 128 * j : 128 * j + 128] = part[:, 256 * j + 128 * (n % 2) : 256 * j + 128 * (n % 2) + 128]
    small = small_in[...] + recv_ref[rows : rows + 16, :].astype(f32)
    for n in range(6):
        outs[4 + n][...] = small[n].reshape(D)
    inner_ref, query_ref, value_ref = outs[10:13]
    for i in range(inner_ref.shape[0] // D):
        inner_ref[D * i : D * i + D] = small[10 + i].reshape(D)
    half = query_ref.shape[0]
    query_ref[...] = small[12:13, :half].reshape(half)
    value_ref[...] = small[12:13, half:].reshape(half)
    count = small[9:10, 0:1] * 256.0 + small[13:14, 0:1]
    for n in range(3):
        outs[13 + n][...] = jnp.sqrt(jnp.sum(small[6 + n : 7 + n], axis=1, keepdims=True) / (count * D))


def finish(keep, recv, small, units):
    rows, columns = keep.shape
    half = columns // 2
    outs = [shape((rows // 2, half), f32)] * 4 + [shape((D,), f32)] * 6
    outs += [shape((units,), f32), shape((half,), f32), shape((half,), f32)] + [shape((1, 1), f32)] * 3
    return pl.pallas_call(
        finish_kernel,
        out_shape=tuple(outs),
        grid=(1,),
        in_specs=[whole(v.shape) for v in (keep, recv, small)],
        out_specs=[whole(v.shape) for v in outs],
        name="finish",
        **settings(1e6, 2),
    )(keep, recv, small)


def swap_tensor(value):
    return lax.ppermute(value, "tensor", [(0, 1), (1, 0)])


def dp_bits():
    count = lax.axis_size("dp")
    bits = []
    while (1 << len(bits)) < count:
        bits.append(1 << len(bits))
    return count, bits


def swap_dp(value, bit):
    count, _ = dp_bits()
    return lax.ppermute(value, "dp", [(i, i ^ bit) for i in range(count)])


def after(value, *others):
    return lax.optimization_barrier((value,) + others)[0]


def places_of(order):
    count, bits = dp_bits()
    out = []
    for i in range(count):
        position = 0
        for bit in order:
            position = 2 * position + (i // bit) % 2
        out.append(position)
    return out


def sorted_rows(value, places):
    size = value.shape[0] // len(places)
    source = [places.index(p) for p in range(len(places))]
    return jnp.concatenate([value[i * size : (i + 1) * size] for i in source], 0)


class RowScatter:
    def __init__(self, own, other, order, placed):
        if not placed:
            own, other = [sorted_rows(v, places_of(order)) for v in (own, other)]
        self.pair, self.order = ((own, other), list(order))
        self.split()

    def pick(self, side):
        size = self.pair[0].shape[0] // 2
        a, b = [lax.dynamic_slice_in_dim(v, side * size, size, 0).astype(f32) for v in self.pair]
        return (a + b).astype(bf)

    def resume(self, keep, recv, used):
        self.pair, self.order = ((keep, recv), self.order[used:])
        self.split()

    def split(self):
        mine = (lax.axis_index("dp") // self.order[0]) % 2
        self.send, self.keep = (self.pick(1 - mine), self.pick(mine))

    def step(self, *gates):
        keep = after(self.keep, *gates) if gates else self.keep
        self.pair = (keep, swap_dp(self.send, self.order[0]))
        self.order = self.order[1:]
        if self.order:
            self.split()

    def total(self):
        return self.pair[0].astype(f32) + self.pair[1].astype(f32)

    def ready(self):
        return self.send if self.order else self.pair[1]


def local(
    tokens,
    long_lengths,
    short_lengths,
    query_weight,
    query_bias,
    key_weight,
    value_weight,
    value_bias,
    output_weight,
    output_bias,
    first_gain,
    first_shift,
    inner_weight,
    inner_bias,
    outer_weight_here,
    outer_bias,
    second_gain,
    second_shift,
    out_grad,
):
    count, bits = dp_bits()
    order_a, order_b = (bits, bits[1::-1] + bits[2:])
    order_o = bits
    order_i = bits[:1] + bits[2:3] + bits[1:2] + bits[3:]
    placed = D % (16 * count) == 0
    places_a, places_b, places_o, places_i = [
        places_of(order) if placed else None for order in (order_a, order_b, order_o, order_i)
    ]
    width = query_weight.shape[1]
    place = (lax.axis_index("tensor").reshape(1), long_lengths, short_lengths)
    mine = (lax.axis_index("dp") // jnp.array([v for pair in zip(order_a, order_b) for v in pair], jnp.int32)) % 2
    bias, wq, wk, wv, wo, wi, w2 = [
        (v, swap_tensor(v))
        for v in (
            jnp.concatenate([query_bias, value_bias, inner_bias]),
            query_weight,
            key_weight,
            value_weight,
            output_weight,
            inner_weight,
            outer_weight_here,
        )
    ]
    qkv, ctx, inv, e_long, e_short, xhat, dev, low, sums_a = attention_forward(
        place, tokens, wq, wk, wv, bias, wo, output_bias, first_gain, first_shift
    )
    act, slope0, slope1, block_own, back, back_low, outer_other, sums_b = ffn_forward(
        place, low, wi, bias, w2, xhat, out_grad, first_gain, first_shift, outer_bias, second_gain, second_shift, places_o
    )
    outer_other = swap_tensor(outer_other)
    outer = RowScatter(outer_weight(back_low, act, places_o), outer_other, order_o, placed)
    block_other = swap_tensor(block_own)
    back_low = after(back_low, outer.send, block_other)
    inner_own, inner_other, bias0, bias1, first, first_low, sums_c = ffn_backward(
        back_low, (slope0, slope1), w2, wi, low, back, xhat, dev, first_gain, places_i
    )
    outer.step(sums_c)
    inner_own, inner_other, first_low, first = lax.optimization_barrier(
        (inner_own, inner_other, first_low, first, outer.send)
    )[:4]
    inner = RowScatter(inner_own, swap_tensor(inner_other), order_i, placed)
    first_low = after(first_low, inner.send)
    packed, own_a, own_b, other_a, other_b, small, small_other = attention_backward(
        place, tokens, first_low, qkv, ctx, inv, e_long, e_short, wo, (sums_a, sums_b, sums_c), (bias0, bias1), places_a, places_b
    )
    outer.step(small)
    other_a, other_b, small_other = [swap_tensor(after(v, outer.pair[1])) for v in (other_a, other_b, small_other)]
    inner.step(small)
    own_a, own_b, packed, small, block_own = lax.optimization_barrier(
        (own_a, own_b, packed, small, block_own, outer.pair[1], inner.pair[1])
    )[:5]

    def advance(*gates):
        for chain in (outer, inner):
            if chain.order:
                chain.step(*gates)

    if placed:
        rows = outer.pair[0].shape[0]
        chains = [(0, 0, 1, 0, rows), (2, 0, 3, 0, 2 * rows)]
        send_o, keep_o, send_i, keep_i = exchange(mine, (*outer.pair, *inner.pair), chains, None, False, 2)
        recv_o = swap_dp(send_o, order_o[2])
        own_a = after(own_a, send_o)
        chains = [(0, 0, 1, 0, D), (2, 0, 3, 0, D)]
        send_a, keep_a, send_b, keep_b, small = exchange(mine, (own_a, other_a, own_b, other_b, small, small_other), chains, (4, 5, None), False, 0)
        block_out = join_rows(place, after(block_own, send_a), block_other)
        recv_i = swap_dp(after(send_i, send_a, recv_o), order_i[1])
        outer.resume(after(keep_o, block_out), recv_o, 1)
        packed = after(packed, send_a, block_out, outer.send)
        tokens_own = tokens_backward(first, packed, wq, wk, wv)
        recv_a, recv_b = (swap_dp(send_a, order_a[0]), swap_dp(send_b, order_b[0]))
        keep_a = after(keep_a, tokens_own)
        rows = D // 2
        chains = [(0, 0, 1, 0, rows), (2, 0, 3, 0, rows)]
        send_a, keep_a, send_b, keep_b, small = exchange(mine, (keep_a, recv_a, keep_b, recv_b, small), chains, (4, 1, rows), False, 1)
        tokens_own = after(tokens_own, send_a)
        tokens_other = swap_tensor(tokens_own)
        recv_a, recv_b = (swap_dp(send_a, order_a[1]), swap_dp(send_b, order_b[1]))
        inner.resume(after(keep_i, send_a), recv_i, 1)
        rows = D // 4
        chains = [(0, 0, 1, 0, rows), (2, 0, 3, 0, rows)]
        send, keep, small = exchange(mine, (keep_a, recv_a, keep_b, recv_b, small), chains, (4, 1, rows), True, 2)
        for step in range(2, len(bits) - 1):
            recv = swap_dp(send, order_a[step])
            advance(send)
            rows = keep.shape[0] // 2
            chains = [(0, 0, 1, 0, rows), (0, rows, 1, rows, rows)]
            send, keep, small = exchange(mine, (keep, recv, small), chains, (2, 1, 2 * rows), True, step + 1)
        recv = swap_dp(send, order_a[-1])
        while outer.order or inner.order:
            advance(send)
        tokens_grad = join_rows(place, after(tokens_own, send), tokens_other)
        results = finish(after(keep, tokens_grad), recv, small, inner_bias.shape[0])
        query_grad, key_grad, value_grad, output_grad = results[:4]
        sums = list(results[4:13])
        rms = [v.reshape(()) for v in results[13:]]
    else:
        parts = [RowScatter(own_a, other_a, order_a, placed), RowScatter(own_b, other_b, order_b, placed)]
        small = small + small_other
        tokens_own = tokens_backward(first, packed, wq, wk, wv)
        tokens_grad = join_rows(place, tokens_own, swap_tensor(tokens_own))
        block_out = join_rows(place, block_own, block_other)
        for bit in bits:
            small = small + swap_dp(small, bit)
            for chain in [outer, inner] + parts:
                if chain.order:
                    chain.step()
        part_a, part_b = [part.total().reshape(D // count, -1, 2, 128) for part in parts]
        query_grad, key_grad, value_grad, output_grad = [
            v[:, :, i].reshape(-1, width) for v in (part_a, part_b) for i in range(2)
        ]
        sums = [small[i] for i in range(6)] + [small[10:12].reshape(-1), small[12, :width], small[12, width:]]
        squares = jnp.sum(small[6:9], axis=1)
        rms = jnp.sqrt(squares / ((small[9, 0] * 256.0 + small[13, 0]) * D))
    return (
        block_out,
        tokens_grad,
        query_grad,
        sums[7],
        key_grad,
        value_grad,
        sums[8],
        output_grad.T,
        sums[3],
        sums[4],
        sums[5],
        inner.total(),
        sums[6],
        outer.total().T,
        sums[2],
        sums[0],
        sums[1],
        rms[0],
        rms[1],
        rms[2],
    )


def solution(mesh):
    return jax.shard_map(
        local,
        mesh=mesh,
        in_specs=(
            P("dp", None),
            P("dp"),
            P("dp"),
            P(None, "tensor"),
            P("tensor"),
            P(None, "tensor"),
            P(None, "tensor"),
            P("tensor"),
            P("tensor", None),
            P(),
            P(),
            P(),
            P(None, "tensor"),
            P("tensor"),
            P("tensor", None),
            P(),
            P(),
            P(),
            P("dp", None),
        ),
        out_specs=(
            P("dp", None),
            P("dp", None),
            P("dp", "tensor"),
            P("tensor"),
            P("dp", "tensor"),
            P("dp", "tensor"),
            P("tensor"),
            P("tensor", "dp"),
            P(),
            P(),
            P(),
            P("dp", "tensor"),
            P("tensor"),
            P("tensor", "dp"),
            P(),
            P(),
            P(),
            P(),
            P(),
            P(),
        ),
        check_vma=False,
    )
```

```python
import jax
import jax.numpy as jnp
from jax import lax
from jax.experimental import pallas as pl
from jax.experimental.pallas import tpu as pltpu
from jax.sharding import PartitionSpec as P

D = 768
LONG = 512
SHORT = 256
eps_norm = 1e-05
bf = jnp.bfloat16
f32 = jnp.float32
shape = jax.ShapeDtypeStruct


def nt(a, b):
    return lax.dot_general(a, b, (((1,), (1,)), ((), ())), preferred_element_type=f32)


def nn(a, b):
    return lax.dot_general(a, b, (((1,), (0,)), ((), ())), preferred_element_type=f32)


def tn(a, b):
    return lax.dot_general(a, b, (((0,), (0,)), ((), ())), preferred_element_type=f32)


def whole(dims):
    return pl.BlockSpec(dims, lambda *_: (0,) * len(dims))


def anywhere():
    return pl.BlockSpec(memory_space=pl.ANY)


def settings(flops, mebibytes):
    return dict(
        compiler_params=pltpu.CompilerParams(vmem_limit_bytes=mebibytes << 20),
        cost_estimate=pl.CostEstimate(flops=int(flops), bytes_accessed=int(1e6), transcendentals=0),
    )


def line(ref):
    return ref[...].reshape(1, ref.shape[0])


def slots(rows):
    longs = rows // 2 // LONG
    shorts = rows // 2 // SHORT
    out = [(i * LONG, LONG, i) for i in range(longs)]
    return out + [(rows // 2 + i * SHORT, SHORT, longs + i) for i in range(shorts)]


def slot_length(side_ref, long_ref, short_ref, rows, index):
    longs = rows // 2 // LONG
    shorts = rows // 2 // SHORT
    if index < longs:
        return long_ref[side_ref[0] * longs + index]
    return short_ref[side_ref[0] * shorts + index - longs]


def place_rows(ref, value, places):
    if places is None:
        ref[...] = value
        return
    size = value.shape[0] // len(places)
    for i, p in enumerate(places):
        ref[p * size : (p + 1) * size, :] = value[i * size : (i + 1) * size, :]


def pair_forward(length, q, k, v, put):
    size = q.shape[0]
    lane = lax.broadcasted_iota(jnp.int32, (size, 128), 1)
    low = lane < 64
    pos = lax.broadcasted_iota(jnp.int32, (size, 128), 0)
    bias = jnp.where(pos < length, 0.0, -1e30).astype(bf)
    one = jnp.ones((), bf)
    zero = jnp.zeros((), bf)
    es = []
    for h in range(2):
        mine = low if h == 0 else ~low
        flag = lane == (64 if h == 0 else 0)
        qh = jnp.where(mine, q, jnp.where(flag, one, zero))
        kh = jnp.where(mine, k, jnp.where(flag, bias, zero))
        s = nt(qh, kh)
        m = jnp.max(s, axis=-1, keepdims=True)
        e = jnp.exp(s - m).astype(bf)
        put(h, e)
        es.append(e)
    here = jnp.where(low, one, zero)
    there = jnp.where(low, zero, one)
    both = [jnp.concatenate([v * here, here], 1), jnp.concatenate([v * there, there], 1)]
    out = nn(jnp.concatenate(es, 1), jnp.concatenate(both, 0))
    inv = 1.0 / out[:, 128:]
    return out[:, :128] * inv, inv


def attention_forward_kernel(
    side_ref, long_ref, short_ref,
    x0, x1, wq0, wq1, wk0, wk1, wv0, wv1, bias0, bias1, wo0, wo1, bo_ref, gain_ref, shift_ref,
    qkv_ref, ctx_ref, inv_ref, el_ref, es_ref, xhat_ref, dev_ref, low_ref, sums_ref, acc_ref, all_ref,
):
    step = pl.program_id(0)
    half = x0.shape[0]
    rows = 2 * half
    zero = jnp.zeros((1, 256), f32)
    cols = pl.ds(pl.multiple_of(128 * step, 128), 128)
    weights = jnp.concatenate([w[...] for w in (wq0, wq1, wk0, wk1, wv0, wv1)], 1)
    late = pl.ds(pl.multiple_of(wo0.shape[0] + 128 * step, 128), 128)
    bias = [b[at].reshape(1, 128) for at in (cols, late) for b in (bias0, bias1)]
    bias = jnp.concatenate(bias[:2] + [zero] + bias[2:], 1)
    for i, x in enumerate((x0, x1)):
        qkv_ref[i * half : (i + 1) * half, :] = (nn(x[...], weights) + bias).astype(bf)
    scale = jnp.asarray(0.125, bf)
    for first, size, index in slots(rows):
        at = pl.ds(first, size)
        length = slot_length(side_ref, long_ref, short_ref, rows, index)
        for p in range(2):
            q = qkv_ref[at, 128 * p : 128 * p + 128] * scale
            k = qkv_ref[at, 256 + 128 * p : 384 + 128 * p]
            v = qkv_ref[at, 512 + 128 * p : 640 + 128 * p]

            def put(h, e, p=p, size=size, index=index):
                if size == LONG:
                    el_ref[0, 4 * index + 2 * p + h] = e
                else:
                    es_ref[0, 4 * (index - half // LONG) + 2 * p + h] = e

            ctx, inv = pair_forward(length, q, k, v, put)
            ctx_ref[at, 128 * p : 128 * p + 128] = ctx.astype(bf)
            inv_ref[at, 128 * p : 128 * p + 128] = inv
    all_ref[:, pl.ds(pl.multiple_of(256 * step, 256), 256)] = ctx_ref[...]

    @pl.when(step == pl.num_programs(0) - 1)
    def _():
        parts = []
        for i in range(0, wo0.shape[0], 128):
            parts += [wo0[i : i + 128, :], wo1[i : i + 128, :]]
        acc_ref[...] = nn(all_ref[...], jnp.concatenate(parts, 0))
        resid = jnp.zeros((1, D), f32)
        attn = jnp.zeros((1, D), f32)
        count = jnp.zeros((), jnp.int32)
        for first, size, index in slots(rows):
            at = pl.ds(first, size)
            length = slot_length(side_ref, long_ref, short_ref, rows, index)
            count += length
            usable = lax.broadcasted_iota(jnp.int32, (size, D), 0) < length
            branch = acc_ref[at, :] + line(bo_ref)
            source = x0[at, :] if first < half else x1[first - half : first - half + size, :]
            total = source.astype(f32) + branch
            resid += jnp.sum(jnp.where(usable, total * total, 0.0), axis=0, keepdims=True)
            attn += jnp.sum(jnp.where(usable, branch * branch, 0.0), axis=0, keepdims=True)
            centred = total - jnp.mean(total, axis=-1, keepdims=True)
            dev = lax.rsqrt(jnp.mean(centred * centred, axis=-1, keepdims=True) + eps_norm)
            xhat = centred * dev
            xhat_ref[at, :] = xhat
            dev_ref[at, :] = jnp.broadcast_to(dev, (size, 128))
            low_ref[at, :] = (xhat * line(gain_ref) + line(shift_ref)).astype(bf)
        count = jnp.full((1, D), count, jnp.int32).astype(f32)
        sums_ref[...] = jnp.concatenate([resid, attn, count, jnp.zeros((5, D), f32)], 0)


def attention_forward(place, tokens, wq, wk, wv, bias, wo, bo, gain, shift):
    half = tokens.shape[0] // 4
    rows = 2 * half
    width = wq[0].shape[1]
    steps = width // 128
    longs = half // LONG
    shorts = half // SHORT
    wide = pl.BlockSpec((D, 128), lambda i, *_: (0, i))

    def part(columns):
        return pl.BlockSpec((rows, columns), lambda i, *_: (0, i))

    return pl.pallas_call(
        attention_forward_kernel,
        out_shape=(
            shape((rows, steps * 768), bf),
            shape((rows, steps * 256), bf),
            shape((rows, steps * 256), f32),
            shape((steps, 4 * longs, LONG, LONG), bf),
            shape((steps, 4 * shorts, SHORT, SHORT), bf),
            shape((rows, D), f32),
            shape((rows, 128), f32),
            shape((rows, D), bf),
            shape((8, D), f32),
        ),
        grid_spec=pltpu.PrefetchScalarGridSpec(
            num_scalar_prefetch=3,
            grid=(steps,),
            in_specs=[
                pl.BlockSpec((half, D), lambda i, side, *_: (side[0], 0)),
                pl.BlockSpec((half, D), lambda i, side, *_: (2 + side[0], 0)),
            ]
            + [wide] * 6
            + [whole(bias[0].shape)] * 2
            + [whole((width, D))] * 2
            + [whole((D,))] * 3,
            out_specs=[
                part(768),
                part(256),
                part(256),
                pl.BlockSpec((1, 4 * longs, LONG, LONG), lambda i, *_: (i, 0, 0, 0)),
                pl.BlockSpec((1, 4 * shorts, SHORT, SHORT), lambda i, *_: (i, 0, 0, 0)),
                whole((rows, D)),
                whole((rows, 128)),
                whole((rows, D)),
                whole((8, D)),
            ],
            scratch_shapes=[pltpu.VMEM((rows, D), f32), pltpu.VMEM((rows, 2 * width), bf)],
        ),
        name="attention_forward",
        **settings(40e9, 58),
    )(*place, tokens, tokens, *wq, *wk, *wv, *bias, *wo, bo, gain, shift)


def gelu_parts(v):
    cdf = 0.5 * (1.0 + lax.erf(v * 0.7071067811865476))
    return cdf, v * (0.3989422804014327 * jnp.exp(-0.5 * (v * v)))


def ffn_forward_kernel(
    side_ref, long_ref, short_ref,
    low_ref, wi0, wi1, bi0, bi1, wo0, wo1, xhat_hbm, grad_hbm, gain1_ref, shift1_ref, bo_ref, gain_ref, shift_ref,
    act0, slope0, slope1, out_hbm, back_hbm, low_hbm, other_ref, sums_ref,
    acc_ref, act1, xhat_ref, grad_ref, out_ref, back_low, in_sem, out_sem, *, chunk, places,
):
    step = pl.program_id(0)
    rows = low_ref.shape[0]
    half = rows // 2
    width = wi0.shape[1]
    fetches = [pltpu.make_async_copy(xhat_hbm, xhat_ref, in_sem.at[0])]
    for i in range(2):
        source = grad_hbm.at[pl.ds(pl.multiple_of((2 * i + side_ref[0]) * half, half), half), :]
        fetches.append(pltpu.make_async_copy(source, grad_ref.at[i * half : (i + 1) * half, :], in_sem.at[1 + i]))

    @pl.when(step == 0)
    def _():
        for fetch in fetches:
            fetch.start()

    cols = pl.ds(pl.multiple_of(width * step, width), width)
    place = pl.ds(pl.multiple_of(bi0.shape[0] - act1.shape[1] + width * step, 128), width)
    win = jnp.concatenate([wi0[...], wi1[...]], 1)
    bias = jnp.concatenate([b[place].reshape(1, width) for b in (bi0, bi1)], 1)
    wout = jnp.concatenate([wo0[...], wo1[...]], 0)
    for first in range(0, rows, chunk):
        at = pl.ds(first, chunk)
        inner = nn(low_ref[at, :], win) + bias
        cdf, bell = gelu_parts(inner)
        active = (inner * cdf).astype(bf)
        slope = (cdf + bell).astype(bf)
        act0[at, :] = active[:, :width]
        act1[at, cols] = active[:, width:]
        slope0[at, :] = slope[:, :width]
        slope1[at, :] = slope[:, width:]
        part = nn(active, wout)

        @pl.when(step == 0)
        def _():
            acc_ref[at, :] = part

        @pl.when(step > 0)
        def _():
            acc_ref[at, :] += part

    @pl.when(step == pl.num_programs(0) - 1)
    def _():
        for fetch in fetches:
            fetch.wait()
        ffn_sum = jnp.zeros((1, D), f32)
        gain_sum = jnp.zeros((1, D), f32)
        shift_sum = jnp.zeros((1, D), f32)
        bias_sum = jnp.zeros((1, D), f32)
        stores = []
        for i, (first, size, index) in enumerate(slots(rows)):
            at = pl.ds(first, size)
            length = slot_length(side_ref, long_ref, short_ref, rows, index)
            usable = lax.broadcasted_iota(jnp.int32, (size, D), 0) < length
            ffn = acc_ref[at, :] + line(bo_ref)
            ffn_sum += jnp.sum(jnp.where(usable, ffn * ffn, 0.0), axis=0, keepdims=True)
            total = xhat_ref[at, :] * line(gain1_ref) + line(shift1_ref) + ffn
            centred = total - jnp.mean(total, axis=-1, keepdims=True)
            dev = lax.rsqrt(jnp.mean(centred * centred, axis=-1, keepdims=True) + eps_norm)
            xhat = centred * dev
            out_ref[at, :] = (xhat * line(gain_ref) + line(shift_ref)).astype(bf)
            cot = jnp.where(usable, grad_ref[at, :].astype(f32), 0.0)
            gain_sum += jnp.sum(cot * xhat, axis=0, keepdims=True)
            shift_sum += jnp.sum(cot, axis=0, keepdims=True)
            u = cot * line(gain_ref)
            slant = jnp.mean(u * xhat, axis=-1, keepdims=True)
            back = dev * (u - jnp.mean(u, axis=-1, keepdims=True) - xhat * slant)
            bias_sum += jnp.sum(back, axis=0, keepdims=True)
            acc_ref[at, :] = back
            back_low[at, :] = back.astype(bf)
            for j, (source, target) in enumerate(((out_ref, out_hbm), (acc_ref, back_hbm), (back_low, low_hbm))):
                store = pltpu.make_async_copy(source.at[at, :], target.at[at, :], out_sem.at[3 * i + j])
                store.start()
                stores.append(store)
        sums_ref[...] = jnp.concatenate([ffn_sum, gain_sum, shift_sum, bias_sum, jnp.zeros((4, D), f32)], 0)
        place_rows(other_ref, tn(back_low[...], act1[...]).astype(bf), places)
        for store in stores:
            store.wait()


def ffn_forward(place, low, wi, bi, wo, xhat, grad, gain1, shift1, bo, gain, shift, places, width=512, chunk=512):
    rows = low.shape[0]
    half = wi[0].shape[1]
    cols = pl.BlockSpec((D, width), lambda i, *_: (0, i))
    tall = pl.BlockSpec((width, D), lambda i, *_: (i, 0))
    act = pl.BlockSpec((rows, width), lambda i, *_: (0, i))
    row = whole((D,))
    count = len(slots(rows))
    return pl.pallas_call(
        lambda *refs: ffn_forward_kernel(*refs, chunk=chunk, places=places),
        out_shape=(shape((rows, half), bf),) * 3
        + (shape((rows, D), bf), shape((rows, D), f32), shape((rows, D), bf), shape((D, half), bf), shape((8, D), f32)),
        grid_spec=pltpu.PrefetchScalarGridSpec(
            num_scalar_prefetch=3,
            grid=(half // width,),
            in_specs=[whole((rows, D)), cols, cols, whole(bi[0].shape), whole(bi[1].shape), tall, tall, anywhere(), anywhere()] + [row] * 5,
            out_specs=[act] * 3 + [anywhere()] * 3 + [whole((D, half)), whole((8, D))],
            scratch_shapes=[
                pltpu.VMEM((rows, D), f32),
                pltpu.VMEM((rows, half), bf),
                pltpu.VMEM((rows, D), f32),
                pltpu.VMEM((rows, D), bf),
                pltpu.VMEM((rows, D), bf),
                pltpu.VMEM((rows, D), bf),
                pltpu.SemaphoreType.DMA((3,)),
                pltpu.SemaphoreType.DMA((3 * count,)),
            ],
        ),
        name="ffn_forward",
        **settings(40e9, 58),
    )(*place, low, *wi, *bi, *wo, xhat, grad, gain1, shift1, bo, gain, shift)


def outer_weight_kernel(low_ref, act_ref, out_ref, *, places):
    place_rows(out_ref, tn(low_ref[...], act_ref[...]).astype(bf), places)


def outer_weight(low, act, places, width=512):
    rows, half = act.shape
    return pl.pallas_call(
        lambda *refs: outer_weight_kernel(*refs, places=places),
        out_shape=shape((D, half), bf),
        grid=(half // width,),
        in_specs=[whole((rows, D)), pl.BlockSpec((rows, width), lambda i: (0, i))],
        out_specs=pl.BlockSpec((D, width), lambda i: (0, i)),
        name="outer_weight",
        **settings(10e9, 8),
    )(low, act)


def ffn_backward_kernel(
    back_low, slope0, slope1, wo0, wo1, wi0, wi1, low_ref, back_hbm, xhat_hbm, dev_ref, gain_ref,
    own_ref, other_ref, bias0, bias1, first_hbm, low_hbm, sums_ref,
    inner_ref, acc_ref, xhat_ref, first_low, in_sem, out_sem, *, chunk, places,
):
    step = pl.program_id(0)
    rows = low_ref.shape[0]
    half = wi0.shape[1]
    fetches = [
        pltpu.make_async_copy(back_hbm, acc_ref, in_sem.at[0]),
        pltpu.make_async_copy(xhat_hbm, xhat_ref, in_sem.at[1]),
    ]

    @pl.when(step == 0)
    def _():
        for fetch in fetches:
            fetch.start()

    wout = jnp.concatenate([wo0[...], wo1[...]], 0)
    win = jnp.concatenate([wi0[...], wi1[...]], 1)
    total = jnp.zeros((1, 2 * half), f32)
    for first in range(0, rows, chunk):
        at = pl.ds(first, chunk)
        slope = jnp.concatenate([slope0[at, :], slope1[at, :]], 1).astype(f32)
        inner = (nt(back_low[at, :], wout) * slope).astype(bf)
        total += jnp.sum(inner.astype(f32), axis=0, keepdims=True)
        inner_ref[at, :] = inner
    bias0[...] = jnp.broadcast_to(total[:, :half], bias0.shape)
    bias1[...] = jnp.broadcast_to(total[:, half:], bias1.shape)
    place_rows(own_ref, tn(low_ref[...], inner_ref[:, :half]).astype(bf), places)
    place_rows(other_ref, tn(low_ref[...], inner_ref[:, half:]).astype(bf), places)

    @pl.when(step == 0)
    def _():
        for fetch in fetches:
            fetch.wait()

    for first in range(0, rows, chunk):
        at = pl.ds(first, chunk)
        acc_ref[at, :] += nt(inner_ref[at, :], win)

    @pl.when(step == pl.num_programs(0) - 1)
    def _():
        gain_sum = jnp.zeros((1, D), f32)
        shift_sum = jnp.zeros((1, D), f32)
        bias_sum = jnp.zeros((1, D), f32)
        stores = []
        for i, first in enumerate(range(0, rows, chunk)):
            at = pl.ds(first, chunk)
            grad = acc_ref[at, :]
            xhat = xhat_ref[at, :]
            gain_sum += jnp.sum(grad * xhat, axis=0, keepdims=True)
            shift_sum += jnp.sum(grad, axis=0, keepdims=True)
            u = grad * line(gain_ref)
            slant = jnp.mean(u * xhat, axis=-1, keepdims=True)
            out = dev_ref[at, 0:1] * (u - jnp.mean(u, axis=-1, keepdims=True) - xhat * slant)
            bias_sum += jnp.sum(out, axis=0, keepdims=True)
            acc_ref[at, :] = out
            first_low[at, :] = out.astype(bf)
            for j, (source, target) in enumerate(((acc_ref, first_hbm), (first_low, low_hbm))):
                store = pltpu.make_async_copy(source.at[at, :], target.at[at, :], out_sem.at[2 * i + j])
                store.start()
                stores.append(store)
        sums_ref[...] = jnp.concatenate([bias_sum, gain_sum, shift_sum, jnp.zeros((5, D), f32)], 0)
        for store in stores:
            store.wait()


def ffn_backward(back_low, slope, wo, wi, low, back, xhat, dev, gain, places, width=512, chunk=512):
    rows = low.shape[0]
    half = wi[0].shape[1]
    cols = pl.BlockSpec((D, width), lambda i: (0, i))
    tall = pl.BlockSpec((width, D), lambda i: (i, 0))
    act = pl.BlockSpec((rows, width), lambda i: (0, i))
    bias = pl.BlockSpec((8, width), lambda i: (0, i))
    full = whole((rows, D))
    return pl.pallas_call(
        lambda *refs: ffn_backward_kernel(*refs, chunk=chunk, places=places),
        out_shape=(shape((D, half), bf),) * 2
        + (shape((8, half), f32),) * 2
        + (shape((rows, D), f32), shape((rows, D), bf), shape((8, D), f32)),
        grid=(half // width,),
        in_specs=[full, act, act, tall, tall, cols, cols, full, anywhere(), anywhere(), whole((rows, 128)), whole((D,))],
        out_specs=[cols] * 2 + [bias] * 2 + [anywhere()] * 2 + [whole((8, D))],
        scratch_shapes=[
            pltpu.VMEM((rows, 2 * width), bf),
            pltpu.VMEM((rows, D), f32),
            pltpu.VMEM((rows, D), f32),
            pltpu.VMEM((rows, D), bf),
            pltpu.SemaphoreType.DMA((2,)),
            pltpu.SemaphoreType.DMA((2 * (rows // chunk),)),
        ],
        name="ffn_backward",
        **settings(40e9, 58),
    )(back_low, *slope, *wo, *wi, low, back, xhat, dev, gain)


def pair_backward(q, k, v, ctx, inv, grad, es):
    size = q.shape[0]
    lane = lax.broadcasted_iota(jnp.int32, (size, 128), 1)
    low = lane < 64
    one = jnp.ones((), bf)
    zero = jnp.zeros((), bf)
    grad = grad * inv
    prod = grad * ctx.astype(f32)
    grad = grad.astype(bf)
    dss = []
    for h in range(2):
        mine = low if h == 0 else ~low
        base = 64 if h == 0 else 0
        delta = -jnp.sum(jnp.where(mine, prod, 0.0), axis=-1, keepdims=True)
        high = delta.astype(bf)
        rest = (delta - high.astype(f32)).astype(bf)
        gh = jnp.where(mine, grad, jnp.where(lane == base, high, jnp.where(lane == base + 1, rest, zero)))
        dp = nt(gh, jnp.where(mine, v, one))
        dss.append((es[h].astype(f32) * dp).astype(bf))
    dq = jnp.where(low, nn(dss[0], k), nn(dss[1], k))
    q_t = q.T
    g_t = grad.T
    dk = jnp.concatenate([nn(q_t[:64], dss[0]), nn(q_t[64:], dss[1])], 0).T
    dv = jnp.concatenate([nn(g_t[:64], es[0]), nn(g_t[64:], es[1])], 0).T
    return dq.astype(bf), dk.astype(bf), dv.astype(bf)


def attention_backward_kernel(
    side_ref, x0, x1, low_ref, qkv_ref, ctx_ref, inv_ref, el_ref, es_ref, wo0, wo1, sums_a, sums_b, sums_c, bias0, bias1,
    out_ref, own_a, own_b, other_a, other_b, small0, small1, grad_ref, *, places_a, places_b,
):
    step = pl.program_id(0)
    half = x0.shape[0]
    rows = 2 * half
    scale = jnp.asarray(0.125, bf)
    low = low_ref[...]
    grad_ref[...] = nt(low, jnp.concatenate([wo0[...], wo1[...]], 0)).astype(bf)
    for first, size, index in slots(rows):
        at = pl.ds(first, size)
        for p in range(2):
            cols = [slice(256 * i + 128 * p, 256 * i + 128 * p + 128) for i in range(3)]
            q = qkv_ref[at, cols[0]] * scale
            k = qkv_ref[at, cols[1]] * scale
            v = qkv_ref[at, cols[2]]
            if size == LONG:
                es = [el_ref[0, 4 * index + 2 * p + h] for h in range(2)]
            else:
                es = [es_ref[0, 4 * (index - half // LONG) + 2 * p + h] for h in range(2)]
            grads = pair_backward(q, k, v, ctx_ref[at, cols[0]], inv_ref[at, cols[0]], grad_ref[at, cols[0]].astype(f32), es)
            for i in range(3):
                out_ref[at, cols[i]] = grads[i]
    packed = out_ref[...]
    wide = (tn(x0[...], packed[:half]) + tn(x1[...], packed[half:])).astype(bf)
    tail = tn(low, ctx_ref[...]).astype(bf)
    for side, (ref_a, ref_b) in enumerate(((own_a, own_b), (other_a, other_b))):
        pieces = [wide[:, 256 * i + 128 * side : 256 * i + 128 * side + 128] for i in range(3)]
        pieces.append(tail[:, 128 * side : 128 * side + 128])
        place_rows(ref_a, jnp.concatenate(pieces[:2], 1), places_a)
        place_rows(ref_b, jnp.concatenate(pieces[2:], 1), places_b)

    @pl.when(step == 0)
    def _():
        for ref, bias in ((small0, bias0), (small1, bias1)):
            ref[0:3, :] = sums_b[1:4, :]
            ref[3:6, :] = sums_c[0:3, :]
            ref[6:8, :] = sums_a[0:2, :]
            ref[8:9, :] = sums_b[0:1, :]
            high = jnp.floor(sums_a[2:3, :] * (1.0 / 256.0))
            ref[9:10, :] = high
            for i in range(bias.shape[1] // D):
                ref[10 + i : 11 + i, :] = bias[0:1, D * i : D * i + D]
            ref[12:16, :] = jnp.zeros((4, D), f32)
            ref[13:14, :] = sums_a[2:3, :] - 256.0 * high

    sums = jnp.sum(packed.astype(f32), axis=0, keepdims=True)
    for side, ref in enumerate((small0, small1)):
        for i in range(2):
            start = pl.multiple_of(i * (D // 2) + 128 * step, 128)
            ref[12:13, pl.ds(start, 128)] = sums[:, 512 * i + 128 * side : 512 * i + 128 * side + 128]


def attention_backward(place, tokens, low, qkv, ctx, inv, e_long, e_short, wo, sums, bias, places_a, places_b):
    half = tokens.shape[0] // 4
    rows = 2 * half
    steps = ctx.shape[1] // 256
    tall = pl.BlockSpec((128, D), lambda i, *_: (i, 0))

    def part(height, width):
        return pl.BlockSpec((height, width), lambda i, *_: (0, i))

    return pl.pallas_call(
        lambda *refs: attention_backward_kernel(*refs, places_a=places_a, places_b=places_b),
        out_shape=(shape((rows, 768 * steps), bf),) + (shape((D, 256 * steps), bf),) * 4 + (shape((16, D), f32),) * 2,
        grid_spec=pltpu.PrefetchScalarGridSpec(
            num_scalar_prefetch=1,
            grid=(steps,),
            in_specs=[
                pl.BlockSpec((half, D), lambda i, side, *_: (side[0], 0)),
                pl.BlockSpec((half, D), lambda i, side, *_: (2 + side[0], 0)),
                whole((rows, D)),
                part(rows, 768),
                part(rows, 256),
                part(rows, 256),
                pl.BlockSpec((1,) + e_long.shape[1:], lambda i, *_: (i, 0, 0, 0)),
                pl.BlockSpec((1,) + e_short.shape[1:], lambda i, *_: (i, 0, 0, 0)),
                tall,
                tall,
            ]
            + [whole((8, D))] * 3
            + [whole(bias[0].shape)] * 2,
            out_specs=[part(rows, 768)] + [part(D, 256)] * 4 + [whole((16, D))] * 2,
            scratch_shapes=[pltpu.VMEM((rows, 256), bf)],
        ),
        name="attention_backward",
        **settings(1e6, 58),
    )(place[0], tokens, tokens, low, qkv, ctx, inv, e_long, e_short, *wo, *sums, *bias)


def tokens_backward_kernel(first_ref, packed_ref, wq0, wq1, wk0, wk1, wv0, wv1, out_ref):
    total = first_ref[...]
    for i in range(packed_ref.shape[1] // 768):
        weights = jnp.concatenate([w[:, 128 * i : 128 * i + 128] for w in (wq0, wq1, wk0, wk1, wv0, wv1)], 1)
        total += nt(packed_ref[:, 768 * i : 768 * i + 768], weights)
    out_ref[...] = total.astype(bf)


def tokens_backward(first, packed, wq, wk, wv):
    rows = first.shape[0]
    chunk = 512
    return pl.pallas_call(
        tokens_backward_kernel,
        out_shape=shape((rows, D), bf),
        grid=(rows // chunk,),
        in_specs=[pl.BlockSpec((chunk, D), lambda i: (i, 0)), pl.BlockSpec((chunk, packed.shape[1]), lambda i: (i, 0))]
        + [whole(wq[0].shape)] * 6,
        out_specs=pl.BlockSpec((chunk, D), lambda i: (i, 0)),
        name="tokens_backward",
        **settings(1e6, 16),
    )(first, packed, *wq, *wk, *wv)


def join_kernel(side_ref, own_ref, other_ref, out_ref, buffer_ref, in_sems, out_sems):
    half = own_ref.shape[0] // 2
    fetches = []
    stores = []
    for i, ref in enumerate((own_ref, other_ref)):
        for j in range(2):
            n = 2 * i + j
            block = 2 * j + (side_ref[0] if i == 0 else 1 - side_ref[0])
            target = out_ref.at[pl.ds(pl.multiple_of(block * half, half), half), :]
            place = buffer_ref.at[n * half : (n + 1) * half, :]
            fetches.append(pltpu.make_async_copy(ref.at[j * half : (j + 1) * half, :], place, in_sems.at[n]))
            stores.append(pltpu.make_async_copy(place, target, out_sems.at[n]))
    for fetch in fetches:
        fetch.start()
    for fetch, store in zip(fetches, stores):
        fetch.wait()
        store.start()
    for store in stores:
        store.wait()


def join_rows(place, own, other):
    return pl.pallas_call(
        join_kernel,
        out_shape=shape((2 * own.shape[0], D), own.dtype),
        grid_spec=pltpu.PrefetchScalarGridSpec(
            num_scalar_prefetch=1,
            grid=(1,),
            in_specs=[anywhere(), anywhere()],
            out_specs=anywhere(),
            scratch_shapes=[
                pltpu.VMEM((2 * own.shape[0], D), own.dtype),
                pltpu.SemaphoreType.DMA((4,)),
                pltpu.SemaphoreType.DMA((4,)),
            ],
        ),
        name="join_rows",
        **settings(1e6, 4),
    )(place[0], *[pltpu.with_memory_space_constraint(v, pltpu.HBM) for v in (own, other)])


def exchange_kernel(mine_ref, *refs, chains, small, count, merge, step):
    ins, outs = (refs[:count], refs[count:])
    if small is not None:
        kept, source, first = small
        arrived = ins[source][...] if first is None else ins[source][first : first + 16, :].astype(f32)
        sums = ins[kept][...] + arrived
        sums = sums.astype(bf)
        outs[-1][...] = sums.astype(f32)
    base = 0
    for i, (keep, k0, recv, r0, rows) in enumerate(chains):
        half = rows // 2
        send_ref, keep_ref = (outs[0], outs[1]) if merge else (outs[2 * i], outs[2 * i + 1])
        for ref, side in ((send_ref, 1 - mine_ref[2 * step + i]), (keep_ref, mine_ref[2 * step + i])):
            at = side * half
            mine = ins[keep][pl.ds(pl.multiple_of(k0 + at, 16), half), :].astype(f32)
            sent = ins[recv][pl.ds(pl.multiple_of(r0 + at, 16), half), :].astype(f32)
            ref[base : base + half, :] = (mine + sent).astype(bf)
        end = base + half
        base = end if merge else 0
        if small is not None and i == (len(chains) - 1 if merge else 0):
            send_ref[end : end + 16, :] = sums


def exchange(mine, arrays, chains, small, merge, step):
    columns = arrays[0].shape[1]
    halves = [chain[4] // 2 for chain in chains]
    extra = 0 if small is None else 16
    if merge:
        outs = [shape((sum(halves) + extra, columns), bf), shape((sum(halves), columns), bf)]
    else:
        outs = []
        for i, half in enumerate(halves):
            kind = shape
            outs += [kind((half + (extra if i == 0 else 0), columns), bf), kind((half, columns), bf)]
    if small is not None:
        outs.append(shape((16, D), f32))
    return pl.pallas_call(
        lambda *refs: exchange_kernel(
            *refs, chains=chains, small=small, count=len(arrays), merge=merge, step=step
        ),
        out_shape=tuple(outs),
        grid_spec=pltpu.PrefetchScalarGridSpec(
            num_scalar_prefetch=1,
            grid=(1,),
            in_specs=[whole(v.shape) for v in arrays],
            out_specs=[whole(v.shape) for v in outs],
        ),
        name="exchange",
        **settings(1e6, 8),
    )(mine, *arrays)


def finish_kernel(keep_ref, recv_ref, small_in, *outs):
    rows = keep_ref.shape[0]
    total = keep_ref[...].astype(f32) + recv_ref[0:rows, :].astype(f32)
    for n, ref in enumerate(outs[:4]):
        part = total[(n // 2) * (rows // 2) : (n // 2 + 1) * (rows // 2)]
        for j in range(total.shape[1] // 256):
            ref[:, 128 * j : 128 * j + 128] = part[:, 256 * j + 128 * (n % 2) : 256 * j + 128 * (n % 2) + 128]
    small = small_in[...] + recv_ref[rows : rows + 16, :].astype(f32)
    for n in range(6):
        outs[4 + n][...] = small[n].reshape(D)
    inner_ref, query_ref, value_ref = outs[10:13]
    for i in range(inner_ref.shape[0] // D):
        inner_ref[D * i : D * i + D] = small[10 + i].reshape(D)
    half = query_ref.shape[0]
    query_ref[...] = small[12:13, :half].reshape(half)
    value_ref[...] = small[12:13, half:].reshape(half)
    count = small[9:10, 0:1] * 256.0 + small[13:14, 0:1]
    for n in range(3):
        outs[13 + n][...] = jnp.sqrt(jnp.sum(small[6 + n : 7 + n], axis=1, keepdims=True) / (count * D))


def finish(keep, recv, small, units):
    rows, columns = keep.shape
    half = columns // 2
    outs = [shape((rows // 2, half), f32)] * 4 + [shape((D,), f32)] * 6
    outs += [shape((units,), f32), shape((half,), f32), shape((half,), f32)] + [shape((1, 1), f32)] * 3
    return pl.pallas_call(
        finish_kernel,
        out_shape=tuple(outs),
        grid=(1,),
        in_specs=[whole(v.shape) for v in (keep, recv, small)],
        out_specs=[whole(v.shape) for v in outs],
        name="finish",
        **settings(1e6, 2),
    )(keep, recv, small)


def swap_tensor(value):
    return lax.ppermute(value, "tensor", [(0, 1), (1, 0)])


def dp_bits():
    count = lax.axis_size("dp")
    bits = []
    while (1 << len(bits)) < count:
        bits.append(1 << len(bits))
    return count, bits


def swap_dp(value, bit):
    count, _ = dp_bits()
    return lax.ppermute(value, "dp", [(i, i ^ bit) for i in range(count)])


def after(value, *others):
    return lax.optimization_barrier((value,) + others)[0]


def places_of(order):
    count, bits = dp_bits()
    out = []
    for i in range(count):
        position = 0
        for bit in order:
            position = 2 * position + (i // bit) % 2
        out.append(position)
    return out


def sorted_rows(value, places):
    size = value.shape[0] // len(places)
    source = [places.index(p) for p in range(len(places))]
    return jnp.concatenate([value[i * size : (i + 1) * size] for i in source], 0)


class RowScatter:
    def __init__(self, own, other, order, placed):
        if not placed:
            own, other = [sorted_rows(v, places_of(order)) for v in (own, other)]
        self.pair, self.order = ((own, other), list(order))
        self.split()

    def pick(self, side):
        size = self.pair[0].shape[0] // 2
        a, b = [lax.dynamic_slice_in_dim(v, side * size, size, 0).astype(f32) for v in self.pair]
        return (a + b).astype(bf)

    def resume(self, keep, recv, used):
        self.pair, self.order = ((keep, recv), self.order[used:])
        self.split()

    def split(self):
        mine = (lax.axis_index("dp") // self.order[0]) % 2
        self.send, self.keep = (self.pick(1 - mine), self.pick(mine))

    def step(self, *gates):
        keep = after(self.keep, *gates) if gates else self.keep
        self.pair = (keep, swap_dp(self.send, self.order[0]))
        self.order = self.order[1:]
        if self.order:
            self.split()

    def total(self):
        return self.pair[0].astype(f32) + self.pair[1].astype(f32)

    def ready(self):
        return self.send if self.order else self.pair[1]


def local(
    tokens,
    long_lengths,
    short_lengths,
    query_weight,
    query_bias,
    key_weight,
    value_weight,
    value_bias,
    output_weight,
    output_bias,
    first_gain,
    first_shift,
    inner_weight,
    inner_bias,
    outer_weight_here,
    outer_bias,
    second_gain,
    second_shift,
    out_grad,
):
    count, bits = dp_bits()
    order_a, order_b = (bits, bits[1::-1] + bits[2:])
    order_o = bits
    order_i = bits[:1] + bits[2:3] + bits[1:2] + bits[3:]
    placed = D % (16 * count) == 0
    places_a, places_b, places_o, places_i = [
        places_of(order) if placed else None for order in (order_a, order_b, order_o, order_i)
    ]
    width = query_weight.shape[1]
    place = (lax.axis_index("tensor").reshape(1), long_lengths, short_lengths)
    mine = (lax.axis_index("dp") // jnp.array([v for pair in zip(order_a, order_b) for v in pair], jnp.int32)) % 2
    bias, wq, wk, wv, wo, wi, w2 = [
        (v, swap_tensor(v))
        for v in (
            jnp.concatenate([query_bias, value_bias, inner_bias]),
            query_weight,
            key_weight,
            value_weight,
            output_weight,
            inner_weight,
            outer_weight_here,
        )
    ]
    qkv, ctx, inv, e_long, e_short, xhat, dev, low, sums_a = attention_forward(
        place, tokens, wq, wk, wv, bias, wo, output_bias, first_gain, first_shift
    )
    act, slope0, slope1, block_own, back, back_low, outer_other, sums_b = ffn_forward(
        place, low, wi, bias, w2, xhat, out_grad, first_gain, first_shift, outer_bias, second_gain, second_shift, places_o
    )
    outer_other = swap_tensor(outer_other)
    outer = RowScatter(outer_weight(back_low, act, places_o), outer_other, order_o, placed)
    block_other = swap_tensor(block_own)
    back_low = after(back_low, outer.send, block_other)
    inner_own, inner_other, bias0, bias1, first, first_low, sums_c = ffn_backward(
        back_low, (slope0, slope1), w2, wi, low, back, xhat, dev, first_gain, places_i
    )
    outer.step(sums_c)
    inner_own, inner_other, first_low, first = lax.optimization_barrier(
        (inner_own, inner_other, first_low, first, outer.send)
    )[:4]
    inner = RowScatter(inner_own, swap_tensor(inner_other), order_i, placed)
    first_low = after(first_low, inner.send)
    packed, own_a, own_b, other_a, other_b, small, small_other = attention_backward(
        place, tokens, first_low, qkv, ctx, inv, e_long, e_short, wo, (sums_a, sums_b, sums_c), (bias0, bias1), places_a, places_b
    )
    outer.step(small)
    other_a, other_b, small_other = [swap_tensor(after(v, outer.pair[1])) for v in (other_a, other_b, small_other)]
    inner.step(small)
    own_a, own_b, packed, small, block_own = lax.optimization_barrier(
        (own_a, own_b, packed, small, block_own, outer.pair[1], inner.pair[1])
    )[:5]

    def advance(*gates):
        for chain in (outer, inner):
            if chain.order:
                chain.step(*gates)

    if placed:
        rows = outer.pair[0].shape[0]
        chains = [(0, 0, 1, 0, rows), (2, 0, 3, 0, 2 * rows)]
        send_o, keep_o, send_i, keep_i = exchange(mine, (*outer.pair, *inner.pair), chains, None, False, 2)
        recv_o = swap_dp(send_o, order_o[2])
        own_a = after(own_a, send_o)
        chains = [(0, 0, 1, 0, D), (2, 0, 3, 0, D)]
        send_a, keep_a, send_b, keep_b, small = exchange(mine, (own_a, other_a, own_b, other_b, small, small_other), chains, (4, 5, None), False, 0)
        block_out = join_rows(place, after(block_own, send_a), block_other)
        recv_i = swap_dp(after(send_i, send_a, recv_o), order_i[1])
        outer.resume(after(keep_o, block_out), recv_o, 1)
        packed = after(packed, send_a, block_out, outer.send)
        tokens_own = tokens_backward(first, packed, wq, wk, wv)
        recv_a, recv_b = (swap_dp(send_a, order_a[0]), swap_dp(send_b, order_b[0]))
        keep_a = after(keep_a, tokens_own)
        rows = D // 2
        chains = [(0, 0, 1, 0, rows), (2, 0, 3, 0, rows)]
        send_a, keep_a, send_b, keep_b, small = exchange(mine, (keep_a, recv_a, keep_b, recv_b, small), chains, (4, 1, rows), False, 1)
        tokens_own = after(tokens_own, send_a)
        tokens_other = swap_tensor(tokens_own)
        recv_a, recv_b = (swap_dp(send_a, order_a[1]), swap_dp(send_b, order_b[1]))
        inner.resume(after(keep_i, send_a), recv_i, 1)
        rows = D // 4
        chains = [(0, 0, 1, 0, rows), (2, 0, 3, 0, rows)]
        send, keep, small = exchange(mine, (keep_a, recv_a, keep_b, recv_b, small), chains, (4, 1, rows), True, 2)
        for step in range(2, len(bits) - 1):
            recv = swap_dp(send, order_a[step])
            advance(send)
            rows = keep.shape[0] // 2
            chains = [(0, 0, 1, 0, rows), (0, rows, 1, rows, rows)]
            send, keep, small = exchange(mine, (keep, recv, small), chains, (2, 1, 2 * rows), True, step + 1)
        recv = swap_dp(send, order_a[-1])
        while outer.order or inner.order:
            advance(send)
        tokens_grad = join_rows(place, after(tokens_own, send), tokens_other)
        results = finish(after(keep, tokens_grad), recv, small, inner_bias.shape[0])
        query_grad, key_grad, value_grad, output_grad = results[:4]
        sums = list(results[4:13])
        rms = [v.reshape(()) for v in results[13:]]
    else:
        parts = [RowScatter(own_a, other_a, order_a, placed), RowScatter(own_b, other_b, order_b, placed)]
        small = small + small_other
        tokens_own = tokens_backward(first, packed, wq, wk, wv)
        tokens_grad = join_rows(place, tokens_own, swap_tensor(tokens_own))
        block_out = join_rows(place, block_own, block_other)
        for bit in bits:
            small = small + swap_dp(small, bit)
            for chain in [outer, inner] + parts:
                if chain.order:
                    chain.step()
        part_a, part_b = [part.total().reshape(D // count, -1, 2, 128) for part in parts]
        query_grad, key_grad, value_grad, output_grad = [
            v[:, :, i].reshape(-1, width) for v in (part_a, part_b) for i in range(2)
        ]
        sums = [small[i] for i in range(6)] + [small[10:12].reshape(-1), small[12, :width], small[12, width:]]
        squares = jnp.sum(small[6:9], axis=1)
        rms = jnp.sqrt(squares / ((small[9, 0] * 256.0 + small[13, 0]) * D))
    return (
        block_out,
        tokens_grad,
        query_grad,
        sums[7],
        key_grad,
        value_grad,
        sums[8],
        output_grad.T,
        sums[3],
        sums[4],
        sums[5],
        inner.total(),
        sums[6],
        outer.total().T,
        sums[2],
        sums[0],
        sums[1],
        rms[0],
        rms[1],
        rms[2],
    )


def solution(mesh):
    return jax.shard_map(
        local,
        mesh=mesh,
        in_specs=(
            P("dp", None),
            P("dp"),
            P("dp"),
            P(None, "tensor"),
            P("tensor"),
            P(None, "tensor"),
            P(None, "tensor"),
            P("tensor"),
            P("tensor", None),
            P(),
            P(),
            P(),
            P(None, "tensor"),
            P("tensor"),
            P("tensor", None),
            P(),
            P(),
            P(),
            P("dp", None),
        ),
        out_specs=(
            P("dp", None),
            P("dp", None),
            P("dp", "tensor"),
            P("tensor"),
            P("dp", "tensor"),
            P("dp", "tensor"),
            P("tensor"),
            P("tensor", "dp"),
            P(),
            P(),
            P(),
            P("dp", "tensor"),
            P("tensor"),
            P("tensor", "dp"),
            P(),
            P(),
            P(),
            P(),
            P(),
            P(),
        ),
        check_vma=False,
    )
```
